128 devices in a mesh: grp: 8 (over y, core), mem: 16 (over x, z).
Axes of the slice: x: 4, y: 4, z: 4, core: 2. Of those that a mesh axis runs over, the one named last changes fastest.
Arguments:
- background: float32 [256, 256, 512], P(('grp', 'mem')), may hold values from -6 to 6
- obs_ensemble: float32 [256, 256, 1024], P(('grp', 'mem')), may hold values from -6 to 6
- obs_value: float32 [256, 1024], replicated, may hold values from -12 to 12
- obs_precision: float32 [256, 1024], replicated, may hold values from 0.5 to 4
- obs_count: int32 [256], replicated, may hold values from 64 to 1024, as said below
Outputs:
- analysis: float32 [256, 256, 512], P(('grp', 'mem'))
The draws below stay inside these ranges and needn't reach their ends.
Inputs may be any that keep to these rules, and one draw needn't show every extreme that they name: `obs_count`: the number of leading slots of each patch that hold observations; exactly 128 patches use more than 512 slots, and some patch uses exactly 1024.
All inputs are finite; a program needn't handle non-finite values.
Results may differ from the reference program's by a relative error of at most 0.0003.
Values sent between devices are 32-bit elements; how exact they have to be, the bound alone decides.
No kernel may reach another device: no remote copies, remote signals or barrier semaphores. Data moves between devices by JAX's collectives and lax.ppermute only.
A program may use at most 64 MiB of HBM per device.

```python
import math
import jax
import jax.numpy as jnp
from jax import lax

MEMBERS = 256
CELLS = 512
OBS_MAX = 1024
SWEEPS = 8
PATCHES = 256


def draw_obs_count(key, part):
    first, second, third, fourth = jax.random.split(jax.random.fold_in(key, 11), 4)
    half = OBS_MAX // 2
    ranks = jax.random.permutation(first, PATCHES).astype(jnp.int32)
    heavy = ranks < PATCHES // 2
    level = jax.random.randint(second, (PATCHES,), 0, 4)
    base = OBS_MAX // 16 * jnp.left_shift(jnp.int32(1), level.astype(jnp.int32))
    extra = jax.random.randint(third, (PATCHES,), 0, base)
    light_counts = jnp.minimum(base + extra, half)
    heavy_counts = jax.random.randint(fourth, (PATCHES,), half + 1, OBS_MAX + 1)
    counts = jnp.where(heavy, heavy_counts, light_counts)
    counts = jnp.where(ranks == 0, OBS_MAX, counts)
    return counts.astype(jnp.int32)


def shard_levels(rng, dims, pieces, low, top_value):
    def one(axis_at, parts):
        steps = jax.random.uniform(jax.random.fold_in(jax.random.fold_in(rng, 6), axis_at), (parts,), jnp.float32, low / len(pieces), top_value / len(pieces))
        return jnp.repeat(jnp.exp(steps), dims[axis_at] // parts).reshape((-1,) + (1,) * (len(dims) - axis_at - 1))

    level = one(*pieces[0])
    for cut in pieces[1:]:
        level = level * one(*cut)
    return level


def scatter_about(rng, shape, scale, most, cuts=(), kind=jnp.bfloat16):
    array = jax.random.normal(rng, shape, jnp.float32) * scale
    if len(cuts) > 0:
        array = shard_levels(rng, shape, cuts, -0.22, 0.18) * array
    return jnp.clip(array, min=-most, max=most).astype(kind)


def setup_inputs(seed: int = 0) -> dict:
    key_of = jax.random.split(jax.random.key(seed), 6)
    background = scatter_about(key_of[0], (MEMBERS, PATCHES, CELLS), 1.0, 6.0, ((0, 128),), jnp.float32)
    obs_ensemble = scatter_about(key_of[1], (MEMBERS, PATCHES, OBS_MAX), 1.0, 6.0, ((0, 128),), jnp.float32)
    obs_value = scatter_about(key_of[2], (PATCHES, OBS_MAX), 2.0, 12.0, (), jnp.float32)
    obs_precision = jnp.clip(jnp.exp(jax.random.uniform(key_of[3], (PATCHES, OBS_MAX), jnp.float32, math.log(0.5), math.log(4.0))), 0.5, 4.0)
    obs_count = draw_obs_count(jax.random.fold_in(key_of[5], 71), 0)
    return {"background": background, "obs_ensemble": obs_ensemble, "obs_value": obs_value, "obs_precision": obs_precision, "obs_count": obs_count}


highest = lax.Precision.HIGHEST

def inverse_root(amatrix):
    members = amatrix.shape[0]
    identity = jnp.eye(members, dtype=jnp.float32)
    scaler = jnp.sqrt(jnp.sum(amatrix * amatrix))
    iterate = amatrix / scaler
    result = identity
    for sweep in range(SWEEPS):
        factor = 1.5 * identity - 0.5 * jnp.dot(result, iterate, precision=highest)
        iterate = jnp.dot(iterate, factor, precision=highest)
        result = jnp.dot(factor, result, precision=highest)
    return result / jnp.sqrt(scaler)

def update_patch(inflation, states, perturb, weight, innov):
    members = states.shape[0]
    gram = jnp.dot(perturb * weight[None, :], perturb.T, precision=highest)
    amatrix = (members - 1.0) * jnp.eye(members, dtype=jnp.float32) + inflation * inflation * gram
    root = inverse_root(amatrix)
    inverse = jnp.dot(root, root, precision=highest)
    forcing = inflation * jnp.dot(perturb, weight * innov, precision=highest)
    shifts = jnp.dot(inverse, forcing, precision=highest)
    transform = jnp.sqrt(members - 1.0) * root + shifts[:, None]
    center = lax.optimization_barrier(jnp.mean(states, axis=0))
    deviation = states - center[None, :]
    return center[None, :] + inflation * jnp.dot(transform.T, deviation, precision=highest)

def reference(background, obs_ensemble, obs_value, obs_precision, obs_count):
    members = background.shape[0]
    slots = jnp.arange(OBS_MAX, dtype=jnp.int32)
    live = (slots[None, :] < obs_count[:, None]).astype(jnp.float32)
    weight = obs_precision * live
    obs_mean = lax.optimization_barrier(jnp.mean(obs_ensemble, axis=0))
    perturb = obs_ensemble - obs_mean[None]
    innov = obs_value - obs_mean
    spread = lax.optimization_barrier(jnp.sum(perturb * perturb, axis=0)) / (members - 1.0)
    misfit = jnp.sum(weight * innov * innov)
    expected = jnp.sum(live * (1.0 + obs_precision * spread))
    inflation = jnp.sqrt(misfit / expected)

    def per_patch(items):
        return update_patch(inflation, items[0], items[1], items[2], items[3])
    result = lax.map(per_patch, (jnp.swapaxes(background, 0, 1), jnp.swapaxes(perturb, 0, 1), weight, innov))
    return jnp.swapaxes(result, 0, 1)
```

```python
import functools

import jax
import jax.numpy as jnp
from jax import lax
from jax.experimental import pallas as pl
from jax.experimental.pallas import tpu as pltpu
from jax.sharding import PartitionSpec as P

SWEEPS = 8
LANES = 128
AXES = ("grp", "mem")
F32 = jnp.float32
BF16 = jnp.bfloat16
VMEM_LIMIT = 48 << 20


def dot(a, b):
    return jnp.dot(a, b, preferred_element_type=F32)


def dot_nt(a, b):
    return lax.dot_general(a, b, (((1,), (1,)), ((), ())), preferred_element_type=F32)


def halves(x):
    high = x.astype(BF16)
    return high, (x - high.astype(F32)).astype(BF16)


def thirds(x):
    high = x.astype(BF16)
    rest = x - high.astype(F32)
    mid = rest.astype(BF16)
    return high, mid, (rest - mid.astype(F32)).astype(BF16)


def left_form(x):
    high, low = halves(x)
    return jnp.concatenate([high, high, low], axis=1)


def right_form(x):
    high, low = halves(x)
    return jnp.concatenate([high, low, high], axis=0)


def owners(counts, half, devices):
    patches = counts.shape[1]
    heavy = (counts > half).astype(F32)
    before = lax.broadcasted_iota(jnp.int32, (patches, patches), 0) < lax.broadcasted_iota(
        jnp.int32, (patches, patches), 1
    )
    rank = dot(jnp.broadcast_to(heavy, (8, patches)).astype(BF16), before.astype(F32).astype(BF16))[:1]
    position = lax.broadcasted_iota(jnp.int32, (1, patches), 1).astype(F32)
    device = lax.broadcasted_iota(jnp.int32, (devices, patches), 0).astype(F32)
    heavies = jnp.where((device == rank) & (heavy > 0.0), 1.0, 0.0)
    lights = jnp.where((device == position - rank) & (heavy == 0.0), 1.0, 0.0)
    return heavies, lights


def pick(onehot, x):
    chosen = onehot.astype(BF16)
    return dot(jnp.concatenate([chosen] * 3, axis=1), jnp.concatenate(thirds(x), axis=0))


def pack_obs_kernel(counts_ref, obs_ref, out_ref):
    local, _, slots = obs_ref.shape
    half = slots // 2
    per = (slots + half) // LANES * local
    devices = out_ref.shape[0] // per
    heavies, lights = owners(counts_ref[...], half, devices)
    for member in range(local):
        heavy = pick(heavies, obs_ref[member])
        for c in range(slots // LANES):
            row = member * (slots // LANES) + c
            out_ref[pl.ds(row, devices, stride=per), :] = heavy[:, c * LANES : (c + 1) * LANES]
        light = pick(lights, obs_ref[member, :, :half])
        for c in range(half // LANES):
            row = local * (slots // LANES) + member * (half // LANES) + c
            out_ref[pl.ds(row, devices, stride=per), :] = light[:, c * LANES : (c + 1) * LANES]


def pack_states_kernel(mine_ref, counts_ref, states_ref, value_ref, precision_ref, out_ref, rows_ref):
    local, patches, cells = states_ref.shape
    slots = value_ref.shape[1]
    blocks = cells // LANES
    per = 2 * local * blocks
    devices = out_ref.shape[0] // per
    counts = counts_ref[...]
    heavies, lights = owners(counts, slots // 2, devices)
    for member in range(local):
        x = states_ref[member]
        for k, onehot in enumerate((heavies, lights)):
            chosen = pick(onehot, x)
            for c in range(blocks):
                row = (k * local + member) * blocks + c
                out_ref[pl.ds(row, devices, stride=per), :] = chosen[:, c * LANES : (c + 1) * LANES]
    here = lax.broadcasted_iota(jnp.int32, (devices, patches), 0) == mine_ref[0]
    own = [jnp.sum(jnp.where(here, onehot, 0.0), axis=0, keepdims=True) for onehot in (heavies, lights)]
    both = jnp.concatenate(own + [jnp.zeros((6, patches), F32)], axis=0)
    values = pick(both, value_ref[...])
    precisions = pick(both, precision_ref[...])
    slot = lax.broadcasted_iota(jnp.int32, (1, slots), 1).astype(F32)
    rows = []
    for k in range(2):
        count = jnp.sum(own[k] * counts.astype(F32), axis=1, keepdims=True)
        live = jnp.where(slot < count, 1.0, 0.0)
        rows += [values[k : k + 1], precisions[k : k + 1], live]
    rows_ref[...] = jnp.concatenate(rows + [jnp.zeros((2, slots), F32)], axis=0)


def gram_kernel(obs_ref, rows_ref, part_ref, gram_ref, high_ref, low_ref, *, local):
    slots = rows_ref.shape[1]
    half = slots // 2
    per = (slots + half) // LANES * local
    devices = obs_ref.shape[0] // per
    members = local * devices
    misfit = jnp.zeros((1, LANES), F32)
    expected = jnp.zeros((1, LANES), F32)
    for k in range(2):
        width = slots if k == 0 else half
        base = 0 if k == 0 else local * (slots // LANES)
        for c in range(width // LANES):
            columns = slice(c * LANES, (c + 1) * LANES)
            parts = [
                obs_ref[pl.ds(base + m * (width // LANES) + c, devices, stride=per), :] for m in range(local)
            ]
            mean = sum(jnp.sum(p, axis=0, keepdims=True) for p in parts) * (1.0 / members)
            parts = [p - mean for p in parts]
            spread = sum(jnp.sum(p * p, axis=0, keepdims=True) for p in parts) * (1.0 / (members - 1.0))
            value = rows_ref[3 * k : 3 * k + 1, columns]
            precision = rows_ref[3 * k + 1 : 3 * k + 2, columns]
            live = rows_ref[3 * k + 2 : 3 * k + 3, columns]
            innov = value - mean
            weight = precision * live
            misfit += weight * innov * innov
            expected += live * (1.0 + precision * spread)
            scale = jnp.sqrt(weight)
            for m in range(local):
                high, low = halves(parts[m] * scale)
                high_ref[m * devices : (m + 1) * devices, columns] = high
                low_ref[m * devices : (m + 1) * devices, columns] = low
            high, low = halves(jnp.broadcast_to(scale * innov, (16, LANES)))
            high_ref[members : members + 16, columns] = high
            low_ref[members : members + 16, columns] = low
        high = high_ref[:, :width]
        low = low_ref[:, :width]
        gram_ref[k] = (
            dot_nt(high, high_ref[:members, :width])
            + dot_nt(high, low_ref[:members, :width])
            + dot_nt(low, high_ref[:members, :width])
        )
    lane = lax.broadcasted_iota(jnp.int32, (1, LANES), 1)
    row = jnp.where(
        lane == 0,
        jnp.sum(misfit, axis=1, keepdims=True),
        jnp.where(lane == 1, jnp.sum(expected, axis=1, keepdims=True), 0.0),
    )
    part_ref[...] = jnp.broadcast_to(row[None], part_ref.shape)


def root_kernel(part_ref, gram_ref, out_ref, inflation_ref, y_right, z_right, z_left):
    members = gram_ref.shape[2]
    total = jnp.sum(part_ref[...], axis=0)
    lane = lax.broadcasted_iota(jnp.int32, total.shape, 1)
    misfit = jnp.sum(jnp.where(lane == 0, total, 0.0), axis=1, keepdims=True)
    expected = jnp.sum(jnp.where(lane == 1, total, 0.0), axis=1, keepdims=True)
    inflation = jnp.sqrt(misfit / expected)
    inflation_ref[...] = jnp.broadcast_to(inflation, inflation_ref.shape)
    identity = jnp.where(
        lax.broadcasted_iota(jnp.int32, (members, members), 0)
        == lax.broadcasted_iota(jnp.int32, (members, members), 1),
        1.0,
        0.0,
    )
    scalers = []
    for k in range(2):
        amat = (members - 1.0) * identity + inflation * inflation * gram_ref[k, :members, :]
        scaler = jnp.sqrt(jnp.sum(jnp.sum(amat * amat, axis=0, keepdims=True), axis=1, keepdims=True))
        scalers.append(scaler)
        iterate = amat / scaler
        factor = 1.5 * identity - 0.5 * iterate
        y_right[k] = right_form(dot(left_form(factor), right_form(iterate)))
        z_right[k] = right_form(factor)
        z_left[k] = left_form(factor)

    def sweep(_, carry):
        for k in range(2):
            factor = left_form(1.5 * identity - 0.5 * dot(z_left[k], y_right[k]))
            iterate = dot(factor, y_right[k])
            root = dot(factor, z_right[k])
            y_right[k] = right_form(iterate)
            z_right[k] = right_form(root)
            z_left[k] = left_form(root)
        return carry

    lax.fori_loop(0, SWEEPS - 2, sweep, 0)
    for k in range(2):
        factor = left_form(1.5 * identity - 0.5 * dot(z_left[k], y_right[k]))
        root = dot(factor, z_right[k]) / jnp.sqrt(scalers[k])
        root_right = right_form(root)
        forcing = inflation * gram_ref[k, members:, :]
        shifts = dot(left_form(dot(left_form(forcing), root_right)), root_right)[:1]
        out_ref[k] = inflation * ((members - 1.0) ** 0.5 * root + shifts)


def update_kernel(states_ref, transform_ref, out_ref, high_ref, low_ref, *, local):
    members = transform_ref.shape[1]
    devices = members // local
    per = states_ref.shape[0] // devices
    blocks = per // (2 * local)
    for k in range(2):
        centers = []
        for c in range(blocks):
            rows = [(k * local + m) * blocks + c for m in range(local)]
            parts = [states_ref[pl.ds(r, devices, stride=per), :] for r in rows]
            center = sum(jnp.sum(p, axis=0, keepdims=True) for p in parts) * (1.0 / members)
            centers.append(center)
            for m in range(local):
                high, low = halves(parts[m] - center)
                high_ref[m * devices : (m + 1) * devices, c * LANES : (c + 1) * LANES] = high
                low_ref[m * devices : (m + 1) * devices, c * LANES : (c + 1) * LANES] = low
        high, low = halves(transform_ref[k])
        update = dot(high, high_ref[...]) + dot(high, low_ref[...]) + dot(low, high_ref[...])
        for c in range(blocks):
            for m in range(local):
                piece = update[m * devices : (m + 1) * devices, c * LANES : (c + 1) * LANES] + centers[c]
                out_ref[pl.ds((k * local + m) * blocks + c, devices, stride=per), :] = piece


def unpack_kernel(counts_ref, rows_ref, out_ref, *, half):
    local, patches, cells = out_ref.shape
    blocks = cells // LANES
    per = 2 * local * blocks
    devices = rows_ref.shape[0] // per
    onehot = jnp.concatenate(owners(counts_ref[...], half, devices), axis=0).T
    for m in range(local):
        x = jnp.concatenate(
            [
                jnp.concatenate(
                    [
                        rows_ref[pl.ds((k * local + m) * blocks + c, devices, stride=per), :]
                        for c in range(blocks)
                    ],
                    axis=1,
                )
                for k in range(2)
            ],
            axis=0,
        )
        out_ref[m] = pick(onehot, x)


def call(kernel, out_shapes, inputs, scratch=(), smem=()):
    whole = pl.BlockSpec(memory_space=pltpu.VMEM)
    shapes = [jax.ShapeDtypeStruct(s, F32) for s in out_shapes]
    return pl.pallas_call(
        kernel,
        out_shape=shapes,
        in_specs=[pl.BlockSpec(memory_space=pltpu.SMEM) if i in smem else whole for i in range(len(inputs))],
        out_specs=[whole] * len(shapes),
        scratch_shapes=list(scratch),
        compiler_params=pltpu.CompilerParams(vmem_limit_bytes=VMEM_LIMIT),
    )(*inputs)


def exchange(x, devices):
    return lax.all_to_all(x, AXES, split_axis=0, concat_axis=0, tiled=True)


def per_device(background, obs_ensemble, obs_value, obs_precision, obs_count):
    devices = lax.axis_size(AXES)
    local, patches, cells = background.shape
    slots = obs_ensemble.shape[2]
    half = slots // 2
    members = local * devices
    counts = obs_count.reshape(1, patches)
    mine = lax.axis_index(AXES).astype(jnp.int32).reshape(1)
    obs_rows = (slots + half) // LANES * local
    state_rows = 2 * local * cells // LANES
    (obs_sent,) = call(pack_obs_kernel, [(devices * obs_rows, LANES)], (counts, obs_ensemble))
    obs = exchange(obs_sent, devices)
    states_sent, rows = call(
        pack_states_kernel,
        [(devices * state_rows, LANES), (8, slots)],
        (mine, counts, background, obs_value, obs_precision),
        smem=(0,),
    )
    states = exchange(states_sent, devices)
    part, gram = call(
        functools.partial(gram_kernel, local=local),
        [(devices, 1, LANES), (2, members + 16, members)],
        (obs, rows),
        scratch=[pltpu.VMEM((members + 16, slots), BF16)] * 2,
    )
    parts = exchange(part, devices)
    transform, inflation = call(
        root_kernel,
        [(2, members, members), (8, LANES)],
        (parts, gram),
        scratch=[
            pltpu.VMEM((2, 3 * members, members), BF16),
            pltpu.VMEM((2, 3 * members, members), BF16),
            pltpu.VMEM((2, members, 3 * members), BF16),
        ],
    )
    (update,) = call(
        functools.partial(update_kernel, local=local),
        [(devices * state_rows, LANES)],
        (states, transform),
        scratch=[pltpu.VMEM((members, cells), BF16)] * 2,
    )
    returned = exchange(update, devices)
    (analysis,) = call(
        functools.partial(unpack_kernel, half=half), [(local, patches, cells)], (counts, returned)
    )
    return analysis


def solution(mesh):
    placed = (P(AXES, None, None), P(AXES, None, None), P(), P(), P())
    return jax.shard_map(
        per_device, mesh=mesh, in_specs=placed, out_specs=P(AXES, None, None), check_vma=False
    )
```

```python
import functools

import jax
import jax.numpy as jnp
from jax import lax
from jax.experimental import pallas as pl
from jax.experimental.pallas import tpu as pltpu
from jax.sharding import PartitionSpec as P

SWEEPS = 8
LANES = 128
AXES = ("grp", "mem")
F32 = jnp.float32
BF16 = jnp.bfloat16
VMEM_LIMIT = 12 << 20


def dot(a, b):
    return jnp.dot(a, b, preferred_element_type=F32)


def dot_nt(a, b):
    return lax.dot_general(a, b, (((1,), (1,)), ((), ())), preferred_element_type=F32)


def exact_dot(a, b):
    return jnp.dot(a, b, preferred_element_type=F32, precision=lax.Precision.HIGHEST)


def halves(x):
    high = x.astype(BF16)
    return high, (x - high.astype(F32)).astype(BF16)


def thirds(x):
    high = x.astype(BF16)
    rest = x - high.astype(F32)
    mid = rest.astype(BF16)
    return high, mid, (rest - mid.astype(F32)).astype(BF16)


def left_form(x):
    high, low = halves(x)
    return jnp.concatenate([high, high, low], axis=1)


def right_form(x):
    high, low = halves(x)
    return jnp.concatenate([high, low, high], axis=0)


def owners(counts, half, devices):
    patches = counts.shape[1]
    heavy = (counts > half).astype(F32)
    before = lax.broadcasted_iota(jnp.int32, (patches, patches), 0) < lax.broadcasted_iota(
        jnp.int32, (patches, patches), 1
    )
    rank = dot(jnp.broadcast_to(heavy, (8, patches)).astype(BF16), before.astype(F32).astype(BF16))[:1]
    position = lax.broadcasted_iota(jnp.int32, (1, patches), 1).astype(F32)
    device = lax.broadcasted_iota(jnp.int32, (devices, patches), 0).astype(F32)
    heavies = jnp.where((device == rank) & (heavy > 0.0), 1.0, 0.0)
    lights = jnp.where((device == position - rank) & (heavy == 0.0), 1.0, 0.0)
    return heavies, lights


def store_rows(ref, first, stride, x):
    for j in range(x.shape[1] // LANES):
        ref[pl.ds(first + j, x.shape[0], stride=stride), :] = x[:, j * LANES : (j + 1) * LANES]


def gather_rows(ref, first, stride, rows, blocks):
    return jnp.concatenate([ref[pl.ds(first + j, rows, stride=stride), :] for j in range(blocks)], axis=1)


def load_rows(ref, first, rows, blocks):
    return jnp.concatenate([ref[first + j * rows : first + (j + 1) * rows] for j in range(blocks)], axis=1)


def pick(onehot, x):
    chosen = onehot.astype(BF16)
    return dot(jnp.concatenate([chosen] * 3, axis=1), jnp.concatenate(thirds(x), axis=0))


def pack_obs_kernel(counts_hbm, obs_hbm, out_hbm, counts_ref, obs_ref, out_ref, sems):
    local, patches, slots = obs_hbm.shape
    half = slots // 2
    pieces, wide = obs_ref.shape[1], obs_ref.shape[3]
    blocks = slots // LANES
    per = (slots + half) // LANES * local
    devices = out_ref.shape[0] // per
    count_copy = pltpu.make_async_copy(counts_hbm, counts_ref, sems.at[local * pieces])
    count_copy.start()
    copies = {}
    for m in range(local):
        for j in range(pieces):
            copies[m, j] = pltpu.make_async_copy(
                obs_hbm.at[m, :, pl.ds(j * wide, wide)], obs_ref.at[m, j], sems.at[m * pieces + j]
            )
            copies[m, j].start()
    count_copy.wait()
    heavies, lights = owners(counts_ref[...], half, devices)
    both = jnp.concatenate([heavies, lights], axis=0)
    for m in range(local):
        for j in range(pieces):
            copies[m, j].wait()
            first = j * wide // LANES
            if (j + 1) * wide <= half:
                chosen = pick(both, obs_ref[m, j])
                store_rows(out_ref, local * blocks + m * blocks // 2 + first, per, chosen[devices:])
            else:
                chosen = pick(heavies, obs_ref[m, j])
            store_rows(out_ref, m * blocks + first, per, chosen[:devices])
    done = pltpu.make_async_copy(out_ref, out_hbm, sems.at[local * pieces])
    done.start()
    done.wait()


def pack_states_kernel(mine_ref, counts_ref, states_ref, value_ref, precision_ref, out_ref, rows_ref):
    local, patches, cells = states_ref.shape
    slots = value_ref.shape[1]
    blocks = cells // LANES
    per = 2 * local * blocks + 1
    devices = out_ref.shape[0] // per
    counts = counts_ref[...]
    heavies, lights = owners(counts, slots // 2, devices)
    both = jnp.concatenate([heavies, lights], axis=0)
    for m in range(local):
        chosen = pick(both, states_ref[m])
        for k in range(2):
            store_rows(out_ref, (k * local + m) * blocks, per, chosen[k * devices : (k + 1) * devices])
    out_ref[pl.ds(per - 1, devices, stride=per), :] = jnp.zeros((devices, LANES), F32)
    here = lax.broadcasted_iota(jnp.int32, (devices, patches), 0) == mine_ref[0]
    own = [jnp.sum(jnp.where(here, onehot, 0.0), axis=0, keepdims=True) for onehot in (heavies, lights)]
    both = jnp.concatenate(own + [jnp.zeros((6, patches), F32)], axis=0)
    values = pick(both, value_ref[...])
    precisions = pick(both, precision_ref[...])
    slot = lax.broadcasted_iota(jnp.int32, (1, slots), 1).astype(F32)
    rows = []
    for k in range(2):
        count = jnp.sum(own[k] * counts.astype(F32), axis=1, keepdims=True)
        live = jnp.where(slot < count, 1.0, 0.0)
        rows += [values[k : k + 1], precisions[k : k + 1], live]
    rows_ref[...] = jnp.concatenate(rows + [jnp.zeros((2, slots), F32)], axis=0)


def obs_columns(obs_ref, rows_ref, local):
    slots = rows_ref.shape[1]
    half = slots // 2
    per = (slots + half) // LANES * local
    devices = obs_ref.shape[0] // per
    for k in range(2):
        width = slots if k == 0 else half
        base = 0 if k == 0 else local * (slots // LANES)
        for c in range(width // LANES):
            columns = slice(c * LANES, (c + 1) * LANES)
            parts = [
                obs_ref[pl.ds(base + m * (width // LANES) + c, devices, stride=per), :] for m in range(local)
            ]
            mean = sum(jnp.sum(p, axis=0, keepdims=True) for p in parts) * (1.0 / (local * devices))
            value, precision, live = (rows_ref[3 * k + i : 3 * k + i + 1, columns] for i in range(3))
            yield k, columns, [p - mean for p in parts], value - mean, precision, live


def sums_kernel(obs_ref, rows_ref, out_ref, *, local):
    members = local * out_ref.shape[0]
    misfit = jnp.zeros((1, LANES), F32)
    expected = jnp.zeros((1, LANES), F32)
    for _, _, parts, innov, precision, live in obs_columns(obs_ref, rows_ref, local):
        spread = sum(jnp.sum(p * p, axis=0, keepdims=True) for p in parts) * (1.0 / (members - 1.0))
        misfit += precision * live * innov * innov
        expected += live * (1.0 + precision * spread)
    lane = lax.broadcasted_iota(jnp.int32, (1, LANES), 1)
    row = jnp.where(
        lane == 0,
        jnp.sum(misfit, axis=1, keepdims=True),
        jnp.where(lane == 1, jnp.sum(expected, axis=1, keepdims=True), 0.0),
    )
    out_ref[...] = jnp.broadcast_to(row[None], out_ref.shape)


def place_kernel(sums_ref, states_hbm, out_hbm, sem):
    copy = pltpu.make_async_copy(sums_ref, out_hbm.at[:, out_hbm.shape[1] - 1], sem)
    copy.start()
    copy.wait()


def gram_kernel(obs_ref, rows_ref, powers_ref, side_ref, high_ref, low_ref, *, local):
    slots = rows_ref.shape[1]
    members = side_ref.shape[2]
    devices = members // local
    for k, columns, parts, innov, precision, live in obs_columns(obs_ref, rows_ref, local):
        scale = jnp.sqrt(precision * live)
        for m in range(local):
            high, low = halves(parts[m] * scale)
            high_ref[k, m * devices : (m + 1) * devices, columns] = high
            low_ref[k, m * devices : (m + 1) * devices, columns] = low
        high, low = halves(jnp.broadcast_to(scale * innov, (16, LANES)))
        high_ref[k, members:, columns] = high
        low_ref[k, members:, columns] = low
    diagonal = lax.broadcasted_iota(jnp.int32, (members, members), 0) == lax.broadcasted_iota(
        jnp.int32, (members, members), 1
    )
    for k in range(2):
        width = slots if k == 0 else slots // 2
        high, low = high_ref[k, :, :width], low_ref[k, :, :width]
        gram = dot_nt(high, high[:members]) + dot_nt(high, low[:members]) + dot_nt(low, high[:members])
        forcing = gram[members : members + 8]
        gram = gram[:members]
        size = jnp.sqrt(jnp.sum(jnp.sum(gram * gram, axis=0, keepdims=True), axis=1, keepdims=True))
        unit = gram / jnp.maximum(size, 1e-30)
        trace = jnp.sum(
            jnp.sum(jnp.where(diagonal, unit, 0.0), axis=0, keepdims=True), axis=1, keepdims=True
        )
        second = exact_dot(unit, unit)
        for i, power in enumerate((unit, second, exact_dot(unit, second))):
            for h in range(members // LANES):
                first = ((k * 3 + i) * (members // LANES) + h) * members
                powers_ref[first : first + members] = power[:, h * LANES : (h + 1) * LANES]
        side_ref[k] = jnp.concatenate(
            [forcing, jnp.broadcast_to(size, (8, members)), jnp.broadcast_to(trace, (8, members))], axis=0
        )


def update_kernel(states_ref, powers_ref, side_ref, out_ref, s_left, sz_right, states_right, *, local):
    members = side_ref.shape[2]
    devices = members // local
    per = states_ref.shape[0] // devices
    blocks = out_ref.shape[0] // devices // (2 * local)
    total = jnp.sum(states_ref[pl.ds(per - 1, devices, stride=per), :], axis=0, keepdims=True)
    lane = lax.broadcasted_iota(jnp.int32, total.shape, 1)
    misfit = jnp.sum(jnp.where(lane == 0, total, 0.0), axis=1, keepdims=True)
    expected = jnp.sum(jnp.where(lane == 1, total, 0.0), axis=1, keepdims=True)
    squared = misfit / expected
    inflation = jnp.sqrt(squared)
    diagonal = lax.broadcasted_iota(jnp.int32, (members, members), 0) == lax.broadcasted_iota(
        jnp.int32, (members, members), 1
    )
    free = members - 1.0

    def plus_diagonal(x, value):
        return x + jnp.where(diagonal, value, 0.0)

    def refine(k, product):
        s = s_left[k, :, :members].astype(F32) + s_left[k, :, 2 * members :].astype(F32)
        return dot(left_form(plus_diagonal(0.25 * product - 1.5 * s, 2.25)), sz_right[k, :, :members])

    scalers = []
    for k in range(2):
        size, trace = side_ref[k, 8:9, :1], side_ref[k, 16:17, :1]
        strength = squared * size
        scaler = jnp.sqrt(free * free * members + strength * (2.0 * free * trace + strength))
        scalers.append(scaler)
        a, b = free / scaler, strength / scaler
        f = 1.5 - 0.5 * a
        s1 = (a * f * f, b * f * (f - a), b * b * (0.25 * a - f), 0.25 * b * b * b)
        powers = [
            load_rows(powers_ref, (k * 3 + i) * (members // LANES) * members, members, members // LANES)
            for i in range(3)
        ]
        s = plus_diagonal(sum(c * p for c, p in zip(s1[1:], powers)), s1[0])
        z = plus_diagonal(-0.5 * b * powers[0], f)
        s_left[k] = left_form(s)
        sz_right[k, :, :members] = right_form(s)
        sz_right[k, :, members:] = right_form(z)
    def times(k):
        z = sz_right[k, :members, members:].astype(F32) + sz_right[k, members : 2 * members, members:].astype(F32)
        return z

    def sweep(_, carry):
        for k in range(2):
            product = dot(s_left[k], sz_right[k])
            z = 1.5 * times(k) - 0.5 * product[:, members:]
            s = refine(k, product[:, :members])
            s_left[k] = left_form(s)
            sz_right[k, :, :members] = right_form(s)
            sz_right[k, :, members:] = right_form(z)
        return carry

    lax.fori_loop(0, SWEEPS - 2, sweep, 0)
    for k in range(2):
        centers = []
        for c in range(blocks):
            rows = [(k * local + m) * blocks + c for m in range(local)]
            parts = [states_ref[pl.ds(r, devices, stride=per), :] for r in rows]
            center = sum(jnp.sum(p, axis=0, keepdims=True) for p in parts) * (1.0 / members)
            centers.append(center)
            for m in range(local):
                high, low = halves(parts[m] - center)
                span = slice(m * devices, (m + 1) * devices)
                columns = slice(c * LANES, (c + 1) * LANES)
                states_right[span, columns] = high
                states_right[members + m * devices : members + (m + 1) * devices, columns] = low
                states_right[2 * members + m * devices : 2 * members + (m + 1) * devices, columns] = high
        product = dot(s_left[k], sz_right[k, :, members:])
        root = (1.5 * times(k) - 0.5 * product) / jnp.sqrt(scalers[k])
        root_right = right_form(root)
        forcing = inflation * side_ref[k, :8]
        shifts = dot(left_form(dot(left_form(forcing), root_right)), root_right)[:1]
        transform = inflation * (free**0.5 * root + shifts)
        update = dot(left_form(transform), states_right[...])
        for c in range(blocks):
            for m in range(local):
                piece = update[m * devices : (m + 1) * devices, c * LANES : (c + 1) * LANES] + centers[c]
                out_ref[pl.ds((k * local + m) * blocks + c, devices, stride=2 * local * blocks), :] = piece


def unpack_kernel(counts_ref, rows_ref, out_hbm, out_ref, sems, *, half):
    local, patches, cells = out_ref.shape
    blocks = cells // LANES
    per = 2 * local * blocks
    devices = rows_ref.shape[0] // per
    onehot = jnp.concatenate(owners(counts_ref[...], half, devices), axis=0).T
    copies = []
    for m in range(local):
        for part in range(2):
            wide = blocks // 2
            x = jnp.concatenate(
                [gather_rows(rows_ref, (k * local + m) * blocks + part * wide, per, devices, wide) for k in range(2)],
                axis=0,
            )
            columns = pl.ds(part * wide * LANES, wide * LANES)
            out_ref[m, :, columns] = pick(onehot, x)
            copies.append(
                pltpu.make_async_copy(
                    out_ref.at[m, :, columns], out_hbm.at[m, :, columns], sems.at[2 * m + part]
                )
            )
            copies[-1].start()
    for copy in copies:
        copy.wait()


HBM = pl.BlockSpec(memory_space=pltpu.HBM)
WHOLE = pl.BlockSpec(memory_space=pltpu.VMEM)
SCALAR = pl.BlockSpec(memory_space=pltpu.SMEM)


def call(kernel, out_shapes, inputs, ins=None, outs=None, scratch=(), aliases={}, limit=VMEM_LIMIT):
    return pl.pallas_call(
        kernel,
        out_shape=[jax.ShapeDtypeStruct(s, F32) for s in out_shapes],
        in_specs=ins or [WHOLE] * len(inputs),
        out_specs=outs or [WHOLE] * len(out_shapes),
        scratch_shapes=list(scratch),
        input_output_aliases=aliases,
        compiler_params=pltpu.CompilerParams(vmem_limit_bytes=limit),
    )(*inputs)


def exchange(x, name):
    with jax.named_scope(name):
        rows = x.reshape(-1, 1, LANES)
        return lax.all_to_all(rows, AXES, split_axis=0, concat_axis=0, tiled=True).reshape(-1, LANES)


def per_device(background, obs_ensemble, obs_value, obs_precision, obs_count):
    devices = lax.axis_size(AXES)
    local, patches, cells = background.shape
    slots = obs_ensemble.shape[2]
    half = slots // 2
    members = local * devices
    counts = obs_count.reshape(1, patches)
    mine = lax.axis_index(AXES).astype(jnp.int32).reshape(1)
    obs_rows = (slots + half) // LANES * local
    state_rows = 2 * local * cells // LANES
    pieces = 4
    (obs_sent,) = call(
        pack_obs_kernel,
        [(devices * obs_rows, LANES)],
        (counts, obs_ensemble),
        ins=[HBM, HBM],
        outs=[HBM],
        scratch=[
            pltpu.VMEM((1, patches), jnp.int32),
            pltpu.VMEM((local, pieces, patches, slots // pieces), F32),
            pltpu.VMEM((devices * obs_rows, LANES), F32),
            pltpu.SemaphoreType.DMA((local * pieces + 1,)),
        ],
        limit=None,
    )
    obs = exchange(obs_sent, "obs_exchange")
    states_sent, rows = call(
        pack_states_kernel,
        [(devices * (state_rows + 1), LANES), (8, slots)],
        (mine, counts, background, obs_value, obs_precision),
        ins=[SCALAR] + [WHOLE] * 4,
        limit=None,
    )
    states_sent = states_sent.reshape(devices, state_rows + 1, 1, LANES)
    (sums,) = call(functools.partial(sums_kernel, local=local), [(devices, 1, LANES)], (obs, rows))
    (states_sent,) = call(
        place_kernel,
        [states_sent.shape],
        (sums, states_sent),
        ins=[WHOLE, HBM],
        outs=[HBM],
        scratch=[pltpu.SemaphoreType.DMA],
        aliases={1: 0},
        limit=None,
    )
    states = exchange(states_sent, "states_exchange")
    powers, side = call(
        functools.partial(gram_kernel, local=local),
        [obs.shape, (2, 24, members)],
        (obs, rows),
        scratch=[pltpu.VMEM((2, members + 16, slots), BF16)] * 2,
        aliases={0: 0},
    )
    (update,) = call(
        functools.partial(update_kernel, local=local),
        [(devices * state_rows, LANES)],
        (states, powers, side),
        scratch=[
            pltpu.VMEM((2, members, 3 * members), BF16),
            pltpu.VMEM((2, 3 * members, 2 * members), BF16),
            pltpu.VMEM((3 * members, cells), BF16),
        ],
    )
    returned = exchange(update, "return_exchange")
    (analysis,) = call(
        functools.partial(unpack_kernel, half=half),
        [(local, patches, cells)],
        (counts, returned),
        outs=[HBM],
        scratch=[pltpu.VMEM((local, patches, cells), F32), pltpu.SemaphoreType.DMA((2 * local,))],
    )
    return analysis


def solution(mesh):
    placed = (P(AXES, None, None), P(AXES, None, None), P(), P(), P())
    return jax.shard_map(
        per_device, mesh=mesh, in_specs=placed, out_specs=P(AXES, None, None), check_vma=False
    )
```

```python
import functools

import jax
import jax.numpy as jnp
from jax import lax
from jax.experimental import pallas as pl
from jax.experimental.pallas import tpu as pltpu
from jax.sharding import PartitionSpec as P

SWEEPS = 8
LANES = 128
AXES = ("grp", "mem")
F32 = jnp.float32
BF16 = jnp.bfloat16
VMEM_LIMIT = 12 << 20


def dot(a, b):
    return jnp.dot(a, b, preferred_element_type=F32)


def dot_nt(a, b):
    return lax.dot_general(a, b, (((1,), (1,)), ((), ())), preferred_element_type=F32)


def exact_dot(a, b):
    return jnp.dot(a, b, preferred_element_type=F32, precision=lax.Precision.HIGHEST)


def halves(x):
    high = x.astype(BF16)
    return high, (x - high.astype(F32)).astype(BF16)


def thirds(x):
    high = x.astype(BF16)
    rest = x - high.astype(F32)
    mid = rest.astype(BF16)
    return high, mid, (rest - mid.astype(F32)).astype(BF16)


def left_form(x):
    high, low = halves(x)
    return jnp.concatenate([high, high, low], axis=1)


def right_form(x):
    high, low = halves(x)
    return jnp.concatenate([high, low, high], axis=0)


def owners(counts, half, devices):
    patches = counts.shape[1]
    heavy = (counts > half).astype(F32)
    before = lax.broadcasted_iota(jnp.int32, (patches, patches), 0) < lax.broadcasted_iota(
        jnp.int32, (patches, patches), 1
    )
    rank = dot(jnp.broadcast_to(heavy, (8, patches)).astype(BF16), before.astype(F32).astype(BF16))[:1]
    position = lax.broadcasted_iota(jnp.int32, (1, patches), 1).astype(F32)
    device = lax.broadcasted_iota(jnp.int32, (devices, patches), 0).astype(F32)
    heavies = jnp.where((device == rank) & (heavy > 0.0), 1.0, 0.0)
    lights = jnp.where((device == position - rank) & (heavy == 0.0), 1.0, 0.0)
    return heavies, lights


def store_rows(ref, first, stride, x):
    for j in range(x.shape[1] // LANES):
        ref[pl.ds(first + j, x.shape[0], stride=stride), :] = x[:, j * LANES : (j + 1) * LANES]


def gather_rows(ref, first, stride, rows, blocks):
    return jnp.concatenate([ref[pl.ds(first + j, rows, stride=stride), :] for j in range(blocks)], axis=1)


def load_rows(ref, first, rows, blocks):
    return jnp.concatenate([ref[first + j * rows : first + (j + 1) * rows] for j in range(blocks)], axis=1)


def pick(onehot, x):
    chosen = onehot.astype(BF16)
    return dot(jnp.concatenate([chosen] * 3, axis=1), jnp.concatenate(thirds(x), axis=0))


def pack_obs_kernel(counts_hbm, obs_hbm, out_hbm, counts_ref, obs_ref, out_ref, table_ref, table, sems, *, slots):
    patches = counts_ref.shape[1]
    blocks = slots // LANES
    each = patches * blocks
    local = obs_hbm.shape[0] // each
    devices, per = out_hbm.shape[:2]
    count_copy = pltpu.make_async_copy(counts_hbm, counts_ref, sems.at[0])
    count_copy.start()
    copies = []
    for m in range(local):
        span = pl.ds(m * each, each)
        copies.append(pltpu.make_async_copy(obs_hbm.at[span], obs_ref.at[span], sems.at[1 + m]))
        copies[-1].start()
    count_copy.wait()
    onehots = owners(counts_ref[...], slots // 2, devices)
    position = lax.broadcasted_iota(jnp.int32, (8, patches), 1).astype(F32).astype(BF16)
    index = [dot_nt(position, onehot.astype(BF16)).astype(jnp.int32) for onehot in onehots]
    start = [(p >> 3) * (8 * blocks) + (p & 7) for p in index]
    row = lax.broadcasted_iota(jnp.int32, (8, devices), 0)
    table_ref[...] = jnp.where(row == 0, start[0], start[1])
    table_copy = pltpu.make_async_copy(table_ref, table, sems.at[1 + local])
    table_copy.start()
    table_copy.wait()
    sent = []
    for m in range(local):
        copies[m].wait()

        @pl.loop(0, devices, unroll=8)
        def _(d):
            heavy = m * each + table[0, d]
            light = m * each + table[1, d]
            out_ref[d, m * blocks : (m + 1) * blocks, :] = obs_ref[pl.ds(heavy, blocks, stride=8), :]
            first = local * blocks + m * blocks // 2
            out_ref[d, first : first + blocks // 2, :] = obs_ref[pl.ds(light, blocks // 2, stride=8), :]

        first = m * blocks
        last = first + blocks if m < local - 1 else per
        sent.append(
            pltpu.make_async_copy(
                out_ref.at[:, first:last], out_hbm.at[:, first:last], sems.at[2 + local + m]
            )
        )
        sent[-1].start()
    for copy in sent:
        copy.wait()


def pack_states_kernel(mine_ref, counts_ref, states_ref, value_ref, precision_ref, out_hbm, rows_ref, out_ref, sem):
    local, patches, cells = states_ref.shape
    slots = value_ref.shape[1]
    blocks = cells // LANES
    per = 2 * local * blocks + 1
    devices = out_ref.shape[0] // per
    counts = counts_ref[...]
    heavies, lights = owners(counts, slots // 2, devices)
    both = jnp.concatenate([heavies, lights], axis=0)
    for m in range(local):
        chosen = pick(both, states_ref[m])
        for k in range(2):
            store_rows(out_ref, (k * local + m) * blocks, per, chosen[k * devices : (k + 1) * devices])
    out_ref[pl.ds(per - 1, devices, stride=per), :] = jnp.zeros((devices, LANES), F32)
    copy = pltpu.make_async_copy(out_ref, out_hbm, sem)
    copy.start()
    here = lax.broadcasted_iota(jnp.int32, (devices, patches), 0) == mine_ref[0]
    own = [jnp.sum(jnp.where(here, onehot, 0.0), axis=0, keepdims=True) for onehot in (heavies, lights)]
    both = jnp.concatenate(own + [jnp.zeros((6, patches), F32)], axis=0)
    values = pick(both, value_ref[...])
    precisions = pick(both, precision_ref[...])
    slot = lax.broadcasted_iota(jnp.int32, (1, slots), 1).astype(F32)
    rows = []
    for k in range(2):
        count = jnp.sum(own[k] * counts.astype(F32), axis=1, keepdims=True)
        live = jnp.where(slot < count, 1.0, 0.0)
        rows += [values[k : k + 1], precisions[k : k + 1], live]
    rows_ref[...] = jnp.concatenate(rows + [jnp.zeros((2, slots), F32)], axis=0)
    copy.wait()


def obs_columns(obs_ref, rows_ref, local):
    slots = rows_ref.shape[1]
    half = slots // 2
    per = (slots + half) // LANES * local
    devices = obs_ref.shape[0] // per
    for k in range(2):
        width = slots if k == 0 else half
        base = 0 if k == 0 else local * (slots // LANES)
        for c in range(width // LANES):
            columns = slice(c * LANES, (c + 1) * LANES)
            parts = [
                obs_ref[pl.ds(base + m * (width // LANES) + c, devices, stride=per), :] for m in range(local)
            ]
            mean = sum(jnp.sum(p, axis=0, keepdims=True) for p in parts) * (1.0 / (local * devices))
            value, precision, live = (rows_ref[3 * k + i : 3 * k + i + 1, columns] for i in range(3))
            yield k, columns, [p - mean for p in parts], value - mean, precision, live


def sums_kernel(obs_ref, rows_ref, states_hbm, out_hbm, row_ref, sem, *, local):
    devices, per = out_hbm.shape[:2]
    members = local * devices
    misfit = jnp.zeros((1, LANES), F32)
    expected = jnp.zeros((1, LANES), F32)
    for _, _, parts, innov, precision, live in obs_columns(obs_ref, rows_ref, local):
        spread = sum(jnp.sum(p * p, axis=0, keepdims=True) for p in parts) * (1.0 / (members - 1.0))
        misfit += precision * live * innov * innov
        expected += live * (1.0 + precision * spread)
    lane = lax.broadcasted_iota(jnp.int32, (1, LANES), 1)
    row = jnp.where(
        lane == 0,
        jnp.sum(misfit, axis=1, keepdims=True),
        jnp.where(lane == 1, jnp.sum(expected, axis=1, keepdims=True), 0.0),
    )
    row_ref[...] = jnp.broadcast_to(row[None], row_ref.shape)
    copy = pltpu.make_async_copy(row_ref, out_hbm.at[:, per - 1], sem)
    copy.start()
    copy.wait()


def gram_kernel(
    obs_ref, rows_ref, counts_ref, powers_ref, fourth_ref, side_ref, spread_hbm, high_ref, low_ref, spread_ref, sem, *, local
):
    slots = rows_ref.shape[1]
    members = side_ref.shape[2]
    devices = members // local
    spread_ref[...] = jnp.concatenate(owners(counts_ref[...], slots // 2, devices), axis=0).T
    copy = pltpu.make_async_copy(spread_ref, spread_hbm, sem)
    copy.start()
    for k, columns, parts, innov, precision, live in obs_columns(obs_ref, rows_ref, local):
        scale = jnp.sqrt(precision * live)
        for m in range(local):
            high, low = halves(parts[m] * scale)
            high_ref[k, m * devices : (m + 1) * devices, columns] = high
            low_ref[k, m * devices : (m + 1) * devices, columns] = low
        high, low = halves(jnp.broadcast_to(scale * innov, (16, LANES)))
        high_ref[k, members:, columns] = high
        low_ref[k, members:, columns] = low
    diagonal = lax.broadcasted_iota(jnp.int32, (members, members), 0) == lax.broadcasted_iota(
        jnp.int32, (members, members), 1
    )
    for k in range(2):
        width = slots if k == 0 else slots // 2
        high, low = high_ref[k, :, :width], low_ref[k, :, :width]
        gram = dot_nt(high, high[:members]) + dot_nt(high, low[:members]) + dot_nt(low, high[:members])
        forcing = gram[members : members + 8]
        gram = gram[:members]
        size = jnp.sqrt(jnp.sum(jnp.sum(gram * gram, axis=0, keepdims=True), axis=1, keepdims=True))
        unit = gram / jnp.maximum(size, 1e-30)
        trace = jnp.sum(
            jnp.sum(jnp.where(diagonal, unit, 0.0), axis=0, keepdims=True), axis=1, keepdims=True
        )
        second = exact_dot(unit, unit)
        for i, power in enumerate((unit, second, exact_dot(unit, second))):
            for h in range(members // LANES):
                first = ((k * 3 + i) * (members // LANES) + h) * members
                powers_ref[first : first + members] = power[:, h * LANES : (h + 1) * LANES]
        fourth = exact_dot(second, second)
        for h in range(members // LANES):
            first = (k * (members // LANES) + h) * members
            fourth_ref[first : first + members] = fourth[:, h * LANES : (h + 1) * LANES]
        side_ref[k] = jnp.concatenate(
            [forcing, jnp.broadcast_to(size, (8, members)), jnp.broadcast_to(trace, (8, members))], axis=0
        )
    copy.wait()


def update_kernel(
    states_ref, powers_ref, fourth_ref, side_ref, out_ref, s_left, s_right, z_right, states_right, center_ref, *, local
):
    members = side_ref.shape[2]
    devices = members // local
    per = states_ref.shape[0] // devices
    blocks = out_ref.shape[0] // devices // (2 * local)
    total = jnp.sum(states_ref[pl.ds(per - 1, devices, stride=per), :], axis=0, keepdims=True)
    lane = lax.broadcasted_iota(jnp.int32, total.shape, 1)
    misfit = jnp.sum(jnp.where(lane == 0, total, 0.0), axis=1, keepdims=True)
    expected = jnp.sum(jnp.where(lane == 1, total, 0.0), axis=1, keepdims=True)
    squared = misfit / expected
    inflation = jnp.sqrt(squared)
    diagonal = lax.broadcasted_iota(jnp.int32, (members, members), 0) == lax.broadcasted_iota(
        jnp.int32, (members, members), 1
    )
    free = members - 1.0

    def plus_diagonal(x, value):
        return x + jnp.where(diagonal, value, 0.0)

    def put(k, s):
        s_left[k] = left_form(s)
        s_right[k] = right_form(s)

    def square(k):
        high = s_left[k, :, :members]
        cross = dot(high, s_right[k, members : 2 * members])
        return dot(high, s_right[k, :members]) + (cross + cross.T)

    def refine(k, product):
        s = s_left[k, :, :members].astype(F32) + s_left[k, :, 2 * members :].astype(F32)
        return dot(left_form(plus_diagonal(0.25 * product - 1.5 * s, 2.25)), s_right[k])

    def advance(k):
        z = z_right[k, :members].astype(F32) + z_right[k, members : 2 * members].astype(F32)
        return 1.5 * z - 0.5 * dot(s_left[k], z_right[k])

    scalers = []
    for k in range(2):
        size, trace = side_ref[k, 8:9, :1], side_ref[k, 16:17, :1]
        strength = squared * size
        scaler = jnp.sqrt(free * free * members + strength * (2.0 * free * trace + strength))
        scalers.append(scaler)
        a, b = free / scaler, strength / scaler
        f = 1.5 - 0.5 * a
        s1 = (a * f * f, b * f * (f - a), b * b * (0.25 * a - f), 0.25 * b * b * b)
        d = (1.5 - 0.5 * s1[0], -0.5 * s1[1], -0.5 * s1[2], -0.5 * s1[3])
        h = -0.5 * b
        z2 = (f * d[0], f * d[1] + h * d[0], f * d[2] + h * d[1], f * d[3] + h * d[2], h * d[3])
        halfs = members // LANES
        powers = [load_rows(powers_ref, (k * 3 + i) * halfs * members, members, halfs) for i in range(3)]
        powers.append(load_rows(fourth_ref, k * halfs * members, members, halfs))
        put(k, plus_diagonal(sum(c * p for c, p in zip(s1[1:], powers)), s1[0]))
        z_right[k] = right_form(plus_diagonal(sum(c * p for c, p in zip(z2[1:], powers)), z2[0]))
    for k in range(2):
        put(k, refine(k, square(k)))
        for c in range(blocks):
            rows = [(k * local + m) * blocks + c for m in range(local)]
            parts = [states_ref[pl.ds(r, devices, stride=per), :] for r in rows]
            center = sum(jnp.sum(p, axis=0, keepdims=True) for p in parts) * (1.0 / members)
            columns = slice(c * LANES, (c + 1) * LANES)
            center_ref[k, :, columns] = jnp.broadcast_to(center, (8, LANES))
            for m in range(local):
                high, low = halves(parts[m] - center)
                for i, piece in enumerate((high, low, high)):
                    first = i * members + m * devices
                    states_right[k, first : first + devices, columns] = piece

    def sweep(_, carry):
        for k in range(2):
            s = refine(k, square(k))
            z = advance(k)
            put(k, s)
            z_right[k] = right_form(z)
        return carry

    lax.fori_loop(0, SWEEPS - 3, sweep, 0)
    for k in range(2):
        root = advance(k) / jnp.sqrt(scalers[k])
        forcing = inflation * side_ref[k, :1]
        half_way = jnp.sum(root * forcing, axis=1, keepdims=True)
        shifts = jnp.sum(root * half_way, axis=0, keepdims=True)
        transform = inflation * (free**0.5 * root + shifts)
        update = dot(left_form(transform), states_right[k]) + center_ref[k, :1]
        for c in range(blocks):
            for m in range(local):
                piece = update[m * devices : (m + 1) * devices, c * LANES : (c + 1) * LANES]
                out_ref[pl.ds((k * local + m) * blocks + c, devices, stride=2 * local * blocks), :] = piece


def unpack_kernel(spread_ref, rows_ref, out_hbm, out_ref, sems):
    local, patches, cells = out_ref.shape
    blocks = cells // LANES
    per = 2 * local * blocks
    devices = rows_ref.shape[0] // per
    onehot = spread_ref[...]
    copies = []
    for m in range(local):
        for part in range(2):
            wide = blocks // 2
            x = jnp.concatenate(
                [gather_rows(rows_ref, (k * local + m) * blocks + part * wide, per, devices, wide) for k in range(2)],
                axis=0,
            )
            columns = pl.ds(part * wide * LANES, wide * LANES)
            out_ref[m, :, columns] = pick(onehot, x)
            copies.append(
                pltpu.make_async_copy(
                    out_ref.at[m, :, columns], out_hbm.at[m, :, columns], sems.at[2 * m + part]
                )
            )
            copies[-1].start()
    for copy in copies:
        copy.wait()


HBM = pl.BlockSpec(memory_space=pltpu.HBM)
WHOLE = pl.BlockSpec(memory_space=pltpu.VMEM)
SCALAR = pl.BlockSpec(memory_space=pltpu.SMEM)


def call(kernel, out_shapes, inputs, ins=None, outs=None, scratch=(), aliases={}, limit=VMEM_LIMIT):
    ins = ins or [WHOLE] * len(inputs)
    outs = outs or [WHOLE] * len(out_shapes)
    inputs = [pltpu.with_memory_space_constraint(x, pltpu.HBM) if s is HBM else x for x, s in zip(inputs, ins)]
    return pl.pallas_call(
        kernel,
        out_shape=[
            pltpu.HBM(shape, F32) if s is HBM else jax.ShapeDtypeStruct(shape, F32)
            for shape, s in zip(out_shapes, outs)
        ],
        in_specs=ins,
        out_specs=outs,
        scratch_shapes=list(scratch),
        input_output_aliases=aliases,
        compiler_params=pltpu.CompilerParams(vmem_limit_bytes=limit),
    )(*inputs)


def exchange(x, name):
    with jax.named_scope(name):
        rows = x.reshape(-1, 1, LANES)
        return lax.all_to_all(rows, AXES, split_axis=0, concat_axis=0, tiled=True).reshape(-1, LANES)


def per_device(background, obs_ensemble, obs_value, obs_precision, obs_count):
    devices = lax.axis_size(AXES)
    local, patches, cells = background.shape
    slots = obs_ensemble.shape[2]
    members = local * devices
    counts = obs_count.reshape(1, patches)
    mine = lax.axis_index(AXES).astype(jnp.int32).reshape(1)
    obs_rows = 3 * slots // 2 // LANES * local
    state_rows = 2 * local * cells // LANES
    blocks = slots // LANES
    in_memory = obs_ensemble.reshape(local, patches // 8, 8, blocks, LANES).swapaxes(2, 3).reshape(-1, LANES)
    (obs_sent,) = call(
        functools.partial(pack_obs_kernel, slots=slots),
        [(devices, obs_rows, LANES)],
        (counts, in_memory),
        ins=[HBM, HBM],
        outs=[HBM],
        scratch=[
            pltpu.VMEM((1, patches), jnp.int32),
            pltpu.VMEM(in_memory.shape, F32),
            pltpu.VMEM((devices, obs_rows, LANES), F32),
            pltpu.VMEM((8, devices), jnp.int32),
            pltpu.SMEM((8, devices), jnp.int32),
            pltpu.SemaphoreType.DMA((2 * local + 2,)),
        ],
    )
    obs = exchange(obs_sent, "obs_exchange")
    states_sent, rows = call(
        pack_states_kernel,
        [(devices * (state_rows + 1), LANES), (8, slots)],
        (mine, counts, background, obs_value, obs_precision),
        ins=[SCALAR] + [WHOLE] * 4,
        outs=[HBM, WHOLE],
        scratch=[pltpu.VMEM((devices * (state_rows + 1), LANES), F32), pltpu.SemaphoreType.DMA],
    )
    states_sent = states_sent.reshape(devices, state_rows + 1, 1, LANES)
    (states_sent,) = call(
        functools.partial(sums_kernel, local=local),
        [states_sent.shape],
        (obs, rows, states_sent),
        ins=[WHOLE, WHOLE, HBM],
        outs=[HBM],
        scratch=[pltpu.VMEM((devices, 1, LANES), F32), pltpu.SemaphoreType.DMA],
        aliases={2: 0},
    )
    states = exchange(states_sent, "states_exchange")
    powers, fourth, side, spread = call(
        functools.partial(gram_kernel, local=local),
        [obs.shape, (2 * members * members // LANES, LANES), (2, 24, members), (patches, members)],
        (obs, rows, counts),
        outs=[WHOLE, WHOLE, WHOLE, HBM],
        scratch=[
            pltpu.VMEM((2, members + 16, slots), BF16),
            pltpu.VMEM((2, members + 16, slots), BF16),
            pltpu.VMEM((patches, members), F32),
            pltpu.SemaphoreType.DMA,
        ],
        aliases={0: 0},
    )
    (update,) = call(
        functools.partial(update_kernel, local=local),
        [(devices * state_rows, LANES)],
        (states, powers, fourth, side),
        scratch=[
            pltpu.VMEM((2, members, 3 * members), BF16),
            pltpu.VMEM((2, 3 * members, members), BF16),
            pltpu.VMEM((2, 3 * members, members), BF16),
            pltpu.VMEM((2, 3 * members, cells), BF16),
            pltpu.VMEM((2, 8, cells), F32),
        ],
    )
    returned = exchange(update, "return_exchange")
    (analysis,) = call(
        unpack_kernel,
        [(local, patches, cells)],
        (spread, returned),
        outs=[HBM],
        scratch=[pltpu.VMEM((local, patches, cells), F32), pltpu.SemaphoreType.DMA((2 * local,))],
    )
    return analysis


def solution(mesh):
    placed = (P(AXES, None, None), P(AXES, None, None), P(), P(), P())
    return jax.shard_map(
        per_device, mesh=mesh, in_specs=placed, out_specs=P(AXES, None, None), check_vma=False
    )
```

```python
import functools

import jax
import jax.numpy as jnp
from jax import lax
from jax.experimental import pallas as pl
from jax.experimental.pallas import tpu as pltpu
from jax.sharding import PartitionSpec as P

SWEEPS = 8
LANES = 128
AXES = ("grp", "mem")
F32 = jnp.float32
BF16 = jnp.bfloat16
VMEM_LIMIT = 12 << 20
IN_PIECES = 2
OUT_PIECES = 4


def dot(a, b):
    return jnp.dot(a, b, preferred_element_type=F32)


def dot_nt(a, b):
    return lax.dot_general(a, b, (((1,), (1,)), ((), ())), preferred_element_type=F32)


def exact_dot(a, b):
    return jnp.dot(a, b, preferred_element_type=F32, precision=lax.Precision.HIGHEST)


def halves(x):
    high = x.astype(BF16)
    return high, (x - high.astype(F32)).astype(BF16)


def thirds(x):
    high = x.astype(BF16)
    rest = x - high.astype(F32)
    mid = rest.astype(BF16)
    return high, mid, (rest - mid.astype(F32)).astype(BF16)


def left_form(x):
    high, low = halves(x)
    return jnp.concatenate([high, high, low], axis=1)


def right_form(x):
    high, low = halves(x)
    return jnp.concatenate([high, low, high], axis=0)


def ranks(counts, half):
    patches = counts.shape[1]
    heavy = (counts > half).astype(F32)
    before = lax.broadcasted_iota(jnp.int32, (patches, patches), 0) < lax.broadcasted_iota(
        jnp.int32, (patches, patches), 1
    )
    rank = dot(jnp.broadcast_to(heavy, (8, patches)).astype(BF16), before.astype(F32).astype(BF16))[:1]
    return heavy, rank


def owners(counts, half, devices):
    patches = counts.shape[1]
    heavy, rank = ranks(counts, half)
    position = lax.broadcasted_iota(jnp.int32, (1, patches), 1).astype(F32)
    device = lax.broadcasted_iota(jnp.int32, (devices, patches), 0).astype(F32)
    heavies = jnp.where((device == rank) & (heavy > 0.0), 1.0, 0.0)
    lights = jnp.where((device == position - rank) & (heavy == 0.0), 1.0, 0.0)
    return heavies, lights


def store_rows(ref, first, stride, x):
    for j in range(x.shape[1] // LANES):
        ref[pl.ds(first + j, x.shape[0], stride=stride), :] = x[:, j * LANES : (j + 1) * LANES]


def load_rows(ref, first, rows, blocks):
    return jnp.concatenate([ref[first + j * rows : first + (j + 1) * rows] for j in range(blocks)], axis=1)


def pick(onehot, x):
    chosen = onehot.astype(BF16)
    return dot(jnp.concatenate([chosen] * 3, axis=1), jnp.concatenate(thirds(x), axis=0))


def pack_obs_kernel(counts_hbm, obs_hbm, out_hbm, counts_ref, obs_ref, out_ref, table_ref, table, sems, *, slots):
    patches = counts_ref.shape[1]
    blocks = slots // LANES
    each = patches * blocks
    local = obs_hbm.shape[0] // each
    devices, per = out_hbm.shape[:2]
    count_copy = pltpu.make_async_copy(counts_hbm, counts_ref, sems.at[0])
    count_copy.start()
    copies = []
    cut = each // IN_PIECES
    for i in range(local * IN_PIECES):
        span = pl.ds(i * cut, cut)
        copies.append(pltpu.make_async_copy(obs_hbm.at[span], obs_ref.at[span], sems.at[1 + i]))
        copies[-1].start()
    count_copy.wait()
    onehots = owners(counts_ref[...], slots // 2, devices)
    position = lax.broadcasted_iota(jnp.int32, (8, patches), 1).astype(F32).astype(BF16)
    index = [dot_nt(position, onehot.astype(BF16)).astype(jnp.int32) for onehot in onehots]
    start = [(p >> 3) * (8 * blocks) + (p & 7) for p in index]
    row = lax.broadcasted_iota(jnp.int32, (8, devices), 0)
    table_ref[...] = jnp.where(row == 0, start[0], start[1])
    table_copy = pltpu.make_async_copy(table_ref, table, sems.at[0])
    table_copy.start()
    table_copy.wait()
    sent = []
    for copy in copies:
        copy.wait()
    group = devices // OUT_PIECES
    for g in range(OUT_PIECES):

        @pl.loop(g * group, (g + 1) * group, unroll=32)
        def _(d):
            heavy = table[0, d]
            light = table[1, d]
            for m in range(local):
                out_ref[d, m * blocks : (m + 1) * blocks, :] = obs_ref[pl.ds(m * each + heavy, blocks, stride=8), :]
                at = local * blocks + m * blocks // 2
                out_ref[d, at : at + blocks // 2, :] = obs_ref[pl.ds(m * each + light, blocks // 2, stride=8), :]

        some = pl.ds(g * group, group)
        sent.append(pltpu.make_async_copy(out_ref.at[some], out_hbm.at[some], sems.at[1 + local * IN_PIECES + g]))
        sent[-1].start()
    for copy in sent:
        copy.wait()


def pack_states_kernel(mine_ref, counts_ref, states_ref, value_ref, precision_ref, out_hbm, rows_ref, out_ref, sem):
    local, patches, cells = states_ref.shape
    slots = value_ref.shape[1]
    blocks = cells // LANES
    per = 2 * local * blocks + 1
    devices = out_ref.shape[0] // per
    counts = counts_ref[...]
    heavies, lights = owners(counts, slots // 2, devices)
    both = jnp.concatenate([heavies, lights], axis=0)
    for m in range(local):
        chosen = pick(both, states_ref[m])
        for k in range(2):
            store_rows(out_ref, (k * local + m) * blocks, per, chosen[k * devices : (k + 1) * devices])
    out_ref[pl.ds(per - 1, devices, stride=per), :] = jnp.zeros((devices, LANES), F32)
    copy = pltpu.make_async_copy(out_ref, out_hbm, sem)
    copy.start()
    here = lax.broadcasted_iota(jnp.int32, (devices, patches), 0) == mine_ref[0]
    own = [jnp.sum(jnp.where(here, onehot, 0.0), axis=0, keepdims=True) for onehot in (heavies, lights)]
    both = jnp.concatenate(own + [jnp.zeros((6, patches), F32)], axis=0)
    values = pick(both, value_ref[...])
    precisions = pick(both, precision_ref[...])
    slot = lax.broadcasted_iota(jnp.int32, (1, slots), 1).astype(F32)
    rows = []
    for k in range(2):
        count = jnp.sum(own[k] * counts.astype(F32), axis=1, keepdims=True)
        live = jnp.where(slot < count, 1.0, 0.0)
        rows += [values[k : k + 1], precisions[k : k + 1], live]
    rows_ref[...] = jnp.concatenate(rows + [jnp.zeros((2, slots), F32)], axis=0)
    copy.wait()


def obs_columns(obs_ref, rows_ref, local):
    slots = rows_ref.shape[1]
    half = slots // 2
    per = (slots + half) // LANES * local
    devices = obs_ref.shape[0] // per
    for k in range(2):
        width = slots if k == 0 else half
        base = 0 if k == 0 else local * (slots // LANES)
        for c in range(width // LANES):
            columns = slice(c * LANES, (c + 1) * LANES)
            parts = [
                obs_ref[pl.ds(base + m * (width // LANES) + c, devices, stride=per), :] for m in range(local)
            ]
            mean = sum(jnp.sum(p, axis=0, keepdims=True) for p in parts) * (1.0 / (local * devices))
            value, precision, live = (rows_ref[3 * k + i : 3 * k + i + 1, columns] for i in range(3))
            yield k, columns, [p - mean for p in parts], value - mean, precision, live


def sums_kernel(obs_ref, rows_ref, states_hbm, out_hbm, row_ref, sem, *, local):
    devices, per = out_hbm.shape[:2]
    members = local * devices
    misfit = jnp.zeros((1, LANES), F32)
    expected = jnp.zeros((1, LANES), F32)
    for _, _, parts, innov, precision, live in obs_columns(obs_ref, rows_ref, local):
        spread = sum(jnp.sum(p * p, axis=0, keepdims=True) for p in parts) * (1.0 / (members - 1.0))
        misfit += precision * live * innov * innov
        expected += live * (1.0 + precision * spread)
    lane = lax.broadcasted_iota(jnp.int32, (1, LANES), 1)
    row = jnp.where(
        lane == 0,
        jnp.sum(misfit, axis=1, keepdims=True),
        jnp.where(lane == 1, jnp.sum(expected, axis=1, keepdims=True), 0.0),
    )
    row_ref[...] = jnp.broadcast_to(row[None], row_ref.shape)
    copy = pltpu.make_async_copy(row_ref, out_hbm.at[:, per - 1], sem)
    copy.start()
    copy.wait()


def gram_kernel(
    obs_ref, rows_ref, counts_ref, powers_ref, fourth_ref, side_ref, table_ref, high_ref, low_ref, *, local, tile
):
    slots = rows_ref.shape[1]
    members = side_ref.shape[2]
    devices = members // local
    heavy, rank = ranks(counts_ref[...], slots // 2)
    position = lax.broadcasted_iota(jnp.int32, rank.shape, 1).astype(F32)
    place = jnp.where(heavy > 0.0, 2.0 * rank, 2.0 * (position - rank) + 1.0)
    table_ref[...] = place.astype(jnp.int32) * tile
    for k, columns, parts, innov, precision, live in obs_columns(obs_ref, rows_ref, local):
        scale = jnp.sqrt(precision * live)
        for m in range(local):
            high, low = halves(parts[m] * scale)
            high_ref[k, m * devices : (m + 1) * devices, columns] = high
            low_ref[k, m * devices : (m + 1) * devices, columns] = low
        high, low = halves(jnp.broadcast_to(scale * innov, (16, LANES)))
        high_ref[k, members:, columns] = high
        low_ref[k, members:, columns] = low
    diagonal = lax.broadcasted_iota(jnp.int32, (members, members), 0) == lax.broadcasted_iota(
        jnp.int32, (members, members), 1
    )
    for k in range(2):
        width = slots if k == 0 else slots // 2
        high, low = high_ref[k, :, :width], low_ref[k, :, :width]
        gram = dot_nt(high, high[:members]) + dot_nt(high, low[:members]) + dot_nt(low, high[:members])
        forcing = gram[members : members + 8]
        gram = gram[:members]
        size = jnp.sqrt(jnp.sum(jnp.sum(gram * gram, axis=0, keepdims=True), axis=1, keepdims=True))
        unit = gram / jnp.maximum(size, 1e-30)
        trace = jnp.sum(
            jnp.sum(jnp.where(diagonal, unit, 0.0), axis=0, keepdims=True), axis=1, keepdims=True
        )
        second = exact_dot(unit, unit)
        for i, power in enumerate((unit, second, exact_dot(unit, second))):
            for h in range(members // LANES):
                first = ((k * 3 + i) * (members // LANES) + h) * members
                powers_ref[first : first + members] = power[:, h * LANES : (h + 1) * LANES]
        fourth = exact_dot(second, second)
        for h in range(members // LANES):
            first = (k * (members // LANES) + h) * members
            fourth_ref[first : first + members] = fourth[:, h * LANES : (h + 1) * LANES]
        side_ref[k] = jnp.concatenate(
            [forcing, jnp.broadcast_to(size, (8, members)), jnp.broadcast_to(trace, (8, members))], axis=0
        )


def update_kernel(
    states_ref, powers_ref, fourth_ref, side_ref, out_ref, s_ref, z_ref, states_right, center_ref, *, local
):
    members = side_ref.shape[2]
    devices = members // local
    per = states_ref.shape[0] // devices
    blocks = out_ref.shape[0] // devices // (2 * local)
    total = jnp.sum(states_ref[pl.ds(per - 1, devices, stride=per), :], axis=0, keepdims=True)
    lane = lax.broadcasted_iota(jnp.int32, total.shape, 1)
    misfit = jnp.sum(jnp.where(lane == 0, total, 0.0), axis=1, keepdims=True)
    expected = jnp.sum(jnp.where(lane == 1, total, 0.0), axis=1, keepdims=True)
    squared = misfit / expected
    inflation = jnp.sqrt(squared)
    diagonal = lax.broadcasted_iota(jnp.int32, (members, members), 0) == lax.broadcasted_iota(
        jnp.int32, (members, members), 1
    )
    free = members - 1.0

    def plus_diagonal(x, value):
        return x + jnp.where(diagonal, value, 0.0)

    def put(ref, k, x):
        ref[k, 0], ref[k, 1] = halves(x)

    def left(ref, k):
        return jnp.concatenate([ref[k, 0], ref[k, 0], ref[k, 1]], axis=1)

    def right(ref, k):
        return jnp.concatenate([ref[k, 0], ref[k, 1], ref[k, 0]], axis=0)

    def whole(ref, k):
        return ref[k, 0].astype(F32) + ref[k, 1].astype(F32)

    def square(k):
        return dot(left(s_ref, k), right(s_ref, k))

    def refine(k, product):
        s = whole(s_ref, k)
        return 2.25 * s + dot(left_form(0.25 * product - 1.5 * s), right(s_ref, k))

    def advance(k):
        return 1.5 * whole(z_ref, k) - 0.5 * dot(left(s_ref, k), right(z_ref, k))

    scalers = []
    for k in range(2):
        size, trace = side_ref[k, 8:9, :1], side_ref[k, 16:17, :1]
        strength = squared * size
        scaler = jnp.sqrt(free * free * members + strength * (2.0 * free * trace + strength))
        scalers.append(scaler)
        a, b = free / scaler, strength / scaler
        f = 1.5 - 0.5 * a
        s1 = (a * f * f, b * f * (f - a), b * b * (0.25 * a - f), 0.25 * b * b * b)
        d = (1.5 - 0.5 * s1[0], -0.5 * s1[1], -0.5 * s1[2], -0.5 * s1[3])
        h = -0.5 * b
        z2 = (f * d[0], f * d[1] + h * d[0], f * d[2] + h * d[1], f * d[3] + h * d[2], h * d[3])
        halfs = members // LANES
        powers = [load_rows(powers_ref, (k * 3 + i) * halfs * members, members, halfs) for i in range(3)]
        powers.append(load_rows(fourth_ref, k * halfs * members, members, halfs))
        put(s_ref, k, plus_diagonal(sum(c * p for c, p in zip(s1[1:], powers)), s1[0]))
        put(z_ref, k, plus_diagonal(sum(c * p for c, p in zip(z2[1:], powers)), z2[0]))
    for k in range(2):
        put(s_ref, k, refine(k, square(k)))
        for c in range(blocks):
            rows = [(k * local + m) * blocks + c for m in range(local)]
            parts = [states_ref[pl.ds(r, devices, stride=per), :] for r in rows]
            center = sum(jnp.sum(p, axis=0, keepdims=True) for p in parts) * (1.0 / members)
            columns = slice(c * LANES, (c + 1) * LANES)
            center_ref[k, :, columns] = jnp.broadcast_to(center, (8, LANES))
            for m in range(local):
                high, low = halves(parts[m] - center)
                for i, piece in enumerate((high, low, high)):
                    first = i * members + m * devices
                    states_right[k, first : first + devices, columns] = piece

    for _ in range(SWEEPS - 3):
        products = [square(k) for k in range(2)]
        roots = [advance(k) for k in range(2)]
        for k in range(2):
            s = refine(k, products[k])
            put(s_ref, k, s)
            put(z_ref, k, roots[k])

    for k in range(2):
        root = advance(k)
        forcing = squared / scalers[k] * side_ref[k, :1]
        half_way = jnp.sum(root * forcing, axis=1, keepdims=True)
        shifts = jnp.sum(root * half_way, axis=0, keepdims=True)
        transform = (inflation * free**0.5 / jnp.sqrt(scalers[k])) * root + shifts
        update = dot(left_form(transform), states_right[k]) + center_ref[k, :1]
        for c in range(blocks):
            for m in range(local):
                piece = update[m * devices : (m + 1) * devices, c * LANES : (c + 1) * LANES]
                out_ref[pl.ds((k * local + m) * blocks + c, devices, stride=2 * local * blocks), :] = piece


def unpack_kernel(table, rows_ref, out_hbm, out_ref, sems, *, local):
    patches = table.shape[1]
    tile = rows_ref.shape[0] // patches
    blocks = tile // local
    each = patches * blocks
    group = patches // OUT_PIECES
    copies = []
    for g in range(OUT_PIECES):

        @pl.loop(g * group, (g + 1) * group, unroll=32)
        def _(p):
            x = rows_ref[pl.ds(pl.multiple_of(table[0, p], tile), tile), :]
            first = (p >> 3) * (8 * blocks) + (p & 7)
            for m in range(local):
                out_ref[pl.ds(m * each + first, blocks, stride=8), :] = x[m * blocks : (m + 1) * blocks]

        for m in range(local):
            some = pl.ds(m * each + g * group * blocks, group * blocks)
            copies.append(
                pltpu.make_async_copy(out_ref.at[some], out_hbm.at[some], sems.at[m * OUT_PIECES + g])
            )
            copies[-1].start()
    for copy in copies:
        copy.wait()


HBM = pl.BlockSpec(memory_space=pltpu.HBM)
WHOLE = pl.BlockSpec(memory_space=pltpu.VMEM)
SCALAR = pl.BlockSpec(memory_space=pltpu.SMEM)


def call(kernel, out_shapes, inputs, ins=None, outs=None, types=None, scratch=(), aliases={}):
    ins = ins or [WHOLE] * len(inputs)
    outs = outs or [WHOLE] * len(out_shapes)
    inputs = [pltpu.with_memory_space_constraint(x, pltpu.HBM) if s is HBM else x for x, s in zip(inputs, ins)]
    return pl.pallas_call(
        kernel,
        out_shape=[
            pltpu.HBM(shape, kind) if s is HBM else jax.ShapeDtypeStruct(shape, kind)
            for shape, kind, s in zip(out_shapes, types or [F32] * len(outs), outs)
        ],
        in_specs=ins,
        out_specs=outs,
        scratch_shapes=list(scratch),
        input_output_aliases=aliases,
        compiler_params=pltpu.CompilerParams(vmem_limit_bytes=VMEM_LIMIT),
    )(*inputs)


def exchange(x, name):
    with jax.named_scope(name):
        rows = x.reshape(-1, 1, LANES)
        return lax.all_to_all(rows, AXES, split_axis=0, concat_axis=0, tiled=True).reshape(-1, LANES)


def per_device(background, obs_ensemble, obs_value, obs_precision, obs_count):
    devices = lax.axis_size(AXES)
    local, patches, cells = background.shape
    slots = obs_ensemble.shape[2]
    members = local * devices
    counts = obs_count.reshape(1, patches)
    mine = lax.axis_index(AXES).astype(jnp.int32).reshape(1)
    obs_rows = 3 * slots // 2 // LANES * local
    state_rows = 2 * local * cells // LANES
    blocks = slots // LANES
    in_memory = obs_ensemble.reshape(local, patches // 8, 8, blocks, LANES).swapaxes(2, 3).reshape(-1, LANES)
    (obs_sent,) = call(
        functools.partial(pack_obs_kernel, slots=slots),
        [(devices, obs_rows, LANES)],
        (counts, in_memory),
        ins=[HBM, HBM],
        outs=[HBM],
        scratch=[
            pltpu.VMEM((1, patches), jnp.int32),
            pltpu.VMEM(in_memory.shape, F32),
            pltpu.VMEM((devices, obs_rows, LANES), F32),
            pltpu.VMEM((8, devices), jnp.int32),
            pltpu.SMEM((8, devices), jnp.int32),
            pltpu.SemaphoreType.DMA((1 + local * IN_PIECES + OUT_PIECES,)),
        ],
    )
    obs = exchange(obs_sent, "obs_exchange")
    states_sent, rows = call(
        pack_states_kernel,
        [(devices * (state_rows + 1), LANES), (8, slots)],
        (mine, counts, background, obs_value, obs_precision),
        ins=[SCALAR] + [WHOLE] * 4,
        outs=[HBM, WHOLE],
        scratch=[pltpu.VMEM((devices * (state_rows + 1), LANES), F32), pltpu.SemaphoreType.DMA],
    )
    states_sent = states_sent.reshape(devices, state_rows + 1, 1, LANES)
    (states_sent,) = call(
        functools.partial(sums_kernel, local=local),
        [states_sent.shape],
        (obs, rows, states_sent),
        ins=[WHOLE, WHOLE, HBM],
        outs=[HBM],
        scratch=[pltpu.VMEM((devices, 1, LANES), F32), pltpu.SemaphoreType.DMA],
        aliases={2: 0},
    )
    states = exchange(states_sent, "states_exchange")
    powers, fourth, side, table = call(
        functools.partial(gram_kernel, local=local, tile=state_rows // 2),
        [obs.shape, (2 * members * members // LANES, LANES), (2, 24, members), (1, patches)],
        (obs, rows, counts),
        types=[F32, F32, F32, jnp.int32],
        scratch=[pltpu.VMEM((2, members + 16, slots), BF16)] * 2,
        aliases={0: 0},
    )
    (update,) = call(
        functools.partial(update_kernel, local=local),
        [(devices * state_rows, LANES)],
        (states, powers, fourth, side),
        scratch=[
            pltpu.VMEM((2, 2, members, members), BF16),
            pltpu.VMEM((2, 2, members, members), BF16),
            pltpu.VMEM((2, 3 * members, cells), BF16),
            pltpu.VMEM((2, 8, cells), F32),
        ],
    )
    returned = exchange(update, "return_exchange")
    (analysis,) = call(
        functools.partial(unpack_kernel, local=local),
        [(devices * state_rows, LANES)],
        (table, returned),
        ins=[SCALAR, WHOLE],
        outs=[HBM],
        scratch=[pltpu.VMEM((devices * state_rows, LANES), F32), pltpu.SemaphoreType.DMA((local * OUT_PIECES,))],
    )
    in_memory = analysis.reshape(local, patches // 8, cells // LANES, 8, LANES)
    return in_memory.swapaxes(2, 3).reshape(local, patches, cells)


def solution(mesh):
    placed = (P(AXES, None, None), P(AXES, None, None), P(), P(), P())
    return jax.shard_map(
        per_device, mesh=mesh, in_specs=placed, out_specs=P(AXES, None, None), check_vma=False
    )
```

```python
import functools

import jax
import jax.numpy as jnp
from jax import lax
from jax.experimental import pallas as pl
from jax.experimental.pallas import tpu as pltpu
from jax.sharding import PartitionSpec as P

SWEEPS = 8
LANES = 128
AXES = ("grp", "mem")
F32 = jnp.float32
BF16 = jnp.bfloat16
VMEM_LIMIT = 12 << 20
IN_PIECES = 2
OUT_PIECES = 4


def dot(a, b):
    return jnp.dot(a, b, preferred_element_type=F32)


def dot_nt(a, b):
    return lax.dot_general(a, b, (((1,), (1,)), ((), ())), preferred_element_type=F32)


def exact_dot(a, b):
    return jnp.dot(a, b, preferred_element_type=F32, precision=lax.Precision.HIGHEST)


def halves(x):
    high = x.astype(BF16)
    return high, (x - high.astype(F32)).astype(BF16)


def thirds(x):
    high = x.astype(BF16)
    rest = x - high.astype(F32)
    mid = rest.astype(BF16)
    return high, mid, (rest - mid.astype(F32)).astype(BF16)


def left_form(x):
    high, low = halves(x)
    return jnp.concatenate([high, high, low], axis=1)


def right_form(x):
    high, low = halves(x)
    return jnp.concatenate([high, low, high], axis=0)


def owners(counts, half, devices):
    patches = counts.shape[1]
    heavy = (counts > half).astype(F32)
    before = lax.broadcasted_iota(jnp.int32, (patches, patches), 0) < lax.broadcasted_iota(
        jnp.int32, (patches, patches), 1
    )
    rank = dot(jnp.broadcast_to(heavy, (8, patches)).astype(BF16), before.astype(F32).astype(BF16))[:1]
    position = lax.broadcasted_iota(jnp.int32, (1, patches), 1).astype(F32)
    device = lax.broadcasted_iota(jnp.int32, (devices, patches), 0).astype(F32)
    heavies = jnp.where((device == rank) & (heavy > 0.0), 1.0, 0.0)
    lights = jnp.where((device == position - rank) & (heavy == 0.0), 1.0, 0.0)
    return heavies, lights


def store_rows(ref, first, stride, x):
    for j in range(x.shape[1] // LANES):
        ref[pl.ds(first + j, x.shape[0], stride=stride), :] = x[:, j * LANES : (j + 1) * LANES]


def load_rows(ref, first, rows, blocks):
    return jnp.concatenate([ref[first + j * rows : first + (j + 1) * rows] for j in range(blocks)], axis=1)


def pick(onehot, x):
    chosen = onehot.astype(BF16)
    return dot(jnp.concatenate([chosen] * 3, axis=1), jnp.concatenate(thirds(x), axis=0))


def pack_obs_kernel(counts_hbm, obs_hbm, out_hbm, counts_ref, obs_ref, out_ref, table_ref, table, sems, *, slots):
    patches = counts_ref.shape[1]
    blocks = slots // LANES
    each = patches * blocks
    local = obs_hbm.shape[0] // each
    devices, per = out_hbm.shape[:2]
    count_copy = pltpu.make_async_copy(counts_hbm, counts_ref, sems.at[0])
    count_copy.start()
    copies = []
    cut = each // IN_PIECES
    for i in range(local * IN_PIECES):
        span = pl.ds(i * cut, cut)
        copies.append(pltpu.make_async_copy(obs_hbm.at[span], obs_ref.at[span], sems.at[1 + i]))
        copies[-1].start()
    count_copy.wait()
    onehots = owners(counts_ref[...], slots // 2, devices)
    position = lax.broadcasted_iota(jnp.int32, (8, patches), 1).astype(F32).astype(BF16)
    index = [dot_nt(position, onehot.astype(BF16)).astype(jnp.int32) for onehot in onehots]
    start = [(p >> 3) * (8 * blocks) + (p & 7) for p in index]
    row = lax.broadcasted_iota(jnp.int32, (8, devices), 0)
    table_ref[...] = jnp.where(row == 0, start[0], start[1])
    table_copy = pltpu.make_async_copy(table_ref, table, sems.at[0])
    table_copy.start()
    table_copy.wait()
    sent = []
    for copy in copies:
        copy.wait()
    group = devices // OUT_PIECES
    for g in range(OUT_PIECES):

        @pl.loop(g * group, (g + 1) * group, unroll=32)
        def _(d):
            heavy = table[0, d]
            light = table[1, d]
            for m in range(local):
                out_ref[d, m * blocks : (m + 1) * blocks, :] = obs_ref[pl.ds(m * each + heavy, blocks, stride=8), :]
                at = local * blocks + m * blocks // 2
                out_ref[d, at : at + blocks // 2, :] = obs_ref[pl.ds(m * each + light, blocks // 2, stride=8), :]

        some = pl.ds(g * group, group)
        sent.append(pltpu.make_async_copy(out_ref.at[some], out_hbm.at[some], sems.at[1 + local * IN_PIECES + g]))
        sent[-1].start()
    for copy in sent:
        copy.wait()


def pack_states_kernel(mine_ref, counts_ref, states_ref, value_ref, precision_ref, out_hbm, rows_ref, out_ref, sem):
    local, patches, cells = states_ref.shape
    slots = value_ref.shape[1]
    blocks = cells // LANES
    per = 2 * local * blocks + 1
    devices = out_ref.shape[0] // per
    counts = counts_ref[...]
    heavies, lights = owners(counts, slots // 2, devices)
    both = jnp.concatenate([heavies, lights], axis=0)
    for m in range(local):
        chosen = pick(both, states_ref[m])
        for k in range(2):
            store_rows(out_ref, (k * local + m) * blocks, per, chosen[k * devices : (k + 1) * devices])
    out_ref[pl.ds(per - 1, devices, stride=per), :] = jnp.zeros((devices, LANES), F32)
    copy = pltpu.make_async_copy(out_ref, out_hbm, sem)
    copy.start()
    here = lax.broadcasted_iota(jnp.int32, (devices, patches), 0) == mine_ref[0]
    own = [jnp.sum(jnp.where(here, onehot, 0.0), axis=0, keepdims=True) for onehot in (heavies, lights)]
    both = jnp.concatenate(own + [jnp.zeros((6, patches), F32)], axis=0)
    values = pick(both, value_ref[...])
    precisions = pick(both, precision_ref[...])
    slot = lax.broadcasted_iota(jnp.int32, (1, slots), 1).astype(F32)
    rows = []
    for k in range(2):
        count = jnp.sum(own[k] * counts.astype(F32), axis=1, keepdims=True)
        live = jnp.where(slot < count, 1.0, 0.0)
        rows += [values[k : k + 1], precisions[k : k + 1], live]
    rows_ref[...] = jnp.concatenate(rows + [jnp.zeros((2, slots), F32)], axis=0)
    copy.wait()


def obs_columns(obs_ref, rows_ref, local):
    slots = rows_ref.shape[1]
    half = slots // 2
    per = (slots + half) // LANES * local
    devices = obs_ref.shape[0] // per
    for k in range(2):
        width = slots if k == 0 else half
        base = 0 if k == 0 else local * (slots // LANES)
        for c in range(width // LANES):
            columns = slice(c * LANES, (c + 1) * LANES)
            parts = [
                obs_ref[pl.ds(base + m * (width // LANES) + c, devices, stride=per), :] for m in range(local)
            ]
            mean = sum(jnp.sum(p, axis=0, keepdims=True) for p in parts) * (1.0 / (local * devices))
            value, precision, live = (rows_ref[3 * k + i : 3 * k + i + 1, columns] for i in range(3))
            yield k, columns, [p - mean for p in parts], value - mean, precision, live


def sums_kernel(obs_ref, rows_ref, states_hbm, out_hbm, row_ref, sem, *, local):
    devices, per = out_hbm.shape[:2]
    members = local * devices
    misfit = jnp.zeros((1, LANES), F32)
    expected = jnp.zeros((1, LANES), F32)
    for _, _, parts, innov, precision, live in obs_columns(obs_ref, rows_ref, local):
        spread = sum(jnp.sum(p * p, axis=0, keepdims=True) for p in parts) * (1.0 / (members - 1.0))
        misfit += precision * live * innov * innov
        expected += live * (1.0 + precision * spread)
    lane = lax.broadcasted_iota(jnp.int32, (1, LANES), 1)
    row = jnp.where(
        lane == 0,
        jnp.sum(misfit, axis=1, keepdims=True),
        jnp.where(lane == 1, jnp.sum(expected, axis=1, keepdims=True), 0.0),
    )
    row_ref[...] = jnp.broadcast_to(row[None], row_ref.shape)
    copy = pltpu.make_async_copy(row_ref, out_hbm.at[:, per - 1], sem)
    copy.start()
    copy.wait()


def gram_kernel(
    obs_ref, rows_ref, counts_ref, powers_ref, fourth_ref, side_ref, spread_ref, high_ref, low_ref, *, local
):
    slots = rows_ref.shape[1]
    members = side_ref.shape[2]
    devices = members // local
    spread_ref[...] = jnp.concatenate(owners(counts_ref[...], slots // 2, devices), axis=0).T.astype(BF16)
    for k, columns, parts, innov, precision, live in obs_columns(obs_ref, rows_ref, local):
        scale = jnp.sqrt(precision * live)
        for m in range(local):
            high, low = halves(parts[m] * scale)
            high_ref[k, m * devices : (m + 1) * devices, columns] = high
            low_ref[k, m * devices : (m + 1) * devices, columns] = low
        high, low = halves(jnp.broadcast_to(scale * innov, (16, LANES)))
        high_ref[k, members:, columns] = high
        low_ref[k, members:, columns] = low
    diagonal = lax.broadcasted_iota(jnp.int32, (members, members), 0) == lax.broadcasted_iota(
        jnp.int32, (members, members), 1
    )
    for k in range(2):
        width = slots if k == 0 else slots // 2
        high, low = high_ref[k, :, :width], low_ref[k, :, :width]
        gram = dot_nt(high, high[:members]) + dot_nt(high, low[:members]) + dot_nt(low, high[:members])
        forcing = gram[members : members + 8]
        gram = gram[:members]
        size = jnp.sqrt(jnp.sum(jnp.sum(gram * gram, axis=0, keepdims=True), axis=1, keepdims=True))
        unit = gram / jnp.maximum(size, 1e-30)
        trace = jnp.sum(
            jnp.sum(jnp.where(diagonal, unit, 0.0), axis=0, keepdims=True), axis=1, keepdims=True
        )
        second = exact_dot(unit, unit)
        for i, power in enumerate((unit, second, exact_dot(unit, second))):
            for h in range(members // LANES):
                first = ((k * 3 + i) * (members // LANES) + h) * members
                powers_ref[first : first + members] = power[:, h * LANES : (h + 1) * LANES]
        fourth = exact_dot(second, second)
        for h in range(members // LANES):
            first = (k * (members // LANES) + h) * members
            fourth_ref[first : first + members] = fourth[:, h * LANES : (h + 1) * LANES]
        side_ref[k] = jnp.concatenate(
            [forcing, jnp.broadcast_to(size, (8, members)), jnp.broadcast_to(trace, (8, members))], axis=0
        )


def update_kernel(
    states_ref, powers_ref, fourth_ref, side_ref, out_ref, s_ref, z_ref, states_right, center_ref, *, local
):
    members = side_ref.shape[2]
    devices = members // local
    per = states_ref.shape[0] // devices
    blocks = out_ref.shape[0] // devices // (2 * local)
    total = jnp.sum(states_ref[pl.ds(per - 1, devices, stride=per), :], axis=0, keepdims=True)
    lane = lax.broadcasted_iota(jnp.int32, total.shape, 1)
    misfit = jnp.sum(jnp.where(lane == 0, total, 0.0), axis=1, keepdims=True)
    expected = jnp.sum(jnp.where(lane == 1, total, 0.0), axis=1, keepdims=True)
    squared = misfit / expected
    inflation = jnp.sqrt(squared)
    diagonal = lax.broadcasted_iota(jnp.int32, (members, members), 0) == lax.broadcasted_iota(
        jnp.int32, (members, members), 1
    )
    free = members - 1.0

    def plus_diagonal(x, value):
        return x + jnp.where(diagonal, value, 0.0)

    def put(ref, k, x):
        ref[k, 0], ref[k, 1] = halves(x)

    def left(ref, k):
        return jnp.concatenate([ref[k, 0], ref[k, 0], ref[k, 1]], axis=1)

    def right(ref, k):
        return jnp.concatenate([ref[k, 0], ref[k, 1], ref[k, 0]], axis=0)

    def whole(ref, k):
        return ref[k, 0].astype(F32) + ref[k, 1].astype(F32)

    def square(k):
        return dot(left(s_ref, k), right(s_ref, k))

    def refine(k, product):
        s = whole(s_ref, k)
        return 2.25 * s + dot(left_form(0.25 * product - 1.5 * s), right(s_ref, k))

    def advance(k):
        return 1.5 * whole(z_ref, k) - 0.5 * dot(left(s_ref, k), right(z_ref, k))

    scalers = []
    for k in range(2):
        size, trace = side_ref[k, 8:9, :1], side_ref[k, 16:17, :1]
        strength = squared * size
        scaler = jnp.sqrt(free * free * members + strength * (2.0 * free * trace + strength))
        scalers.append(scaler)
        a, b = free / scaler, strength / scaler
        f = 1.5 - 0.5 * a
        s1 = (a * f * f, b * f * (f - a), b * b * (0.25 * a - f), 0.25 * b * b * b)
        d = (1.5 - 0.5 * s1[0], -0.5 * s1[1], -0.5 * s1[2], -0.5 * s1[3])
        h = -0.5 * b
        z2 = (f * d[0], f * d[1] + h * d[0], f * d[2] + h * d[1], f * d[3] + h * d[2], h * d[3])
        halfs = members // LANES
        powers = [load_rows(powers_ref, (k * 3 + i) * halfs * members, members, halfs) for i in range(3)]
        powers.append(load_rows(fourth_ref, k * halfs * members, members, halfs))
        put(s_ref, k, plus_diagonal(sum(c * p for c, p in zip(s1[1:], powers)), s1[0]))
        put(z_ref, k, plus_diagonal(sum(c * p for c, p in zip(z2[1:], powers)), z2[0]))
    for k in range(2):
        put(s_ref, k, refine(k, square(k)))
        for c in range(blocks):
            rows = [(k * local + m) * blocks + c for m in range(local)]
            parts = [states_ref[pl.ds(r, devices, stride=per), :] for r in rows]
            center = sum(jnp.sum(p, axis=0, keepdims=True) for p in parts) * (1.0 / members)
            columns = slice(c * LANES, (c + 1) * LANES)
            center_ref[k, :, columns] = jnp.broadcast_to(center, (8, LANES))
            for m in range(local):
                high, low = halves(parts[m] - center)
                for i, piece in enumerate((high, low, high)):
                    first = i * members + m * devices
                    states_right[k, first : first + devices, columns] = piece

    for _ in range(SWEEPS - 3):
        products = [square(k) for k in range(2)]
        roots = [advance(k) for k in range(2)]
        for k in range(2):
            s = refine(k, products[k])
            put(s_ref, k, s)
            put(z_ref, k, roots[k])

    for k in range(2):
        root = advance(k)
        forcing = squared / scalers[k] * side_ref[k, :1]
        half_way = jnp.sum(root * forcing, axis=1, keepdims=True)
        shifts = jnp.sum(root * half_way, axis=0, keepdims=True)
        transform = (inflation * free**0.5 / jnp.sqrt(scalers[k])) * root + shifts
        update = dot(left_form(transform), states_right[k]) + center_ref[k, :1]
        for c in range(blocks):
            for m in range(local):
                piece = update[m * devices : (m + 1) * devices, c * LANES : (c + 1) * LANES]
                out_ref[pl.ds((k * local + m) * blocks + c, devices, stride=2 * local * blocks), :] = piece


def unpack_kernel(spread_ref, rows_ref, out_hbm, out_ref, sems):
    local, patches, cells = out_ref.shape
    blocks = cells // LANES
    per = 2 * local * blocks
    devices = rows_ref.shape[0] // per
    spread = jnp.concatenate([spread_ref[...]] * 2, axis=1)
    wide = blocks // 2
    copies = []
    for m in range(local):
        for part in range(2):
            x = jnp.concatenate(
                [
                    jnp.concatenate(
                        [
                            rows_ref[pl.ds((k * local + m) * blocks + part * wide + j, devices, stride=per), :]
                            for j in range(wide)
                        ],
                        axis=1,
                    )
                    for k in range(2)
                ],
                axis=0,
            )
            columns = pl.ds(part * wide * LANES, wide * LANES)
            out_ref[m, :, columns] = dot(spread, jnp.concatenate(halves(x), axis=0))
            copies.append(
                pltpu.make_async_copy(
                    out_ref.at[m, :, columns], out_hbm.at[m, :, columns], sems.at[2 * m + part]
                )
            )
            copies[-1].start()
    for copy in copies:
        copy.wait()


HBM = pl.BlockSpec(memory_space=pltpu.HBM)
WHOLE = pl.BlockSpec(memory_space=pltpu.VMEM)
SCALAR = pl.BlockSpec(memory_space=pltpu.SMEM)


def call(kernel, out_shapes, inputs, ins=None, outs=None, types=None, scratch=(), aliases={}):
    ins = ins or [WHOLE] * len(inputs)
    outs = outs or [WHOLE] * len(out_shapes)
    inputs = [pltpu.with_memory_space_constraint(x, pltpu.HBM) if s is HBM else x for x, s in zip(inputs, ins)]
    return pl.pallas_call(
        kernel,
        out_shape=[
            pltpu.HBM(shape, kind) if s is HBM else jax.ShapeDtypeStruct(shape, kind)
            for shape, kind, s in zip(out_shapes, types or [F32] * len(outs), outs)
        ],
        in_specs=ins,
        out_specs=outs,
        scratch_shapes=list(scratch),
        input_output_aliases=aliases,
        compiler_params=pltpu.CompilerParams(vmem_limit_bytes=VMEM_LIMIT),
    )(*inputs)


def exchange(x, name):
    with jax.named_scope(name):
        rows = x.reshape(-1, 1, LANES)
        return lax.all_to_all(rows, AXES, split_axis=0, concat_axis=0, tiled=True).reshape(-1, LANES)


def per_device(background, obs_ensemble, obs_value, obs_precision, obs_count):
    devices = lax.axis_size(AXES)
    local, patches, cells = background.shape
    slots = obs_ensemble.shape[2]
    members = local * devices
    counts = obs_count.reshape(1, patches)
    mine = lax.axis_index(AXES).astype(jnp.int32).reshape(1)
    obs_rows = 3 * slots // 2 // LANES * local
    state_rows = 2 * local * cells // LANES
    blocks = slots // LANES
    in_memory = obs_ensemble.reshape(local, patches // 8, 8, blocks, LANES).swapaxes(2, 3).reshape(-1, LANES)
    (obs_sent,) = call(
        functools.partial(pack_obs_kernel, slots=slots),
        [(devices, obs_rows, LANES)],
        (counts, in_memory),
        ins=[HBM, HBM],
        outs=[HBM],
        scratch=[
            pltpu.VMEM((1, patches), jnp.int32),
            pltpu.VMEM(in_memory.shape, F32),
            pltpu.VMEM((devices, obs_rows, LANES), F32),
            pltpu.VMEM((8, devices), jnp.int32),
            pltpu.SMEM((8, devices), jnp.int32),
            pltpu.SemaphoreType.DMA((1 + local * IN_PIECES + OUT_PIECES,)),
        ],
    )
    obs = exchange(obs_sent, "obs_exchange")
    states_sent, rows = call(
        pack_states_kernel,
        [(devices * (state_rows + 1), LANES), (8, slots)],
        (mine, counts, background, obs_value, obs_precision),
        ins=[SCALAR] + [WHOLE] * 4,
        outs=[HBM, WHOLE],
        scratch=[pltpu.VMEM((devices * (state_rows + 1), LANES), F32), pltpu.SemaphoreType.DMA],
    )
    states_sent = states_sent.reshape(devices, state_rows + 1, 1, LANES)
    (states_sent,) = call(
        functools.partial(sums_kernel, local=local),
        [states_sent.shape],
        (obs, rows, states_sent),
        ins=[WHOLE, WHOLE, HBM],
        outs=[HBM],
        scratch=[pltpu.VMEM((devices, 1, LANES), F32), pltpu.SemaphoreType.DMA],
        aliases={2: 0},
    )
    states = exchange(states_sent, "states_exchange")
    powers, fourth, side, spread = call(
        functools.partial(gram_kernel, local=local),
        [obs.shape, (2 * members * members // LANES, LANES), (2, 24, members), (patches, members)],
        (obs, rows, counts),
        types=[F32, F32, F32, BF16],
        scratch=[pltpu.VMEM((2, members + 16, slots), BF16)] * 2,
        aliases={0: 0},
    )
    (update,) = call(
        functools.partial(update_kernel, local=local),
        [(devices * state_rows, LANES)],
        (states, powers, fourth, side),
        scratch=[
            pltpu.VMEM((2, 2, members, members), BF16),
            pltpu.VMEM((2, 2, members, members), BF16),
            pltpu.VMEM((2, 3 * members, cells), BF16),
            pltpu.VMEM((2, 8, cells), F32),
        ],
    )
    returned = exchange(update, "return_exchange")
    (analysis,) = call(
        unpack_kernel,
        [(local, patches, cells)],
        (spread, returned),
        outs=[HBM],
        scratch=[pltpu.VMEM((local, patches, cells), F32), pltpu.SemaphoreType.DMA((2 * local,))],
    )
    return analysis


def solution(mesh):
    placed = (P(AXES, None, None), P(AXES, None, None), P(), P(), P())
    return jax.shard_map(
        per_device, mesh=mesh, in_specs=placed, out_specs=P(AXES, None, None), check_vma=False
    )
```

```python
import functools

import jax
import jax.numpy as jnp
from jax import lax
from jax.experimental import pallas as pl
from jax.experimental.pallas import tpu as pltpu
from jax.sharding import PartitionSpec as P

SWEEPS = 8
LANES = 128
AXES = ("grp", "mem")
F32 = jnp.float32
BF16 = jnp.bfloat16
VMEM_LIMIT = 12 << 20
IN_PIECES = 2
OUT_PIECES = 4


def dot(a, b):
    return jnp.dot(a, b, preferred_element_type=F32)


def dot_nt(a, b):
    return lax.dot_general(a, b, (((1,), (1,)), ((), ())), preferred_element_type=F32)


def exact_dot(a, b):
    return jnp.dot(a, b, preferred_element_type=F32, precision=lax.Precision.HIGHEST)


def halves(x):
    high = x.astype(BF16)
    return high, (x - high.astype(F32)).astype(BF16)


def thirds(x):
    high = x.astype(BF16)
    rest = x - high.astype(F32)
    mid = rest.astype(BF16)
    return high, mid, (rest - mid.astype(F32)).astype(BF16)


def left_form(x):
    high, low = halves(x)
    return jnp.concatenate([high, high, low], axis=1)


def right_form(x):
    high, low = halves(x)
    return jnp.concatenate([high, low, high], axis=0)


def owners(counts, half, devices):
    patches = counts.shape[1]
    heavy = (counts > half).astype(F32)
    key = counts.astype(F32) * patches + lax.broadcasted_iota(jnp.int32, (1, patches), 1).astype(F32)
    sign = jnp.where(heavy > 0.0, -1.0, 1.0)
    order = sign * key
    column = jnp.broadcast_to(order, (8, patches)).T[:, :1]
    before = jnp.where((column < order) & ((column < 0.0) == (order < 0.0)), 1.0, 0.0)
    rank = jnp.sum(before, axis=0, keepdims=True)
    device = lax.broadcasted_iota(jnp.int32, (devices, patches), 0).astype(F32)
    heavies = jnp.where((device == rank) & (heavy > 0.0), 1.0, 0.0)
    lights = jnp.where((device == rank) & (heavy == 0.0), 1.0, 0.0)
    return heavies, lights


def store_rows(ref, first, stride, x):
    for j in range(x.shape[1] // LANES):
        ref[pl.ds(first + j, x.shape[0], stride=stride), :] = x[:, j * LANES : (j + 1) * LANES]


def tiles_sent(slots):
    return slots // LANES + slots // LANES // 4


def light_position(tile, slots):
    blocks = slots // LANES
    return blocks + tile if tile < blocks // 4 else blocks + blocks // 4 - 1 - tile


def pick(onehot, x):
    chosen = onehot.astype(BF16)
    return dot(jnp.concatenate([chosen] * 3, axis=1), jnp.concatenate(thirds(x), axis=0))


def pack_obs_kernel(counts_hbm, obs_hbm, out_hbm, flag_ref, counts_ref, obs_ref, out_ref, table_ref, table, sems, *, slots):
    patches = counts_ref.shape[1]
    blocks = slots // LANES
    each = patches * blocks
    local = obs_hbm.shape[0] // each
    sent_tiles = tiles_sent(slots)
    per = local * sent_tiles
    devices = out_hbm.shape[0] // per
    count_copy = pltpu.make_async_copy(counts_hbm, counts_ref, sems.at[0])
    count_copy.start()
    copies = []
    cut = each // IN_PIECES
    for i in range(local * IN_PIECES):
        span = pl.ds(i * cut, cut)
        copies.append(pltpu.make_async_copy(obs_hbm.at[span], obs_ref.at[span], sems.at[1 + i]))
        copies[-1].start()
    count_copy.wait()
    onehots = owners(counts_ref[...], slots // 2, devices)
    position = lax.broadcasted_iota(jnp.int32, (8, patches), 1).astype(F32).astype(BF16)
    index = [dot_nt(position, onehot.astype(BF16)).astype(jnp.int32) for onehot in onehots]
    lengths = ((counts_ref[...] + (LANES - 1)) >> 7).astype(F32)
    lengths = jnp.broadcast_to(lengths, (8, patches)).astype(BF16)
    long, short = (dot_nt(lengths, onehot.astype(BF16)).astype(jnp.int32) for onehot in onehots)
    excess = jnp.max((long + short).astype(F32), axis=1, keepdims=True) - sent_tiles
    flag_ref[...] = jnp.broadcast_to(excess, flag_ref.shape)
    start = [(p >> 3) * (8 * blocks) + (p & 7) for p in index]
    row = lax.broadcasted_iota(jnp.int32, (8, devices), 0)
    entries = jnp.where(row == 0, start[0], start[1])
    shared = [t for t in range(blocks // 2) if light_position(t, slots) < blocks]
    for i, t in enumerate(shared):
        at = light_position(t, slots)
        entries = jnp.where(row == 2 + i, jnp.where(long > at, start[0] + 8 * at, start[1] + 8 * t), entries)
    table_ref[...] = entries
    table_copy = pltpu.make_async_copy(table_ref, table, sems.at[0])
    table_copy.start()
    table_copy.wait()
    sent = []
    for copy in copies:
        copy.wait()
    group = devices // OUT_PIECES
    own = blocks - len(shared)
    rest = blocks // 2 - len(shared)
    for g in range(OUT_PIECES):
        for d in range(g * group, (g + 1) * group):
            for m in range(local):
                first = d * per + m * sent_tiles
                heavy, light = m * each + table[0, d], m * each + table[1, d]
                out_ref[first : first + own, :] = obs_ref[pl.ds(heavy, own, stride=8), :]
                for i, t in enumerate(shared):
                    at = first + light_position(t, slots)
                    out_ref[at : at + 1, :] = obs_ref[pl.ds(m * each + table[2 + i, d], 1), :]
                out_ref[first + blocks : first + blocks + rest, :] = obs_ref[pl.ds(light, rest, stride=8), :]
        some = pl.ds(g * group * per, group * per)
        sent.append(
            pltpu.make_async_copy(out_ref.at[some], out_hbm.at[some], sems.at[1 + local * IN_PIECES + g])
        )
        sent[-1].start()
    for copy in sent:
        copy.wait()


def pack_states_kernel(
    mine_ref, counts_ref, states_ref, value_ref, precision_ref, obs_hbm, out_hbm, extra_hbm, rows_ref, out_ref, extra_ref, obs_ref, sems
):
    local, patches, cells = states_ref.shape
    slots = value_ref.shape[1]
    blocks = cells // LANES
    per = 2 * local * blocks + 1
    devices = out_ref.shape[0] // per
    quarter = slots // 4
    obs_copies = []
    for m in range(local):
        obs_copies.append(
            pltpu.make_async_copy(obs_hbm.at[m, :, pl.ds(quarter, quarter)], obs_ref.at[m], sems.at[2 + m])
        )
        obs_copies[-1].start()
    counts = counts_ref[...]
    heavies, lights = owners(counts, slots // 2, devices)
    both = jnp.concatenate([heavies, lights], axis=0)
    for m in range(local):
        chosen = pick(both, states_ref[m])
        for k in range(2):
            store_rows(out_ref, (k * local + m) * blocks, per, chosen[k * devices : (k + 1) * devices])
    out_ref[pl.ds(per - 1, devices, stride=per), :] = jnp.zeros((devices, LANES), F32)
    copy = pltpu.make_async_copy(out_ref, out_hbm, sems.at[0])
    copy.start()
    for m in range(local):
        obs_copies[m].wait()
        store_rows(extra_ref, m * quarter // LANES, local * quarter // LANES, pick(lights, obs_ref[m]))
    extra_copy = pltpu.make_async_copy(extra_ref, extra_hbm, sems.at[1])
    extra_copy.start()
    here = lax.broadcasted_iota(jnp.int32, (devices, patches), 0) == mine_ref[0]
    own = [jnp.sum(jnp.where(here, onehot, 0.0), axis=0, keepdims=True) for onehot in (heavies, lights)]
    both = jnp.concatenate(own + [jnp.zeros((6, patches), F32)], axis=0)
    values = pick(both, value_ref[...])
    precisions = pick(both, precision_ref[...])
    slot = lax.broadcasted_iota(jnp.int32, (1, slots), 1).astype(F32)
    rows = []
    for k in range(2):
        count = jnp.sum(own[k] * counts.astype(F32), axis=1, keepdims=True)
        live = jnp.where(slot < count, 1.0, 0.0)
        rows += [values[k : k + 1], precisions[k : k + 1], live]
    length = jnp.sum(own[0] * counts.astype(F32), axis=1, keepdims=True)
    rows_ref[...] = jnp.concatenate(rows + [jnp.broadcast_to(length, (2, slots))], axis=0)
    copy.wait()
    extra_copy.wait()


def obs_columns(obs_ref, extra_ref, rows_ref, local):
    slots = rows_ref.shape[1]
    blocks = slots // LANES
    per = tiles_sent(slots) * local
    devices = obs_ref.shape[0] // per
    length = rows_ref[6:7, :LANES]
    for k in range(2):
        for c in range(blocks if k == 0 else blocks // 2):
            columns = slice(c * LANES, (c + 1) * LANES)
            at = c if k == 0 else light_position(c, slots)
            parts = [obs_ref[pl.ds(m * tiles_sent(slots) + at, devices, stride=per), :] for m in range(local)]
            if k == 1 and at < blocks:
                more = [
                    extra_ref[
                        pl.ds(m * (blocks // 4) + c - blocks // 4, devices, stride=local * (blocks // 4)), :
                    ]
                    for m in range(local)
                ]
                parts = [jnp.where(length > at * LANES, x, p) for x, p in zip(more, parts)]
            mean = sum(jnp.sum(p, axis=0, keepdims=True) for p in parts) * (1.0 / (local * devices))
            value, precision, live = (rows_ref[3 * k + i : 3 * k + i + 1, columns] for i in range(3))
            yield k, columns, [p - mean for p in parts], value - mean, precision, live


def sums_kernel(obs_ref, extra_ref, rows_ref, states_hbm, out_hbm, row_ref, sem, *, local):
    devices, per = out_hbm.shape[:2]
    members = local * devices
    misfit = jnp.zeros((1, LANES), F32)
    expected = jnp.zeros((1, LANES), F32)
    for _, _, parts, innov, precision, live in obs_columns(obs_ref, extra_ref, rows_ref, local):
        spread = sum(jnp.sum(p * p, axis=0, keepdims=True) for p in parts) * (1.0 / (members - 1.0))
        misfit += precision * live * innov * innov
        expected += live * (1.0 + precision * spread)
    lane = lax.broadcasted_iota(jnp.int32, (1, LANES), 1)
    row = jnp.where(
        lane == 0,
        jnp.sum(misfit, axis=1, keepdims=True),
        jnp.where(lane == 1, jnp.sum(expected, axis=1, keepdims=True), 0.0),
    )
    row_ref[...] = jnp.broadcast_to(row[None], row_ref.shape)
    copy = pltpu.make_async_copy(row_ref, out_hbm.at[:, per - 1], sem)
    copy.start()
    copy.wait()


def power_place(powers_ref, more_ref, members, k, i, h):
    place = (i * 2 + k) * (members // LANES) + h
    held = powers_ref.shape[0] // members
    return (powers_ref, place * members) if place < held else (more_ref, (place - held) * members)


def gram_kernel(
    obs_ref, extra_ref, rows_ref, counts_ref, powers_ref, more_ref, side_ref, spread_hbm, high_ref, low_ref, spread_ref, sem, *, local
):
    slots = rows_ref.shape[1]
    members = side_ref.shape[2]
    devices = members // local
    spread_ref[...] = jnp.concatenate(owners(counts_ref[...], slots // 2, devices), axis=0).T.astype(BF16)
    copy = pltpu.make_async_copy(spread_ref, spread_hbm, sem)
    copy.start()
    for k, columns, parts, innov, precision, live in obs_columns(obs_ref, extra_ref, rows_ref, local):
        scale = jnp.sqrt(precision * live)
        for m in range(local):
            high, low = halves(parts[m] * scale)
            high_ref[k, m * devices : (m + 1) * devices, columns] = high
            low_ref[k, m * devices : (m + 1) * devices, columns] = low
        high, low = halves(jnp.broadcast_to(scale * innov, (16, LANES)))
        high_ref[k, members:, columns] = high
        low_ref[k, members:, columns] = low
    diagonal = lax.broadcasted_iota(jnp.int32, (members, members), 0) == lax.broadcasted_iota(
        jnp.int32, (members, members), 1
    )
    for k in range(2):
        width = slots if k == 0 else slots // 2
        high, low = high_ref[k, :, :width], low_ref[k, :, :width]
        gram = dot_nt(high, high[:members]) + dot_nt(high, low[:members]) + dot_nt(low, high[:members])
        forcing = gram[members : members + 8]
        gram = gram[:members]
        size = jnp.sqrt(jnp.sum(jnp.sum(gram * gram, axis=0, keepdims=True), axis=1, keepdims=True))
        unit = gram / jnp.maximum(size, 1e-30)
        trace = jnp.sum(
            jnp.sum(jnp.where(diagonal, unit, 0.0), axis=0, keepdims=True), axis=1, keepdims=True
        )
        second = exact_dot(unit, unit)
        for i, power in enumerate((unit, second, exact_dot(unit, second), exact_dot(second, second))):
            for h in range(members // LANES):
                ref, first = power_place(powers_ref, more_ref, members, k, i, h)
                ref[first : first + members] = power[:, h * LANES : (h + 1) * LANES]
        side_ref[k] = jnp.concatenate(
            [forcing, jnp.broadcast_to(size, (8, members)), jnp.broadcast_to(trace, (8, members))], axis=0
        )
    copy.wait()


def update_kernel(
    states_ref, powers_ref, more_ref, side_ref, out_ref, s_ref, z_ref, states_right, center_ref, *, local
):
    members = side_ref.shape[2]
    devices = members // local
    per = states_ref.shape[0] // devices
    blocks = out_ref.shape[0] // devices // (2 * local)
    total = jnp.sum(states_ref[pl.ds(per - 1, devices, stride=per), :], axis=0, keepdims=True)
    lane = lax.broadcasted_iota(jnp.int32, total.shape, 1)
    misfit = jnp.sum(jnp.where(lane == 0, total, 0.0), axis=1, keepdims=True)
    expected = jnp.sum(jnp.where(lane == 1, total, 0.0), axis=1, keepdims=True)
    squared = misfit / expected
    inflation = jnp.sqrt(squared)
    diagonal = lax.broadcasted_iota(jnp.int32, (members, members), 0) == lax.broadcasted_iota(
        jnp.int32, (members, members), 1
    )
    free = members - 1.0

    def plus_diagonal(x, value):
        return x + jnp.where(diagonal, value, 0.0)

    def put(ref, k, x):
        ref[k, 0], ref[k, 1] = halves(x)

    def left(ref, k):
        return jnp.concatenate([ref[k, 0], ref[k, 0], ref[k, 1]], axis=1)

    def right(ref, k):
        return jnp.concatenate([ref[k, 0], ref[k, 1], ref[k, 0]], axis=0)

    def whole(ref, k):
        return ref[k, 0].astype(F32) + ref[k, 1].astype(F32)

    def square(k):
        return dot(left(s_ref, k), right(s_ref, k))

    def refine(k, product):
        s = whole(s_ref, k)
        return 2.25 * s + dot(left_form(0.25 * product - 1.5 * s), right(s_ref, k))

    def advance(k):
        return 1.5 * whole(z_ref, k) - 0.5 * dot(left(s_ref, k), right(z_ref, k))

    scalers = []
    for k in range(2):
        size, trace = side_ref[k, 8:9, :1], side_ref[k, 16:17, :1]
        strength = squared * size
        scaler = jnp.sqrt(free * free * members + strength * (2.0 * free * trace + strength))
        scalers.append(scaler)
        a, b = free / scaler, strength / scaler
        f = 1.5 - 0.5 * a
        s1 = (a * f * f, b * f * (f - a), b * b * (0.25 * a - f), 0.25 * b * b * b)
        d = (1.5 - 0.5 * s1[0], -0.5 * s1[1], -0.5 * s1[2], -0.5 * s1[3])
        h = -0.5 * b
        z2 = (f * d[0], f * d[1] + h * d[0], f * d[2] + h * d[1], f * d[3] + h * d[2], h * d[3])
        powers = []
        for i in range(4):
            places = [power_place(powers_ref, more_ref, members, k, i, h) for h in range(members // LANES)]
            powers.append(jnp.concatenate([ref[first : first + members] for ref, first in places], axis=1))
        put(s_ref, k, plus_diagonal(sum(c * p for c, p in zip(s1[1:], powers)), s1[0]))
        put(z_ref, k, plus_diagonal(sum(c * p for c, p in zip(z2[1:], powers)), z2[0]))
    for k in range(2):
        put(s_ref, k, refine(k, square(k)))
        for c in range(blocks):
            rows = [(k * local + m) * blocks + c for m in range(local)]
            parts = [states_ref[pl.ds(r, devices, stride=per), :] for r in rows]
            center = sum(jnp.sum(p, axis=0, keepdims=True) for p in parts) * (1.0 / members)
            columns = slice(c * LANES, (c + 1) * LANES)
            center_ref[k, :, columns] = jnp.broadcast_to(center, (8, LANES))
            for m in range(local):
                high, low = halves(parts[m] - center)
                for i, piece in enumerate((high, low, high)):
                    first = i * members + m * devices
                    states_right[k, first : first + devices, columns] = piece

    for _ in range(SWEEPS - 3):
        products = [square(k) for k in range(2)]
        roots = [advance(k) for k in range(2)]
        for k in range(2):
            s = refine(k, products[k])
            put(s_ref, k, s)
            put(z_ref, k, roots[k])

    for k in range(2):
        root = advance(k)
        forcing = squared / scalers[k] * side_ref[k, :1]
        half_way = jnp.sum(root * forcing, axis=1, keepdims=True)
        shifts = jnp.sum(root * half_way, axis=0, keepdims=True)
        transform = (inflation * free**0.5 / jnp.sqrt(scalers[k])) * root + shifts
        update = dot(left_form(transform), states_right[k]) + center_ref[k, :1]
        for c in range(blocks):
            for m in range(local):
                piece = update[m * devices : (m + 1) * devices, c * LANES : (c + 1) * LANES]
                out_ref[pl.ds((k * local + m) * blocks + c, devices, stride=2 * local * blocks), :] = piece


def unpack_kernel(spread_ref, rows_ref, out_hbm, out_ref, sems):
    local, patches, cells = out_ref.shape
    blocks = cells // LANES
    per = 2 * local * blocks
    devices = rows_ref.shape[0] // per
    spread = jnp.concatenate([spread_ref[...]] * 2, axis=1)
    wide = blocks // 2
    copies = []
    for m in range(local):
        for part in range(2):
            x = jnp.concatenate(
                [
                    jnp.concatenate(
                        [
                            rows_ref[pl.ds((k * local + m) * blocks + part * wide + j, devices, stride=per), :]
                            for j in range(wide)
                        ],
                        axis=1,
                    )
                    for k in range(2)
                ],
                axis=0,
            )
            columns = pl.ds(part * wide * LANES, wide * LANES)
            out_ref[m, :, columns] = dot(spread, jnp.concatenate(halves(x), axis=0))
            copies.append(
                pltpu.make_async_copy(
                    out_ref.at[m, :, columns], out_hbm.at[m, :, columns], sems.at[2 * m + part]
                )
            )
            copies[-1].start()
    for copy in copies:
        copy.wait()


HBM = pl.BlockSpec(memory_space=pltpu.HBM)
WHOLE = pl.BlockSpec(memory_space=pltpu.VMEM)
SCALAR = pl.BlockSpec(memory_space=pltpu.SMEM)


def call(kernel, out_shapes, inputs, ins=None, outs=None, types=None, scratch=(), aliases={}):
    ins = ins or [WHOLE] * len(inputs)
    outs = outs or [WHOLE] * len(out_shapes)
    inputs = [pltpu.with_memory_space_constraint(x, pltpu.HBM) if s is HBM else x for x, s in zip(inputs, ins)]
    return pl.pallas_call(
        kernel,
        out_shape=[
            pltpu.HBM(shape, kind) if s is HBM else jax.ShapeDtypeStruct(shape, kind)
            for shape, kind, s in zip(out_shapes, types or [F32] * len(outs), outs)
        ],
        in_specs=ins,
        out_specs=outs,
        scratch_shapes=list(scratch),
        input_output_aliases=aliases,
        compiler_params=pltpu.CompilerParams(vmem_limit_bytes=VMEM_LIMIT),
    )(*inputs)


def exchange(x, name):
    with jax.named_scope(name):
        rows = x.reshape(-1, 1, LANES)
        return lax.all_to_all(rows, AXES, split_axis=0, concat_axis=0, tiled=True).reshape(-1, LANES)


def per_device(background, obs_ensemble, obs_value, obs_precision, obs_count):
    devices = lax.axis_size(AXES)
    local, patches, cells = background.shape
    slots = obs_ensemble.shape[2]
    members = local * devices
    counts = obs_count.reshape(1, patches)
    mine = lax.axis_index(AXES).astype(jnp.int32).reshape(1)
    obs_rows = tiles_sent(slots) * local
    extra_rows = local * slots // 4 // LANES
    state_rows = 2 * local * cells // LANES
    blocks = slots // LANES
    in_memory = obs_ensemble.reshape(local, patches // 8, 8, blocks, LANES).swapaxes(2, 3).reshape(-1, LANES)
    obs_sent, excess = call(
        functools.partial(pack_obs_kernel, slots=slots),
        [(devices * obs_rows, LANES), (8, LANES)],
        (counts, in_memory),
        ins=[HBM, HBM],
        outs=[HBM, WHOLE],
        scratch=[
            pltpu.VMEM((1, patches), jnp.int32),
            pltpu.VMEM(in_memory.shape, F32),
            pltpu.VMEM((devices * obs_rows, LANES), F32),
            pltpu.VMEM((8, devices), jnp.int32),
            pltpu.SMEM((8, devices), jnp.int32),
            pltpu.SemaphoreType.DMA((1 + local * IN_PIECES + OUT_PIECES,)),
        ],
    )
    obs = exchange(obs_sent, "obs_exchange")
    states_sent, extra_sent, rows = call(
        pack_states_kernel,
        [(devices * (state_rows + 1), LANES), (devices * extra_rows, LANES), (8, slots)],
        (mine, counts, background, obs_value, obs_precision, obs_ensemble),
        ins=[SCALAR] + [WHOLE] * 4 + [HBM],
        outs=[HBM, HBM, WHOLE],
        scratch=[
            pltpu.VMEM((devices * (state_rows + 1), LANES), F32),
            pltpu.VMEM((devices * extra_rows, LANES), F32),
            pltpu.VMEM((local, patches, slots // 4), F32),
            pltpu.SemaphoreType.DMA((2 + local,)),
        ],
    )
    obs, extra_sent = lax.optimization_barrier((obs, extra_sent))
    extra = lax.cond(excess[0, 0] > 0.0, lambda x: exchange(x, "extra_exchange"), jnp.zeros_like, extra_sent)
    states_sent = states_sent.reshape(devices, state_rows + 1, 1, LANES)
    (states_sent,) = call(
        functools.partial(sums_kernel, local=local),
        [states_sent.shape],
        (obs, extra, rows, states_sent),
        ins=[WHOLE, WHOLE, WHOLE, HBM],
        outs=[HBM],
        scratch=[pltpu.VMEM((devices, 1, LANES), F32), pltpu.SemaphoreType.DMA],
        aliases={3: 0},
    )
    states = exchange(states_sent, "states_exchange")
    powers, more, side, spread = call(
        functools.partial(gram_kernel, local=local),
        [obs.shape, (8 * members * members // LANES - obs.shape[0], LANES), (2, 24, members), (patches, members)],
        (obs, extra, rows, counts),
        outs=[WHOLE, WHOLE, WHOLE, HBM],
        types=[F32, F32, F32, BF16],
        scratch=[
            pltpu.VMEM((2, members + 16, slots), BF16),
            pltpu.VMEM((2, members + 16, slots), BF16),
            pltpu.VMEM((patches, members), BF16),
            pltpu.SemaphoreType.DMA,
        ],
        aliases={0: 0},
    )
    (update,) = call(
        functools.partial(update_kernel, local=local),
        [(devices * state_rows, LANES)],
        (states, powers, more, side),
        scratch=[
            pltpu.VMEM((2, 2, members, members), BF16),
            pltpu.VMEM((2, 2, members, members), BF16),
            pltpu.VMEM((2, 3 * members, cells), BF16),
            pltpu.VMEM((2, 8, cells), F32),
        ],
    )
    returned = exchange(update, "return_exchange")
    (analysis,) = call(
        unpack_kernel,
        [(local, patches, cells)],
        (spread, returned),
        outs=[HBM],
        scratch=[pltpu.VMEM((local, patches, cells), F32), pltpu.SemaphoreType.DMA((2 * local,))],
    )
    return analysis


def solution(mesh):
    placed = (P(AXES, None, None), P(AXES, None, None), P(), P(), P())
    return jax.shard_map(
        per_device, mesh=mesh, in_specs=placed, out_specs=P(AXES, None, None), check_vma=False
    )
```

```python
import functools

import jax
import jax.numpy as jnp
from jax import lax
from jax.experimental import pallas as pl
from jax.experimental.pallas import tpu as pltpu
from jax.sharding import PartitionSpec as P

SWEEPS = 8
LANES = 128
AXES = ("grp", "mem")
F32 = jnp.float32
BF16 = jnp.bfloat16
VMEM_LIMIT = 12 << 20
IN_PIECES = 2
OUT_PIECES = 8


def dot(a, b):
    return jnp.dot(a, b, preferred_element_type=F32)


def dot_nt(a, b):
    return lax.dot_general(a, b, (((1,), (1,)), ((), ())), preferred_element_type=F32)


def exact_dot(a, b):
    return jnp.dot(a, b, preferred_element_type=F32, precision=lax.Precision.HIGHEST)


def halves(x):
    high = x.astype(BF16)
    return high, (x - high.astype(F32)).astype(BF16)


def thirds(x):
    high = x.astype(BF16)
    rest = x - high.astype(F32)
    mid = rest.astype(BF16)
    return high, mid, (rest - mid.astype(F32)).astype(BF16)


def left_form(x):
    high, low = halves(x)
    return jnp.concatenate([high, high, low], axis=1)


def right_form(x):
    high, low = halves(x)
    return jnp.concatenate([high, low, high], axis=0)


def owners(counts, half, devices):
    patches = counts.shape[1]
    heavy = (counts > half).astype(F32)
    key = counts.astype(F32) * patches + lax.broadcasted_iota(jnp.int32, (1, patches), 1).astype(F32)
    sign = jnp.where(heavy > 0.0, -1.0, 1.0)
    order = sign * key
    column = jnp.broadcast_to(order, (8, patches)).T[:, :1]
    before = jnp.where((column < order) & ((column < 0.0) == (order < 0.0)), 1.0, 0.0)
    rank = jnp.sum(before, axis=0, keepdims=True)
    device = lax.broadcasted_iota(jnp.int32, (devices, patches), 0).astype(F32)
    heavies = jnp.where((device == rank) & (heavy > 0.0), 1.0, 0.0)
    lights = jnp.where((device == rank) & (heavy == 0.0), 1.0, 0.0)
    return heavies, lights


def store_rows(ref, first, stride, x):
    for j in range(x.shape[1] // LANES):
        ref[pl.ds(first + j, x.shape[0], stride=stride), :] = x[:, j * LANES : (j + 1) * LANES]


def tiles_sent(slots):
    return slots // LANES + slots // LANES // 4


def light_position(tile, slots):
    blocks = slots // LANES
    return blocks + tile if tile < blocks // 4 else blocks + blocks // 4 - 1 - tile


def pick(onehot, x):
    chosen = onehot.astype(BF16)
    return dot(jnp.concatenate([chosen] * 3, axis=1), jnp.concatenate(thirds(x), axis=0))


def pack_obs_kernel(counts_hbm, obs_hbm, out_hbm, flag_ref, counts_ref, obs_ref, out_ref, sems, *, slots):
    patches = counts_ref.shape[1]
    blocks = slots // LANES
    each = patches * blocks
    local = obs_hbm.shape[0] // each
    sent_tiles = tiles_sent(slots)
    per = local * sent_tiles
    devices = out_hbm.shape[0] // per
    count_copy = pltpu.make_async_copy(counts_hbm, counts_ref, sems.at[0])
    count_copy.start()
    copies = []
    cut = each // IN_PIECES
    for i in range(local * IN_PIECES):
        span = pl.ds(i * cut, cut)
        copies.append(pltpu.make_async_copy(obs_hbm.at[span], obs_ref.at[span], sems.at[1 + i]))
        copies[-1].start()
    count_copy.wait()
    onehots = owners(counts_ref[...], slots // 2, devices)
    lengths = ((counts_ref[...] + (LANES - 1)) >> 7).astype(F32)
    position = lax.broadcasted_iota(jnp.int32, (8, patches), 1).astype(F32)
    first_row = lax.broadcasted_iota(jnp.int32, (8, patches), 0) == 0
    facts = dot_nt(
        jnp.where(first_row, position, lengths).astype(BF16), jnp.concatenate(onehots, axis=0).astype(BF16)
    ).astype(jnp.int32)
    index = [facts[:1, :devices], facts[:1, devices:]]
    long, short = facts[1:2, :devices], facts[1:2, devices:]
    excess = jnp.max((long + short).astype(F32), axis=1, keepdims=True) - sent_tiles
    flag_ref[...] = jnp.broadcast_to(excess, flag_ref.shape)
    start = [(p >> 3) * (8 * blocks) + (p & 7) for p in index]
    shared = [t for t in range(blocks // 2) if light_position(t, slots) < blocks]
    packed = start[0] + (start[1] << 12)
    for i, t in enumerate(shared):
        packed += jnp.where(long > light_position(t, slots), 1 << (24 + i), 0)
    sent = []
    for copy in copies:
        copy.wait()
    group = devices // OUT_PIECES
    own = blocks - len(shared)
    rest = blocks // 2 - len(shared)
    for g in range(OUT_PIECES):
        for d in range(g * group, (g + 1) * group):
            entry = packed[0, d]
            heavy_start, light_start = entry & 4095, (entry >> 12) & 4095
            middle = [
                jnp.where(
                    (entry >> (24 + i)) & 1 == 1,
                    heavy_start + 8 * light_position(t, slots),
                    light_start + 8 * t,
                )
                for i, t in enumerate(shared)
            ]
            for m in range(local):
                first = d * per + m * sent_tiles
                heavy, light = m * each + heavy_start, m * each + light_start
                out_ref[first : first + own, :] = obs_ref[pl.ds(heavy, own, stride=8), :]
                for i, t in enumerate(shared):
                    at = first + light_position(t, slots)
                    out_ref[at : at + 1, :] = obs_ref[pl.ds(m * each + middle[i], 1), :]
                out_ref[first + blocks : first + blocks + rest, :] = obs_ref[pl.ds(light, rest, stride=8), :]
        some = pl.ds(g * group * per, group * per)
        sent.append(
            pltpu.make_async_copy(out_ref.at[some], out_hbm.at[some], sems.at[1 + local * IN_PIECES + g])
        )
        sent[-1].start()
    for copy in sent:
        copy.wait()


def pack_states_kernel(
    mine_ref, counts_ref, states_ref, value_ref, precision_ref, obs_hbm, out_hbm, extra_hbm, rows_ref, out_ref, extra_ref, obs_ref, sems
):
    local, patches, cells = states_ref.shape
    slots = value_ref.shape[1]
    blocks = cells // LANES
    per = 2 * local * blocks + 1
    devices = out_ref.shape[0] // per
    quarter = slots // 4
    obs_copies = []
    for m in range(local):
        obs_copies.append(
            pltpu.make_async_copy(obs_hbm.at[m, :, pl.ds(quarter, quarter)], obs_ref.at[m], sems.at[2 + m])
        )
        obs_copies[-1].start()
    counts = counts_ref[...]
    heavies, lights = owners(counts, slots // 2, devices)
    both = jnp.concatenate([heavies, lights], axis=0)
    for m in range(local):
        chosen = pick(both, states_ref[m])
        for k in range(2):
            store_rows(out_ref, (k * local + m) * blocks, per, chosen[k * devices : (k + 1) * devices])
    out_ref[pl.ds(per - 1, devices, stride=per), :] = jnp.zeros((devices, LANES), F32)
    copy = pltpu.make_async_copy(out_ref, out_hbm, sems.at[0])
    copy.start()
    for m in range(local):
        obs_copies[m].wait()
        store_rows(extra_ref, m * quarter // LANES, local * quarter // LANES, pick(lights, obs_ref[m]))
    extra_copy = pltpu.make_async_copy(extra_ref, extra_hbm, sems.at[1])
    extra_copy.start()
    here = lax.broadcasted_iota(jnp.int32, (devices, patches), 0) == mine_ref[0]
    own = [jnp.sum(jnp.where(here, onehot, 0.0), axis=0, keepdims=True) for onehot in (heavies, lights)]
    both = jnp.concatenate(own + [jnp.zeros((6, patches), F32)], axis=0)
    values = pick(both, value_ref[...])
    precisions = pick(both, precision_ref[...])
    slot = lax.broadcasted_iota(jnp.int32, (1, slots), 1).astype(F32)
    rows = []
    for k in range(2):
        count = jnp.sum(own[k] * counts.astype(F32), axis=1, keepdims=True)
        live = jnp.where(slot < count, 1.0, 0.0)
        rows += [values[k : k + 1], precisions[k : k + 1], live]
    length = jnp.sum(own[0] * counts.astype(F32), axis=1, keepdims=True)
    rows_ref[...] = jnp.concatenate(rows + [jnp.broadcast_to(length, (2, slots))], axis=0)
    copy.wait()
    extra_copy.wait()


def obs_columns(obs_ref, extra_ref, rows_ref, local):
    slots = rows_ref.shape[1]
    blocks = slots // LANES
    per = tiles_sent(slots) * local
    devices = obs_ref.shape[0] // per
    length = rows_ref[6:7, :LANES]
    for k in range(2):
        for c in range(blocks if k == 0 else blocks // 2):
            columns = slice(c * LANES, (c + 1) * LANES)
            at = c if k == 0 else light_position(c, slots)
            parts = [obs_ref[pl.ds(m * tiles_sent(slots) + at, devices, stride=per), :] for m in range(local)]
            if k == 1 and at < blocks:
                more = [
                    extra_ref[
                        pl.ds(m * (blocks // 4) + c - blocks // 4, devices, stride=local * (blocks // 4)), :
                    ]
                    for m in range(local)
                ]
                parts = [jnp.where(length > at * LANES, x, p) for x, p in zip(more, parts)]
            mean = sum(jnp.sum(p, axis=0, keepdims=True) for p in parts) * (1.0 / (local * devices))
            value, precision, live = (rows_ref[3 * k + i : 3 * k + i + 1, columns] for i in range(3))
            yield k, columns, [p - mean for p in parts], value - mean, precision, live


def sums_kernel(obs_ref, extra_ref, rows_ref, states_hbm, out_hbm, row_ref, sem, *, local):
    devices, per = out_hbm.shape[:2]
    members = local * devices
    misfit = jnp.zeros((1, LANES), F32)
    expected = jnp.zeros((1, LANES), F32)
    for _, _, parts, innov, precision, live in obs_columns(obs_ref, extra_ref, rows_ref, local):
        spread = sum(jnp.sum(p * p, axis=0, keepdims=True) for p in parts) * (1.0 / (members - 1.0))
        misfit += precision * live * innov * innov
        expected += live * (1.0 + precision * spread)
    lane = lax.broadcasted_iota(jnp.int32, (1, LANES), 1)
    row = jnp.where(
        lane == 0,
        jnp.sum(misfit, axis=1, keepdims=True),
        jnp.where(lane == 1, jnp.sum(expected, axis=1, keepdims=True), 0.0),
    )
    row_ref[...] = jnp.broadcast_to(row[None], row_ref.shape)
    copy = pltpu.make_async_copy(row_ref, out_hbm.at[:, per - 1], sem)
    copy.start()
    copy.wait()


def power_place(powers_ref, more_ref, members, k, i, h):
    place = (i * 2 + k) * (members // LANES) + h
    held = powers_ref.shape[0] // members
    return (powers_ref, place * members) if place < held else (more_ref, (place - held) * members)


def gram_kernel(
    obs_ref, extra_ref, rows_ref, counts_ref, powers_ref, more_ref, side_ref, spread_hbm, high_ref, low_ref, spread_ref, sem, *, local
):
    slots = rows_ref.shape[1]
    members = side_ref.shape[2]
    devices = members // local
    spread_ref[...] = jnp.concatenate(owners(counts_ref[...], slots // 2, devices), axis=0).T.astype(BF16)
    copy = pltpu.make_async_copy(spread_ref, spread_hbm, sem)
    copy.start()
    for k, columns, parts, innov, precision, live in obs_columns(obs_ref, extra_ref, rows_ref, local):
        scale = jnp.sqrt(precision * live)
        for m in range(local):
            high, low = halves(parts[m] * scale)
            high_ref[k, m * devices : (m + 1) * devices, columns] = high
            low_ref[k, m * devices : (m + 1) * devices, columns] = low
        high, low = halves(jnp.broadcast_to(scale * innov, (16, LANES)))
        high_ref[k, members:, columns] = high
        low_ref[k, members:, columns] = low
    diagonal = lax.broadcasted_iota(jnp.int32, (members, members), 0) == lax.broadcasted_iota(
        jnp.int32, (members, members), 1
    )
    for k in range(2):
        width = slots if k == 0 else slots // 2
        high, low = high_ref[k, :, :width], low_ref[k, :, :width]
        gram = dot_nt(high, high[:members]) + dot_nt(high, low[:members]) + dot_nt(low, high[:members])
        forcing = gram[members : members + 8]
        gram = gram[:members]
        size = jnp.sqrt(jnp.sum(jnp.sum(gram * gram, axis=0, keepdims=True), axis=1, keepdims=True))
        unit = gram / jnp.maximum(size, 1e-30)
        trace = jnp.sum(
            jnp.sum(jnp.where(diagonal, unit, 0.0), axis=0, keepdims=True), axis=1, keepdims=True
        )
        second = exact_dot(unit, unit)
        for i, power in enumerate((unit, second, exact_dot(unit, second), exact_dot(second, second))):
            for h in range(members // LANES):
                ref, first = power_place(powers_ref, more_ref, members, k, i, h)
                ref[first : first + members] = power[:, h * LANES : (h + 1) * LANES]
        side_ref[k] = jnp.concatenate(
            [forcing, jnp.broadcast_to(size, (8, members)), jnp.broadcast_to(trace, (8, members))], axis=0
        )
    copy.wait()


def update_kernel(
    states_ref, powers_ref, more_ref, side_ref, out_ref, s_ref, z_ref, states_right, center_ref, *, local
):
    members = side_ref.shape[2]
    devices = members // local
    per = states_ref.shape[0] // devices
    blocks = out_ref.shape[0] // devices // (2 * local)
    total = jnp.sum(states_ref[pl.ds(per - 1, devices, stride=per), :], axis=0, keepdims=True)
    lane = lax.broadcasted_iota(jnp.int32, total.shape, 1)
    misfit = jnp.sum(jnp.where(lane == 0, total, 0.0), axis=1, keepdims=True)
    expected = jnp.sum(jnp.where(lane == 1, total, 0.0), axis=1, keepdims=True)
    squared = misfit / expected
    inflation = jnp.sqrt(squared)
    diagonal = lax.broadcasted_iota(jnp.int32, (members, members), 0) == lax.broadcasted_iota(
        jnp.int32, (members, members), 1
    )
    free = members - 1.0

    def plus_diagonal(x, value):
        return x + jnp.where(diagonal, value, 0.0)

    def put(ref, k, x):
        ref[k, 0], ref[k, 1] = halves(x)

    def left(ref, k):
        return jnp.concatenate([ref[k, 0], ref[k, 0], ref[k, 1]], axis=1)

    def right(ref, k):
        return jnp.concatenate([ref[k, 0], ref[k, 1], ref[k, 0]], axis=0)

    def whole(ref, k):
        return ref[k, 0].astype(F32) + ref[k, 1].astype(F32)

    def square(k):
        return dot(left(s_ref, k), right(s_ref, k))

    def refine(k, product):
        s = whole(s_ref, k)
        return 2.25 * s + dot(left_form(0.25 * product - 1.5 * s), right(s_ref, k))

    def advance(k):
        return 1.5 * whole(z_ref, k) - 0.5 * dot(left(s_ref, k), right(z_ref, k))

    scalers = []
    for k in range(2):
        size, trace = side_ref[k, 8:9, :1], side_ref[k, 16:17, :1]
        strength = squared * size
        scaler = jnp.sqrt(free * free * members + strength * (2.0 * free * trace + strength))
        scalers.append(scaler)
        a, b = free / scaler, strength / scaler
        f = 1.5 - 0.5 * a
        s1 = (a * f * f, b * f * (f - a), b * b * (0.25 * a - f), 0.25 * b * b * b)
        d = (1.5 - 0.5 * s1[0], -0.5 * s1[1], -0.5 * s1[2], -0.5 * s1[3])
        h = -0.5 * b
        z2 = (f * d[0], f * d[1] + h * d[0], f * d[2] + h * d[1], f * d[3] + h * d[2], h * d[3])
        powers = []
        for i in range(4):
            places = [power_place(powers_ref, more_ref, members, k, i, h) for h in range(members // LANES)]
            powers.append(jnp.concatenate([ref[first : first + members] for ref, first in places], axis=1))
        put(s_ref, k, plus_diagonal(sum(c * p for c, p in zip(s1[1:], powers)), s1[0]))
        put(z_ref, k, plus_diagonal(sum(c * p for c, p in zip(z2[1:], powers)), z2[0]))
    for k in range(2):
        put(s_ref, k, refine(k, square(k)))
        for c in range(blocks):
            rows = [(k * local + m) * blocks + c for m in range(local)]
            parts = [states_ref[pl.ds(r, devices, stride=per), :] for r in rows]
            center = sum(jnp.sum(p, axis=0, keepdims=True) for p in parts) * (1.0 / members)
            columns = slice(c * LANES, (c + 1) * LANES)
            center_ref[k, :, columns] = jnp.broadcast_to(center, (8, LANES))
            for m in range(local):
                high, low = halves(parts[m] - center)
                for i, piece in enumerate((high, low, high)):
                    first = i * members + m * devices
                    states_right[k, first : first + devices, columns] = piece

    for _ in range(SWEEPS - 3):
        products = [square(k) for k in range(2)]
        roots = [advance(k) for k in range(2)]
        for k in range(2):
            s = refine(k, products[k])
            put(s_ref, k, s)
            put(z_ref, k, roots[k])

    for k in range(2):
        root = advance(k)
        forcing = squared / scalers[k] * side_ref[k, :1]
        half_way = jnp.sum(root * forcing, axis=1, keepdims=True)
        shifts = jnp.sum(root * half_way, axis=0, keepdims=True)
        transform = (inflation * free**0.5 / jnp.sqrt(scalers[k])) * root + shifts
        update = dot(left_form(transform), states_right[k]) + center_ref[k, :1]
        for c in range(blocks):
            for m in range(local):
                piece = update[m * devices : (m + 1) * devices, c * LANES : (c + 1) * LANES]
                out_ref[pl.ds((k * local + m) * blocks + c, devices, stride=2 * local * blocks), :] = piece


def unpack_kernel(spread_ref, rows_ref, out_hbm, out_ref, sems):
    local, patches, cells = out_ref.shape
    blocks = cells // LANES
    per = 2 * local * blocks
    devices = rows_ref.shape[0] // per
    spread = jnp.concatenate([spread_ref[...]] * 2, axis=1)
    wide = blocks // 2
    copies = []
    for m in range(local):
        for part in range(2):
            x = jnp.concatenate(
                [
                    jnp.concatenate(
                        [
                            rows_ref[pl.ds((k * local + m) * blocks + part * wide + j, devices, stride=per), :]
                            for j in range(wide)
                        ],
                        axis=1,
                    )
                    for k in range(2)
                ],
                axis=0,
            )
            columns = pl.ds(part * wide * LANES, wide * LANES)
            out_ref[m, :, columns] = dot(spread, jnp.concatenate(halves(x), axis=0))
            copies.append(
                pltpu.make_async_copy(
                    out_ref.at[m, :, columns], out_hbm.at[m, :, columns], sems.at[2 * m + part]
                )
            )
            copies[-1].start()
    for copy in copies:
        copy.wait()


HBM = pl.BlockSpec(memory_space=pltpu.HBM)
WHOLE = pl.BlockSpec(memory_space=pltpu.VMEM)
SCALAR = pl.BlockSpec(memory_space=pltpu.SMEM)


def call(kernel, out_shapes, inputs, ins=None, outs=None, types=None, scratch=(), aliases={}):
    ins = ins or [WHOLE] * len(inputs)
    outs = outs or [WHOLE] * len(out_shapes)
    inputs = [pltpu.with_memory_space_constraint(x, pltpu.HBM) if s is HBM else x for x, s in zip(inputs, ins)]
    return pl.pallas_call(
        kernel,
        out_shape=[
            pltpu.HBM(shape, kind) if s is HBM else jax.ShapeDtypeStruct(shape, kind)
            for shape, kind, s in zip(out_shapes, types or [F32] * len(outs), outs)
        ],
        in_specs=ins,
        out_specs=outs,
        scratch_shapes=list(scratch),
        input_output_aliases=aliases,
        compiler_params=pltpu.CompilerParams(vmem_limit_bytes=VMEM_LIMIT),
    )(*inputs)


def exchange(x, name):
    with jax.named_scope(name):
        rows = x.reshape(-1, 1, LANES)
        return lax.all_to_all(rows, AXES, split_axis=0, concat_axis=0, tiled=True).reshape(-1, LANES)


def per_device(background, obs_ensemble, obs_value, obs_precision, obs_count):
    devices = lax.axis_size(AXES)
    local, patches, cells = background.shape
    slots = obs_ensemble.shape[2]
    members = local * devices
    counts = obs_count.reshape(1, patches)
    mine = lax.axis_index(AXES).astype(jnp.int32).reshape(1)
    obs_rows = tiles_sent(slots) * local
    extra_rows = local * slots // 4 // LANES
    state_rows = 2 * local * cells // LANES
    blocks = slots // LANES
    in_memory = obs_ensemble.reshape(local, patches // 8, 8, blocks, LANES).swapaxes(2, 3).reshape(-1, LANES)
    obs_sent, excess = call(
        functools.partial(pack_obs_kernel, slots=slots),
        [(devices * obs_rows, LANES), (8, LANES)],
        (counts, in_memory),
        ins=[HBM, HBM],
        outs=[HBM, WHOLE],
        scratch=[
            pltpu.VMEM((1, patches), jnp.int32),
            pltpu.VMEM(in_memory.shape, F32),
            pltpu.VMEM((devices * obs_rows, LANES), F32),
            pltpu.SemaphoreType.DMA((1 + local * IN_PIECES + OUT_PIECES,)),
        ],
    )
    obs = exchange(obs_sent, "obs_exchange")
    states_sent, extra_sent, rows = call(
        pack_states_kernel,
        [(devices * (state_rows + 1), LANES), (devices * extra_rows, LANES), (8, slots)],
        (mine, counts, background, obs_value, obs_precision, obs_ensemble),
        ins=[SCALAR] + [WHOLE] * 4 + [HBM],
        outs=[HBM, HBM, WHOLE],
        scratch=[
            pltpu.VMEM((devices * (state_rows + 1), LANES), F32),
            pltpu.VMEM((devices * extra_rows, LANES), F32),
            pltpu.VMEM((local, patches, slots // 4), F32),
            pltpu.SemaphoreType.DMA((2 + local,)),
        ],
    )
    obs, extra_sent = lax.optimization_barrier((obs, extra_sent))
    extra = lax.cond(excess[0, 0] > 0.0, lambda x: exchange(x, "extra_exchange"), jnp.zeros_like, extra_sent)
    states_sent = states_sent.reshape(devices, state_rows + 1, 1, LANES)
    (states_sent,) = call(
        functools.partial(sums_kernel, local=local),
        [states_sent.shape],
        (obs, extra, rows, states_sent),
        ins=[WHOLE, WHOLE, WHOLE, HBM],
        outs=[HBM],
        scratch=[pltpu.VMEM((devices, 1, LANES), F32), pltpu.SemaphoreType.DMA],
        aliases={3: 0},
    )
    states = exchange(states_sent, "states_exchange")
    powers, more, side, spread = call(
        functools.partial(gram_kernel, local=local),
        [obs.shape, (8 * members * members // LANES - obs.shape[0], LANES), (2, 24, members), (patches, members)],
        (obs, extra, rows, counts),
        outs=[WHOLE, WHOLE, WHOLE, HBM],
        types=[F32, F32, F32, BF16],
        scratch=[
            pltpu.VMEM((2, members + 16, slots), BF16),
            pltpu.VMEM((2, members + 16, slots), BF16),
            pltpu.VMEM((patches, members), BF16),
            pltpu.SemaphoreType.DMA,
        ],
        aliases={0: 0},
    )
    (update,) = call(
        functools.partial(update_kernel, local=local),
        [(devices * state_rows, LANES)],
        (states, powers, more, side),
        scratch=[
            pltpu.VMEM((2, 2, members, members), BF16),
            pltpu.VMEM((2, 2, members, members), BF16),
            pltpu.VMEM((2, 3 * members, cells), BF16),
            pltpu.VMEM((2, 8, cells), F32),
        ],
    )
    returned = exchange(update, "return_exchange")
    (analysis,) = call(
        unpack_kernel,
        [(local, patches, cells)],
        (spread, returned),
        outs=[HBM],
        scratch=[pltpu.VMEM((local, patches, cells), F32), pltpu.SemaphoreType.DMA((2 * local,))],
    )
    return analysis


def solution(mesh):
    placed = (P(AXES, None, None), P(AXES, None, None), P(), P(), P())
    return jax.shard_map(
        per_device, mesh=mesh, in_specs=placed, out_specs=P(AXES, None, None), check_vma=False
    )
```

```python
import functools

import jax
import jax.numpy as jnp
from jax import lax
from jax.experimental import pallas as pl
from jax.experimental.pallas import tpu as pltpu
from jax.sharding import PartitionSpec as P

SWEEPS = 8
LANES = 128
AXES = ("grp", "mem")
F32 = jnp.float32
BF16 = jnp.bfloat16
VMEM_LIMIT = 12 << 20
IN_PIECES = 2
OUT_PIECES = 4


def dot(a, b):
    return jnp.dot(a, b, preferred_element_type=F32)


def dot_nt(a, b):
    return lax.dot_general(a, b, (((1,), (1,)), ((), ())), preferred_element_type=F32)


def exact_dot(a, b):
    return jnp.dot(a, b, preferred_element_type=F32, precision=lax.Precision.HIGHEST)


def halves(x):
    high = x.astype(BF16)
    return high, (x - high.astype(F32)).astype(BF16)


def thirds(x):
    high = x.astype(BF16)
    rest = x - high.astype(F32)
    mid = rest.astype(BF16)
    return high, mid, (rest - mid.astype(F32)).astype(BF16)


def left_form(x):
    high, low = halves(x)
    return jnp.concatenate([high, high, low], axis=1)


def right_form(x):
    high, low = halves(x)
    return jnp.concatenate([high, low, high], axis=0)


def owners(counts, half, devices):
    patches = counts.shape[1]
    heavy = (counts > half).astype(F32)
    key = counts.astype(F32) * patches + lax.broadcasted_iota(jnp.int32, (1, patches), 1).astype(F32)
    sign = jnp.where(heavy > 0.0, -1.0, 1.0)
    order = sign * key
    column = jnp.broadcast_to(order, (8, patches)).T[:, :1]
    before = jnp.where((column < order) & ((column < 0.0) == (order < 0.0)), 1.0, 0.0)
    rank = jnp.sum(before, axis=0, keepdims=True)
    device = lax.broadcasted_iota(jnp.int32, (devices, patches), 0).astype(F32)
    heavies = jnp.where((device == rank) & (heavy > 0.0), 1.0, 0.0)
    lights = jnp.where((device == rank) & (heavy == 0.0), 1.0, 0.0)
    return heavies, lights


def store_rows(ref, first, stride, x):
    for j in range(x.shape[1] // LANES):
        ref[pl.ds(first + j, x.shape[0], stride=stride), :] = x[:, j * LANES : (j + 1) * LANES]


def tiles_sent(slots):
    return slots // LANES + slots // LANES // 4


def light_position(tile, slots):
    blocks = slots // LANES
    return blocks + tile if tile < blocks // 4 else blocks + blocks // 4 - 1 - tile


def pick(onehot, x):
    chosen = onehot.astype(BF16)
    return dot(jnp.concatenate([chosen] * 3, axis=1), jnp.concatenate(thirds(x), axis=0))


def pack_obs_kernel(counts_hbm, obs_hbm, out_hbm, flag_ref, counts_ref, obs_ref, out_ref, table_ref, table, sems, *, slots):
    patches = counts_ref.shape[1]
    blocks = slots // LANES
    each = patches * blocks
    local = obs_hbm.shape[0] // each
    sent_tiles = tiles_sent(slots)
    per = local * sent_tiles
    devices = out_hbm.shape[0] // per
    count_copy = pltpu.make_async_copy(counts_hbm, counts_ref, sems.at[0])
    count_copy.start()
    copies = []
    cut = each // IN_PIECES
    for i in range(local * IN_PIECES):
        span = pl.ds(i * cut, cut)
        copies.append(pltpu.make_async_copy(obs_hbm.at[span], obs_ref.at[span], sems.at[1 + i]))
        copies[-1].start()
    count_copy.wait()
    onehots = owners(counts_ref[...], slots // 2, devices)
    position = lax.broadcasted_iota(jnp.int32, (8, patches), 1).astype(F32).astype(BF16)
    index = [dot_nt(position, onehot.astype(BF16)).astype(jnp.int32) for onehot in onehots]
    lengths = ((counts_ref[...] + (LANES - 1)) >> 7).astype(F32)
    lengths = jnp.broadcast_to(lengths, (8, patches)).astype(BF16)
    long, short = (dot_nt(lengths, onehot.astype(BF16)).astype(jnp.int32) for onehot in onehots)
    excess = jnp.max((long + short).astype(F32), axis=1, keepdims=True) - sent_tiles
    flag_ref[...] = jnp.broadcast_to(excess, flag_ref.shape)
    start = [(p >> 3) * (8 * blocks) + (p & 7) for p in index]
    row = lax.broadcasted_iota(jnp.int32, (8, devices), 0)
    entries = jnp.where(row == 0, start[0], start[1])
    shared = [t for t in range(blocks // 2) if light_position(t, slots) < blocks]
    for i, t in enumerate(shared):
        at = light_position(t, slots)
        entries = jnp.where(row == 2 + i, jnp.where(long > at, start[0] + 8 * at, start[1] + 8 * t), entries)
    table_ref[...] = entries
    table_copy = pltpu.make_async_copy(table_ref, table, sems.at[0])
    table_copy.start()
    table_copy.wait()
    sent = []
    for copy in copies:
        copy.wait()
    group = devices // OUT_PIECES
    own = blocks - len(shared)
    rest = blocks // 2 - len(shared)
    for g in range(OUT_PIECES):
        for d in range(g * group, (g + 1) * group):
            for m in range(local):
                first = d * per + m * sent_tiles
                heavy, light = m * each + table[0, d], m * each + table[1, d]
                out_ref[first : first + own, :] = obs_ref[pl.ds(heavy, own, stride=8), :]
                for i, t in enumerate(shared):
                    at = first + light_position(t, slots)
                    out_ref[at : at + 1, :] = obs_ref[pl.ds(m * each + table[2 + i, d], 1), :]
                out_ref[first + blocks : first + blocks + rest, :] = obs_ref[pl.ds(light, rest, stride=8), :]
        some = pl.ds(g * group * per, group * per)
        sent.append(
            pltpu.make_async_copy(out_ref.at[some], out_hbm.at[some], sems.at[1 + local * IN_PIECES + g])
        )
        sent[-1].start()
    for copy in sent:
        copy.wait()


def pack_states_kernel(
    mine_ref, counts_ref, states_ref, value_ref, precision_ref, obs_hbm, out_hbm, extra_hbm, rows_ref, out_ref, extra_ref, obs_ref, sems
):
    local, patches, cells = states_ref.shape
    slots = value_ref.shape[1]
    blocks = cells // LANES
    per = 2 * local * blocks + 1
    devices = out_ref.shape[0] // per
    quarter = slots // 4
    obs_copies = []
    for m in range(local):
        obs_copies.append(
            pltpu.make_async_copy(obs_hbm.at[m, :, pl.ds(quarter, quarter)], obs_ref.at[m], sems.at[2 + m])
        )
        obs_copies[-1].start()
    counts = counts_ref[...]
    heavies, lights = owners(counts, slots // 2, devices)
    both = jnp.concatenate([heavies, lights], axis=0)
    for m in range(local):
        chosen = pick(both, states_ref[m])
        for k in range(2):
            store_rows(out_ref, (k * local + m) * blocks, per, chosen[k * devices : (k + 1) * devices])
    out_ref[pl.ds(per - 1, devices, stride=per), :] = jnp.zeros((devices, LANES), F32)
    copy = pltpu.make_async_copy(out_ref, out_hbm, sems.at[0])
    copy.start()
    for m in range(local):
        obs_copies[m].wait()
        store_rows(extra_ref, m * quarter // LANES, local * quarter // LANES, pick(lights, obs_ref[m]))
    extra_copy = pltpu.make_async_copy(extra_ref, extra_hbm, sems.at[1])
    extra_copy.start()
    here = lax.broadcasted_iota(jnp.int32, (devices, patches), 0) == mine_ref[0]
    own = [jnp.sum(jnp.where(here, onehot, 0.0), axis=0, keepdims=True) for onehot in (heavies, lights)]
    both = jnp.concatenate(own + [jnp.zeros((6, patches), F32)], axis=0)
    values = pick(both, value_ref[...])
    precisions = pick(both, precision_ref[...])
    slot = lax.broadcasted_iota(jnp.int32, (1, slots), 1).astype(F32)
    rows = []
    for k in range(2):
        count = jnp.sum(own[k] * counts.astype(F32), axis=1, keepdims=True)
        live = jnp.where(slot < count, 1.0, 0.0)
        rows += [values[k : k + 1], precisions[k : k + 1], live]
    length = jnp.sum(own[0] * counts.astype(F32), axis=1, keepdims=True)
    rows_ref[...] = jnp.concatenate(rows + [jnp.broadcast_to(length, (2, slots))], axis=0)
    copy.wait()
    extra_copy.wait()


def obs_columns(obs_ref, extra_ref, rows_ref, local):
    slots = rows_ref.shape[1]
    blocks = slots // LANES
    per = tiles_sent(slots) * local
    devices = obs_ref.shape[0] // per
    length = rows_ref[6:7, :LANES]
    for k in range(2):
        for c in range(blocks if k == 0 else blocks // 2):
            columns = slice(c * LANES, (c + 1) * LANES)
            at = c if k == 0 else light_position(c, slots)
            parts = [obs_ref[pl.ds(m * tiles_sent(slots) + at, devices, stride=per), :] for m in range(local)]
            if k == 1 and at < blocks:
                more = [
                    extra_ref[
                        pl.ds(m * (blocks // 4) + c - blocks // 4, devices, stride=local * (blocks // 4)), :
                    ]
                    for m in range(local)
                ]
                parts = [jnp.where(length > at * LANES, x, p) for x, p in zip(more, parts)]
            mean = sum(jnp.sum(p, axis=0, keepdims=True) for p in parts) * (1.0 / (local * devices))
            value, precision, live = (rows_ref[3 * k + i : 3 * k + i + 1, columns] for i in range(3))
            yield k, columns, [p - mean for p in parts], value - mean, precision, live


def sums_kernel(obs_ref, extra_ref, rows_ref, states_hbm, out_hbm, row_ref, sem, *, local):
    devices, per = out_hbm.shape[:2]
    members = local * devices
    misfit = jnp.zeros((1, LANES), F32)
    expected = jnp.zeros((1, LANES), F32)
    for _, _, parts, innov, precision, live in obs_columns(obs_ref, extra_ref, rows_ref, local):
        spread = sum(jnp.sum(p * p, axis=0, keepdims=True) for p in parts) * (1.0 / (members - 1.0))
        misfit += precision * live * innov * innov
        expected += live * (1.0 + precision * spread)
    lane = lax.broadcasted_iota(jnp.int32, (1, LANES), 1)
    row = jnp.where(
        lane == 0,
        jnp.sum(misfit, axis=1, keepdims=True),
        jnp.where(lane == 1, jnp.sum(expected, axis=1, keepdims=True), 0.0),
    )
    row_ref[...] = jnp.broadcast_to(row[None], row_ref.shape)
    copy = pltpu.make_async_copy(row_ref, out_hbm.at[:, per - 1], sem)
    copy.start()
    copy.wait()


def power_place(powers_ref, more_ref, members, k, i, h):
    place = (i * 2 + k) * (members // LANES) + h
    held = powers_ref.shape[0] // members
    return (powers_ref, place * members) if place < held else (more_ref, (place - held) * members)


def gram_kernel(
    obs_ref, extra_ref, rows_ref, counts_ref, powers_ref, more_ref, side_ref, spread_hbm, high_ref, low_ref, spread_ref, sem, *, local
):
    slots = rows_ref.shape[1]
    members = side_ref.shape[2]
    devices = members // local
    spread_ref[...] = jnp.concatenate(owners(counts_ref[...], slots // 2, devices), axis=0).T.astype(BF16)
    copy = pltpu.make_async_copy(spread_ref, spread_hbm, sem)
    copy.start()
    for k, columns, parts, innov, precision, live in obs_columns(obs_ref, extra_ref, rows_ref, local):
        scale = jnp.sqrt(precision * live)
        for m in range(local):
            high, low = halves(parts[m] * scale)
            high_ref[k, m * devices : (m + 1) * devices, columns] = high
            low_ref[k, m * devices : (m + 1) * devices, columns] = low
        high, low = halves(jnp.broadcast_to(scale * innov, (16, LANES)))
        high_ref[k, members:, columns] = high
        low_ref[k, members:, columns] = low
    diagonal = lax.broadcasted_iota(jnp.int32, (members, members), 0) == lax.broadcasted_iota(
        jnp.int32, (members, members), 1
    )
    for k in range(2):
        width = slots if k == 0 else slots // 2
        high, low = high_ref[k, :, :width], low_ref[k, :, :width]
        gram = dot_nt(high, high[:members]) + dot_nt(high, low[:members]) + dot_nt(low, high[:members])
        forcing = gram[members : members + 8]
        gram = gram[:members]
        size = jnp.sqrt(jnp.sum(jnp.sum(gram * gram, axis=0, keepdims=True), axis=1, keepdims=True))
        unit = gram / jnp.maximum(size, 1e-30)
        trace = jnp.sum(
            jnp.sum(jnp.where(diagonal, unit, 0.0), axis=0, keepdims=True), axis=1, keepdims=True
        )
        second = exact_dot(unit, unit)
        for i, power in enumerate((unit, second, exact_dot(unit, second), exact_dot(second, second))):
            for h in range(members // LANES):
                ref, first = power_place(powers_ref, more_ref, members, k, i, h)
                ref[first : first + members] = power[:, h * LANES : (h + 1) * LANES]
        side_ref[k] = jnp.concatenate(
            [forcing, jnp.broadcast_to(size, (8, members)), jnp.broadcast_to(trace, (8, members))], axis=0
        )
    copy.wait()


def update_kernel(
    states_ref, powers_ref, more_ref, side_ref, out_ref, s_ref, z_ref, states_right, center_ref, *, local
):
    members = side_ref.shape[2]
    devices = members // local
    per = states_ref.shape[0] // devices
    blocks = out_ref.shape[0] // devices // (2 * local)
    total = jnp.sum(states_ref[pl.ds(per - 1, devices, stride=per), :], axis=0, keepdims=True)
    lane = lax.broadcasted_iota(jnp.int32, total.shape, 1)
    misfit = jnp.sum(jnp.where(lane == 0, total, 0.0), axis=1, keepdims=True)
    expected = jnp.sum(jnp.where(lane == 1, total, 0.0), axis=1, keepdims=True)
    squared = misfit / expected
    inflation = jnp.sqrt(squared)
    diagonal = lax.broadcasted_iota(jnp.int32, (members, members), 0) == lax.broadcasted_iota(
        jnp.int32, (members, members), 1
    )
    free = members - 1.0

    def plus_diagonal(x, value):
        return x + jnp.where(diagonal, value, 0.0)

    def put(ref, k, x):
        ref[k, 0], ref[k, 1] = halves(x)

    def left(ref, k):
        return jnp.concatenate([ref[k, 0], ref[k, 0], ref[k, 1]], axis=1)

    def right(ref, k):
        return jnp.concatenate([ref[k, 0], ref[k, 1], ref[k, 0]], axis=0)

    def whole(ref, k):
        return ref[k, 0].astype(F32) + ref[k, 1].astype(F32)

    def square(k):
        return dot(left(s_ref, k), right(s_ref, k))

    def refine(k, product):
        s = whole(s_ref, k)
        return 2.25 * s + dot(left_form(0.25 * product - 1.5 * s), right(s_ref, k))

    def advance(k):
        return 1.5 * whole(z_ref, k) - 0.5 * dot(left(s_ref, k), right(z_ref, k))

    scalers = []
    for k in range(2):
        size, trace = side_ref[k, 8:9, :1], side_ref[k, 16:17, :1]
        strength = squared * size
        scaler = jnp.sqrt(free * free * members + strength * (2.0 * free * trace + strength))
        scalers.append(scaler)
        a, b = free / scaler, strength / scaler
        f = 1.5 - 0.5 * a
        s1 = (a * f * f, b * f * (f - a), b * b * (0.25 * a - f), 0.25 * b * b * b)
        d = (1.5 - 0.5 * s1[0], -0.5 * s1[1], -0.5 * s1[2], -0.5 * s1[3])
        h = -0.5 * b
        z2 = (f * d[0], f * d[1] + h * d[0], f * d[2] + h * d[1], f * d[3] + h * d[2], h * d[3])
        powers = []
        for i in range(4):
            places = [power_place(powers_ref, more_ref, members, k, i, h) for h in range(members // LANES)]
            powers.append(jnp.concatenate([ref[first : first + members] for ref, first in places], axis=1))
        put(s_ref, k, plus_diagonal(sum(c * p for c, p in zip(s1[1:], powers)), s1[0]))
        put(z_ref, k, plus_diagonal(sum(c * p for c, p in zip(z2[1:], powers)), z2[0]))
    for k in range(2):
        put(s_ref, k, refine(k, square(k)))
        for c in range(blocks):
            rows = [(k * local + m) * blocks + c for m in range(local)]
            parts = [states_ref[pl.ds(r, devices, stride=per), :] for r in rows]
            center = sum(jnp.sum(p, axis=0, keepdims=True) for p in parts) * (1.0 / members)
            columns = slice(c * LANES, (c + 1) * LANES)
            center_ref[k, :, columns] = jnp.broadcast_to(center, (8, LANES))
            for m in range(local):
                high, low = halves(parts[m] - center)
                for i, piece in enumerate((high, low)):
                    first = i * members + m * devices
                    states_right[k, first : first + devices, columns] = piece

    for _ in range(SWEEPS - 3):
        products = [square(k) for k in range(2)]
        roots = [advance(k) for k in range(2)]
        for k in range(2):
            s = refine(k, products[k])
            put(s_ref, k, s)
            put(z_ref, k, roots[k])

    roots = [advance(k) for k in range(2)]
    transforms = []
    for k in range(2):
        root = roots[k]
        forcing = squared / scalers[k] * side_ref[k, :1]
        half_way = jnp.sum(root * forcing, axis=1, keepdims=True)
        shifts = jnp.sum(root * half_way, axis=0, keepdims=True)
        transforms.append((inflation * free**0.5 / jnp.sqrt(scalers[k])) * root + shifts)
    for k in range(2):
        high, low = states_right[k, :members], states_right[k, members:]
        update = dot(left_form(transforms[k]), jnp.concatenate([high, low, high], axis=0)) + center_ref[k, :1]
        for c in range(blocks):
            for m in range(local):
                piece = update[m * devices : (m + 1) * devices, c * LANES : (c + 1) * LANES]
                out_ref[pl.ds((k * local + m) * blocks + c, devices, stride=2 * local * blocks), :] = piece


def unpack_kernel(spread_ref, rows_ref, out_hbm, out_ref, sems):
    local, patches, cells = out_ref.shape
    blocks = cells // LANES
    per = 2 * local * blocks
    devices = rows_ref.shape[0] // per
    spread = jnp.concatenate([spread_ref[...]] * 2, axis=1)
    wide = blocks // 2
    copies = []
    for m in range(local):
        for part in range(2):
            x = jnp.concatenate(
                [
                    jnp.concatenate(
                        [
                            rows_ref[pl.ds((k * local + m) * blocks + part * wide + j, devices, stride=per), :]
                            for j in range(wide)
                        ],
                        axis=1,
                    )
                    for k in range(2)
                ],
                axis=0,
            )
            columns = pl.ds(part * wide * LANES, wide * LANES)
            out_ref[m, :, columns] = dot(spread, jnp.concatenate(halves(x), axis=0))
            copies.append(
                pltpu.make_async_copy(
                    out_ref.at[m, :, columns], out_hbm.at[m, :, columns], sems.at[2 * m + part]
                )
            )
            copies[-1].start()
    for copy in copies:
        copy.wait()


HBM = pl.BlockSpec(memory_space=pltpu.HBM)
WHOLE = pl.BlockSpec(memory_space=pltpu.VMEM)
SCALAR = pl.BlockSpec(memory_space=pltpu.SMEM)


def call(kernel, out_shapes, inputs, ins=None, outs=None, types=None, scratch=(), aliases={}):
    ins = ins or [WHOLE] * len(inputs)
    outs = outs or [WHOLE] * len(out_shapes)
    inputs = [pltpu.with_memory_space_constraint(x, pltpu.HBM) if s is HBM else x for x, s in zip(inputs, ins)]
    return pl.pallas_call(
        kernel,
        out_shape=[
            pltpu.HBM(shape, kind) if s is HBM else jax.ShapeDtypeStruct(shape, kind)
            for shape, kind, s in zip(out_shapes, types or [F32] * len(outs), outs)
        ],
        in_specs=ins,
        out_specs=outs,
        scratch_shapes=list(scratch),
        input_output_aliases=aliases,
        compiler_params=pltpu.CompilerParams(vmem_limit_bytes=VMEM_LIMIT),
    )(*inputs)


def exchange(x, name):
    with jax.named_scope(name):
        rows = x.reshape(-1, 1, LANES)
        return lax.all_to_all(rows, AXES, split_axis=0, concat_axis=0, tiled=True).reshape(-1, LANES)


def per_device(background, obs_ensemble, obs_value, obs_precision, obs_count):
    devices = lax.axis_size(AXES)
    local, patches, cells = background.shape
    slots = obs_ensemble.shape[2]
    members = local * devices
    counts = obs_count.reshape(1, patches)
    mine = lax.axis_index(AXES).astype(jnp.int32).reshape(1)
    obs_rows = tiles_sent(slots) * local
    extra_rows = local * slots // 4 // LANES
    state_rows = 2 * local * cells // LANES
    blocks = slots // LANES
    in_memory = obs_ensemble.reshape(local, patches // 8, 8, blocks, LANES).swapaxes(2, 3).reshape(-1, LANES)
    obs_sent, excess = call(
        functools.partial(pack_obs_kernel, slots=slots),
        [(devices * obs_rows, LANES), (8, LANES)],
        (counts, in_memory),
        ins=[HBM, HBM],
        outs=[HBM, WHOLE],
        scratch=[
            pltpu.VMEM((1, patches), jnp.int32),
            pltpu.VMEM(in_memory.shape, F32),
            pltpu.VMEM((devices * obs_rows, LANES), F32),
            pltpu.VMEM((8, devices), jnp.int32),
            pltpu.SMEM((8, devices), jnp.int32),
            pltpu.SemaphoreType.DMA((1 + local * IN_PIECES + OUT_PIECES,)),
        ],
    )
    obs = exchange(obs_sent, "obs_exchange")
    states_sent, extra_sent, rows = call(
        pack_states_kernel,
        [(devices * (state_rows + 1), LANES), (devices * extra_rows, LANES), (8, slots)],
        (mine, counts, background, obs_value, obs_precision, obs_ensemble),
        ins=[SCALAR] + [WHOLE] * 4 + [HBM],
        outs=[HBM, HBM, WHOLE],
        scratch=[
            pltpu.VMEM((devices * (state_rows + 1), LANES), F32),
            pltpu.VMEM((devices * extra_rows, LANES), F32),
            pltpu.VMEM((local, patches, slots // 4), F32),
            pltpu.SemaphoreType.DMA((2 + local,)),
        ],
    )
    obs, extra_sent = lax.optimization_barrier((obs, extra_sent))
    extra = lax.cond(excess[0, 0] > 0.0, lambda x: exchange(x, "extra_exchange"), jnp.zeros_like, extra_sent)
    states_sent = states_sent.reshape(devices, state_rows + 1, 1, LANES)
    (states_sent,) = call(
        functools.partial(sums_kernel, local=local),
        [states_sent.shape],
        (obs, extra, rows, states_sent),
        ins=[WHOLE, WHOLE, WHOLE, HBM],
        outs=[HBM],
        scratch=[pltpu.VMEM((devices, 1, LANES), F32), pltpu.SemaphoreType.DMA],
        aliases={3: 0},
    )
    states = exchange(states_sent, "states_exchange")
    powers, more, side, spread = call(
        functools.partial(gram_kernel, local=local),
        [obs.shape, (8 * members * members // LANES - obs.shape[0], LANES), (2, 24, members), (patches, members)],
        (obs, extra, rows, counts),
        outs=[WHOLE, WHOLE, WHOLE, HBM],
        types=[F32, F32, F32, BF16],
        scratch=[
            pltpu.VMEM((2, members + 16, slots), BF16),
            pltpu.VMEM((2, members + 16, slots), BF16),
            pltpu.VMEM((patches, members), BF16),
            pltpu.SemaphoreType.DMA,
        ],
        aliases={0: 0},
    )
    (update,) = call(
        functools.partial(update_kernel, local=local),
        [(devices * state_rows, LANES)],
        (states, powers, more, side),
        scratch=[
            pltpu.VMEM((2, 2, members, members), BF16),
            pltpu.VMEM((2, 2, members, members), BF16),
            pltpu.VMEM((2, 2 * members, cells), BF16),
            pltpu.VMEM((2, 8, cells), F32),
        ],
    )
    returned = exchange(update, "return_exchange")
    (analysis,) = call(
        unpack_kernel,
        [(local, patches, cells)],
        (spread, returned),
        outs=[HBM],
        scratch=[pltpu.VMEM((local, patches, cells), F32), pltpu.SemaphoreType.DMA((2 * local,))],
    )
    return analysis


def solution(mesh):
    placed = (P(AXES, None, None), P(AXES, None, None), P(), P(), P())
    return jax.shard_map(
        per_device, mesh=mesh, in_specs=placed, out_specs=P(AXES, None, None), check_vma=False
    )
```

```python
import functools

import jax
import jax.numpy as jnp
from jax import lax
from jax.experimental import pallas as pl
from jax.experimental.pallas import tpu as pltpu
from jax.sharding import PartitionSpec as P

SWEEPS = 8
LANES = 128
AXES = ("grp", "mem")
F32 = jnp.float32
BF16 = jnp.bfloat16
VMEM_LIMIT = 12 << 20
IN_PIECES = 2
OUT_PIECES = 8


def dot(a, b):
    return jnp.dot(a, b, preferred_element_type=F32)


def dot_nt(a, b):
    return lax.dot_general(a, b, (((1,), (1,)), ((), ())), preferred_element_type=F32)


def exact_dot(a, b):
    return jnp.dot(a, b, preferred_element_type=F32, precision=lax.Precision.HIGHEST)


def halves(x):
    high = x.astype(BF16)
    return high, (x - high.astype(F32)).astype(BF16)


def thirds(x):
    high = x.astype(BF16)
    rest = x - high.astype(F32)
    mid = rest.astype(BF16)
    return high, mid, (rest - mid.astype(F32)).astype(BF16)


def left_form(x):
    high, low = halves(x)
    return jnp.concatenate([high, high, low], axis=1)


def right_form(x):
    high, low = halves(x)
    return jnp.concatenate([high, low, high], axis=0)


def owners(counts, half, devices):
    patches = counts.shape[1]
    heavy = (counts > half).astype(F32)
    key = counts.astype(F32) * patches + lax.broadcasted_iota(jnp.int32, (1, patches), 1).astype(F32)
    sign = jnp.where(heavy > 0.0, -1.0, 1.0)
    order = sign * key
    column = jnp.broadcast_to(order, (8, patches)).T[:, :1]
    before = jnp.where((column < order) & ((column < 0.0) == (order < 0.0)), 1.0, 0.0)
    rank = jnp.sum(before, axis=0, keepdims=True)
    device = lax.broadcasted_iota(jnp.int32, (devices, patches), 0).astype(F32)
    heavies = jnp.where((device == rank) & (heavy > 0.0), 1.0, 0.0)
    lights = jnp.where((device == rank) & (heavy == 0.0), 1.0, 0.0)
    return heavies, lights


def store_rows(ref, first, stride, x):
    for j in range(x.shape[1] // LANES):
        ref[pl.ds(first + j, x.shape[0], stride=stride), :] = x[:, j * LANES : (j + 1) * LANES]


def tiles_sent(slots):
    return slots // LANES + slots // LANES // 4


def light_position(tile, slots):
    blocks = slots // LANES
    return blocks + tile if tile < blocks // 4 else blocks + blocks // 4 - 1 - tile


def pick(onehot, x):
    chosen = onehot.astype(BF16)
    return dot(jnp.concatenate([chosen] * 3, axis=1), jnp.concatenate(thirds(x), axis=0))


def pack_obs_kernel(counts_hbm, obs_hbm, out_hbm, flag_ref, counts_ref, obs_ref, out_ref, sems, *, slots):
    patches = counts_ref.shape[1]
    blocks = slots // LANES
    each = patches * blocks
    local = obs_hbm.shape[0] // each
    sent_tiles = tiles_sent(slots)
    per = local * sent_tiles
    devices = out_hbm.shape[0] // per
    count_copy = pltpu.make_async_copy(counts_hbm, counts_ref, sems.at[0])
    count_copy.start()
    copies = []
    cut = each // IN_PIECES
    for i in range(local * IN_PIECES):
        span = pl.ds(i * cut, cut)
        copies.append(pltpu.make_async_copy(obs_hbm.at[span], obs_ref.at[span], sems.at[1 + i]))
        copies[-1].start()
    count_copy.wait()
    onehots = owners(counts_ref[...], slots // 2, devices)
    lengths = ((counts_ref[...] + (LANES - 1)) >> 7).astype(F32)
    position = lax.broadcasted_iota(jnp.int32, (8, patches), 1).astype(F32)
    first_row = lax.broadcasted_iota(jnp.int32, (8, patches), 0) == 0
    facts = dot_nt(
        jnp.where(first_row, position, lengths).astype(BF16), jnp.concatenate(onehots, axis=0).astype(BF16)
    ).astype(jnp.int32)
    index = [facts[:1, :devices], facts[:1, devices:]]
    long, short = facts[1:2, :devices], facts[1:2, devices:]
    excess = jnp.max((long + short).astype(F32), axis=1, keepdims=True) - sent_tiles
    flag_ref[...] = jnp.broadcast_to(excess, flag_ref.shape)
    start = [(p >> 3) * (8 * blocks) + (p & 7) for p in index]
    shared = [t for t in range(blocks // 2) if light_position(t, slots) < blocks]
    packed = start[0] + (start[1] << 12)
    for i, t in enumerate(shared):
        packed += jnp.where(long > light_position(t, slots), 1 << (24 + i), 0)
    sent = []
    for copy in copies:
        copy.wait()
    group = devices // OUT_PIECES
    own = blocks - len(shared)
    rest = blocks // 2 - len(shared)
    for g in range(OUT_PIECES):
        for d in range(g * group, (g + 1) * group):
            entry = packed[0, d]
            heavy_start, light_start = entry & 4095, (entry >> 12) & 4095
            middle = [
                jnp.where(
                    (entry >> (24 + i)) & 1 == 1,
                    heavy_start + 8 * light_position(t, slots),
                    light_start + 8 * t,
                )
                for i, t in enumerate(shared)
            ]
            for m in range(local):
                first = d * per + m * sent_tiles
                heavy, light = m * each + heavy_start, m * each + light_start
                out_ref[first : first + own, :] = obs_ref[pl.ds(heavy, own, stride=8), :]
                for i, t in enumerate(shared):
                    at = first + light_position(t, slots)
                    out_ref[at : at + 1, :] = obs_ref[pl.ds(m * each + middle[i], 1), :]
                out_ref[first + blocks : first + blocks + rest, :] = obs_ref[pl.ds(light, rest, stride=8), :]
        some = pl.ds(g * group * per, group * per)
        sent.append(
            pltpu.make_async_copy(out_ref.at[some], out_hbm.at[some], sems.at[1 + local * IN_PIECES + g])
        )
        sent[-1].start()
    for copy in sent:
        copy.wait()


def pack_states_kernel(
    mine_ref, counts_ref, states_ref, value_ref, precision_ref, obs_hbm, out_hbm, extra_hbm, rows_ref, out_ref, extra_ref, obs_ref, sems
):
    local, patches, cells = states_ref.shape
    slots = value_ref.shape[1]
    blocks = cells // LANES
    per = 2 * local * blocks + 1
    devices = out_ref.shape[0] // per
    quarter = slots // 4
    obs_copies = []
    for m in range(local):
        obs_copies.append(
            pltpu.make_async_copy(obs_hbm.at[m, :, pl.ds(quarter, quarter)], obs_ref.at[m], sems.at[2 + m])
        )
        obs_copies[-1].start()
    counts = counts_ref[...]
    heavies, lights = owners(counts, slots // 2, devices)
    both = jnp.concatenate([heavies, lights], axis=0)
    for m in range(local):
        chosen = pick(both, states_ref[m])
        for k in range(2):
            store_rows(out_ref, (k * local + m) * blocks, per, chosen[k * devices : (k + 1) * devices])
    out_ref[pl.ds(per - 1, devices, stride=per), :] = jnp.zeros((devices, LANES), F32)
    copy = pltpu.make_async_copy(out_ref, out_hbm, sems.at[0])
    copy.start()
    for m in range(local):
        obs_copies[m].wait()
        store_rows(extra_ref, m * quarter // LANES, local * quarter // LANES, pick(lights, obs_ref[m]))
    extra_copy = pltpu.make_async_copy(extra_ref, extra_hbm, sems.at[1])
    extra_copy.start()
    here = lax.broadcasted_iota(jnp.int32, (devices, patches), 0) == mine_ref[0]
    own = [jnp.sum(jnp.where(here, onehot, 0.0), axis=0, keepdims=True) for onehot in (heavies, lights)]
    both = jnp.concatenate(own + [jnp.zeros((6, patches), F32)], axis=0)
    values = pick(both, value_ref[...])
    precisions = pick(both, precision_ref[...])
    slot = lax.broadcasted_iota(jnp.int32, (1, slots), 1).astype(F32)
    rows = []
    for k in range(2):
        count = jnp.sum(own[k] * counts.astype(F32), axis=1, keepdims=True)
        live = jnp.where(slot < count, 1.0, 0.0)
        rows += [values[k : k + 1], precisions[k : k + 1], live]
    length = jnp.sum(own[0] * counts.astype(F32), axis=1, keepdims=True)
    rows_ref[...] = jnp.concatenate(rows + [jnp.broadcast_to(length, (2, slots))], axis=0)
    copy.wait()
    extra_copy.wait()


def obs_columns(obs_ref, extra_ref, rows_ref, local):
    slots = rows_ref.shape[1]
    blocks = slots // LANES
    per = tiles_sent(slots) * local
    devices = obs_ref.shape[0] // per
    length = rows_ref[6:7, :LANES]
    for k in range(2):
        for c in range(blocks if k == 0 else blocks // 2):
            columns = slice(c * LANES, (c + 1) * LANES)
            at = c if k == 0 else light_position(c, slots)
            parts = [obs_ref[pl.ds(m * tiles_sent(slots) + at, devices, stride=per), :] for m in range(local)]
            if k == 1 and at < blocks:
                more = [
                    extra_ref[
                        pl.ds(m * (blocks // 4) + c - blocks // 4, devices, stride=local * (blocks // 4)), :
                    ]
                    for m in range(local)
                ]
                parts = [jnp.where(length > at * LANES, x, p) for x, p in zip(more, parts)]
            mean = sum(jnp.sum(p, axis=0, keepdims=True) for p in parts) * (1.0 / (local * devices))
            value, precision, live = (rows_ref[3 * k + i : 3 * k + i + 1, columns] for i in range(3))
            yield k, columns, [p - mean for p in parts], value - mean, precision, live


def sums_kernel(obs_ref, extra_ref, rows_ref, states_hbm, out_hbm, row_ref, sem, *, local):
    devices, per = out_hbm.shape[:2]
    members = local * devices
    misfit = jnp.zeros((1, LANES), F32)
    expected = jnp.zeros((1, LANES), F32)
    for _, _, parts, innov, precision, live in obs_columns(obs_ref, extra_ref, rows_ref, local):
        spread = sum(jnp.sum(p * p, axis=0, keepdims=True) for p in parts) * (1.0 / (members - 1.0))
        misfit += precision * live * innov * innov
        expected += live * (1.0 + precision * spread)
    lane = lax.broadcasted_iota(jnp.int32, (1, LANES), 1)
    row = jnp.where(
        lane == 0,
        jnp.sum(misfit, axis=1, keepdims=True),
        jnp.where(lane == 1, jnp.sum(expected, axis=1, keepdims=True), 0.0),
    )
    row_ref[...] = jnp.broadcast_to(row[None], row_ref.shape)
    copy = pltpu.make_async_copy(row_ref, out_hbm.at[:, per - 1], sem)
    copy.start()
    copy.wait()


def power_place(powers_ref, more_ref, members, k, i, h):
    place = (i * 2 + k) * (members // LANES) + h
    held = powers_ref.shape[0] // members
    return (powers_ref, place * members) if place < held else (more_ref, (place - held) * members)


def gram_kernel(
    obs_ref, extra_ref, rows_ref, counts_ref, powers_ref, more_ref, side_ref, spread_hbm, high_ref, low_ref, spread_ref, sem, *, local
):
    slots = rows_ref.shape[1]
    members = side_ref.shape[2]
    devices = members // local
    spread_ref[...] = jnp.concatenate(owners(counts_ref[...], slots // 2, devices), axis=0).T.astype(BF16)
    copy = pltpu.make_async_copy(spread_ref, spread_hbm, sem)
    copy.start()
    for k, columns, parts, innov, precision, live in obs_columns(obs_ref, extra_ref, rows_ref, local):
        scale = jnp.sqrt(precision * live)
        for m in range(local):
            high, low = halves(parts[m] * scale)
            high_ref[k, m * devices : (m + 1) * devices, columns] = high
            low_ref[k, m * devices : (m + 1) * devices, columns] = low
        high, low = halves(jnp.broadcast_to(scale * innov, (16, LANES)))
        high_ref[k, members:, columns] = high
        low_ref[k, members:, columns] = low
    diagonal = lax.broadcasted_iota(jnp.int32, (members, members), 0) == lax.broadcasted_iota(
        jnp.int32, (members, members), 1
    )
    for k in range(2):
        width = slots if k == 0 else slots // 2
        high, low = high_ref[k, :, :width], low_ref[k, :, :width]
        gram = dot_nt(high, high[:members]) + dot_nt(high, low[:members]) + dot_nt(low, high[:members])
        forcing = gram[members : members + 8]
        gram = gram[:members]
        size = jnp.sqrt(jnp.sum(jnp.sum(gram * gram, axis=0, keepdims=True), axis=1, keepdims=True))
        unit = gram / jnp.maximum(size, 1e-30)
        trace = jnp.sum(
            jnp.sum(jnp.where(diagonal, unit, 0.0), axis=0, keepdims=True), axis=1, keepdims=True
        )
        second = exact_dot(unit, unit)
        for i, power in enumerate((unit, second, exact_dot(unit, second), exact_dot(second, second))):
            for h in range(members // LANES):
                ref, first = power_place(powers_ref, more_ref, members, k, i, h)
                ref[first : first + members] = power[:, h * LANES : (h + 1) * LANES]
        side_ref[k] = jnp.concatenate(
            [forcing, jnp.broadcast_to(size, (8, members)), jnp.broadcast_to(trace, (8, members))], axis=0
        )
    copy.wait()


def update_kernel(
    states_ref, powers_ref, more_ref, side_ref, out_ref, s_ref, z_ref, states_right, center_ref, *, local
):
    members = side_ref.shape[2]
    devices = members // local
    per = states_ref.shape[0] // devices
    blocks = out_ref.shape[0] // devices // (2 * local)
    total = jnp.sum(states_ref[pl.ds(per - 1, devices, stride=per), :], axis=0, keepdims=True)
    lane = lax.broadcasted_iota(jnp.int32, total.shape, 1)
    misfit = jnp.sum(jnp.where(lane == 0, total, 0.0), axis=1, keepdims=True)
    expected = jnp.sum(jnp.where(lane == 1, total, 0.0), axis=1, keepdims=True)
    squared = misfit / expected
    inflation = jnp.sqrt(squared)
    diagonal = lax.broadcasted_iota(jnp.int32, (members, members), 0) == lax.broadcasted_iota(
        jnp.int32, (members, members), 1
    )
    free = members - 1.0

    def plus_diagonal(x, value):
        return x + jnp.where(diagonal, value, 0.0)

    def put(ref, k, x):
        ref[k, 0], ref[k, 1] = halves(x)

    def left(ref, k):
        return jnp.concatenate([ref[k, 0], ref[k, 0], ref[k, 1]], axis=1)

    def right(ref, k):
        return jnp.concatenate([ref[k, 0], ref[k, 1], ref[k, 0]], axis=0)

    def whole(ref, k):
        return ref[k, 0].astype(F32) + ref[k, 1].astype(F32)

    def square(k):
        return dot(left(s_ref, k), right(s_ref, k))

    def refine(k, product):
        s = whole(s_ref, k)
        return 2.25 * s + dot(left_form(0.25 * product - 1.5 * s), right(s_ref, k))

    def advance(k):
        return 1.5 * whole(z_ref, k) - 0.5 * dot(left(s_ref, k), right(z_ref, k))

    scalers = []
    for k in range(2):
        size, trace = side_ref[k, 8:9, :1], side_ref[k, 16:17, :1]
        strength = squared * size
        scaler = jnp.sqrt(free * free * members + strength * (2.0 * free * trace + strength))
        scalers.append(scaler)
        a, b = free / scaler, strength / scaler
        f = 1.5 - 0.5 * a
        s1 = (a * f * f, b * f * (f - a), b * b * (0.25 * a - f), 0.25 * b * b * b)
        d = (1.5 - 0.5 * s1[0], -0.5 * s1[1], -0.5 * s1[2], -0.5 * s1[3])
        h = -0.5 * b
        z2 = (f * d[0], f * d[1] + h * d[0], f * d[2] + h * d[1], f * d[3] + h * d[2], h * d[3])
        powers = []
        for i in range(4):
            places = [power_place(powers_ref, more_ref, members, k, i, h) for h in range(members // LANES)]
            powers.append(jnp.concatenate([ref[first : first + members] for ref, first in places], axis=1))
        put(s_ref, k, plus_diagonal(sum(c * p for c, p in zip(s1[1:], powers)), s1[0]))
        put(z_ref, k, plus_diagonal(sum(c * p for c, p in zip(z2[1:], powers)), z2[0]))
    for k in range(2):
        put(s_ref, k, refine(k, square(k)))
        for c in range(blocks):
            rows = [(k * local + m) * blocks + c for m in range(local)]
            parts = [states_ref[pl.ds(r, devices, stride=per), :] for r in rows]
            center = sum(jnp.sum(p, axis=0, keepdims=True) for p in parts) * (1.0 / members)
            columns = slice(c * LANES, (c + 1) * LANES)
            center_ref[k, :, columns] = jnp.broadcast_to(center, (8, LANES))
            for m in range(local):
                high, low = halves(parts[m] - center)
                for i, piece in enumerate((high, low)):
                    first = i * members + m * devices
                    states_right[k, first : first + devices, columns] = piece

    for _ in range(SWEEPS - 3):
        products = [square(k) for k in range(2)]
        roots = [advance(k) for k in range(2)]
        for k in range(2):
            s = refine(k, products[k])
            put(s_ref, k, s)
            put(z_ref, k, roots[k])

    roots = [advance(k) for k in range(2)]
    transforms = []
    for k in range(2):
        root = roots[k]
        forcing = squared / scalers[k] * side_ref[k, :1]
        half_way = jnp.sum(root * forcing, axis=1, keepdims=True)
        shifts = jnp.sum(root * half_way, axis=0, keepdims=True)
        transforms.append((inflation * free**0.5 / jnp.sqrt(scalers[k])) * root + shifts)
    for k in range(2):
        high, low = states_right[k, :members], states_right[k, members:]
        update = dot(left_form(transforms[k]), jnp.concatenate([high, low, high], axis=0)) + center_ref[k, :1]
        for c in range(blocks):
            for m in range(local):
                piece = update[m * devices : (m + 1) * devices, c * LANES : (c + 1) * LANES]
                out_ref[pl.ds((k * local + m) * blocks + c, devices, stride=2 * local * blocks), :] = piece


def unpack_kernel(spread_ref, rows_ref, out_hbm, out_ref, sems):
    local, patches, cells = out_ref.shape
    blocks = cells // LANES
    per = 2 * local * blocks
    devices = rows_ref.shape[0] // per
    spread = jnp.concatenate([spread_ref[...]] * 2, axis=1)
    wide = blocks // 2
    copies = []
    for m in range(local):
        for part in range(2):
            x = jnp.concatenate(
                [
                    jnp.concatenate(
                        [
                            rows_ref[pl.ds((k * local + m) * blocks + part * wide + j, devices, stride=per), :]
                            for j in range(wide)
                        ],
                        axis=1,
                    )
                    for k in range(2)
                ],
                axis=0,
            )
            columns = pl.ds(part * wide * LANES, wide * LANES)
            out_ref[m, :, columns] = dot(spread, jnp.concatenate(halves(x), axis=0))
            copies.append(
                pltpu.make_async_copy(
                    out_ref.at[m, :, columns], out_hbm.at[m, :, columns], sems.at[2 * m + part]
                )
            )
            copies[-1].start()
    for copy in copies:
        copy.wait()


HBM = pl.BlockSpec(memory_space=pltpu.HBM)
WHOLE = pl.BlockSpec(memory_space=pltpu.VMEM)
SCALAR = pl.BlockSpec(memory_space=pltpu.SMEM)


def call(kernel, out_shapes, inputs, ins=None, outs=None, types=None, scratch=(), aliases={}):
    ins = ins or [WHOLE] * len(inputs)
    outs = outs or [WHOLE] * len(out_shapes)
    inputs = [pltpu.with_memory_space_constraint(x, pltpu.HBM) if s is HBM else x for x, s in zip(inputs, ins)]
    return pl.pallas_call(
        kernel,
        out_shape=[
            pltpu.HBM(shape, kind) if s is HBM else jax.ShapeDtypeStruct(shape, kind)
            for shape, kind, s in zip(out_shapes, types or [F32] * len(outs), outs)
        ],
        in_specs=ins,
        out_specs=outs,
        scratch_shapes=list(scratch),
        input_output_aliases=aliases,
        compiler_params=pltpu.CompilerParams(vmem_limit_bytes=VMEM_LIMIT),
    )(*inputs)


def exchange(x, name):
    with jax.named_scope(name):
        rows = x.reshape(-1, 1, LANES)
        return lax.all_to_all(rows, AXES, split_axis=0, concat_axis=0, tiled=True).reshape(-1, LANES)


def per_device(background, obs_ensemble, obs_value, obs_precision, obs_count):
    devices = lax.axis_size(AXES)
    local, patches, cells = background.shape
    slots = obs_ensemble.shape[2]
    members = local * devices
    counts = obs_count.reshape(1, patches)
    mine = lax.axis_index(AXES).astype(jnp.int32).reshape(1)
    obs_rows = tiles_sent(slots) * local
    extra_rows = local * slots // 4 // LANES
    state_rows = 2 * local * cells // LANES
    blocks = slots // LANES
    in_memory = obs_ensemble.reshape(local, patches // 8, 8, blocks, LANES).swapaxes(2, 3).reshape(-1, LANES)
    obs_sent, excess = call(
        functools.partial(pack_obs_kernel, slots=slots),
        [(devices * obs_rows, LANES), (8, LANES)],
        (counts, in_memory),
        ins=[HBM, HBM],
        outs=[HBM, WHOLE],
        scratch=[
            pltpu.VMEM((1, patches), jnp.int32),
            pltpu.VMEM(in_memory.shape, F32),
            pltpu.VMEM((devices * obs_rows, LANES), F32),
            pltpu.SemaphoreType.DMA((1 + local * IN_PIECES + OUT_PIECES,)),
        ],
    )
    obs = exchange(obs_sent, "obs_exchange")
    states_sent, extra_sent, rows = call(
        pack_states_kernel,
        [(devices * (state_rows + 1), LANES), (devices * extra_rows, LANES), (8, slots)],
        (mine, counts, background, obs_value, obs_precision, obs_ensemble),
        ins=[SCALAR] + [WHOLE] * 4 + [HBM],
        outs=[HBM, HBM, WHOLE],
        scratch=[
            pltpu.VMEM((devices * (state_rows + 1), LANES), F32),
            pltpu.VMEM((devices * extra_rows, LANES), F32),
            pltpu.VMEM((local, patches, slots // 4), F32),
            pltpu.SemaphoreType.DMA((2 + local,)),
        ],
    )
    obs, extra_sent = lax.optimization_barrier((obs, extra_sent))
    extra = lax.cond(excess[0, 0] > 0.0, lambda x: exchange(x, "extra_exchange"), jnp.zeros_like, extra_sent)
    states_sent = states_sent.reshape(devices, state_rows + 1, 1, LANES)
    (states_sent,) = call(
        functools.partial(sums_kernel, local=local),
        [states_sent.shape],
        (obs, extra, rows, states_sent),
        ins=[WHOLE, WHOLE, WHOLE, HBM],
        outs=[HBM],
        scratch=[pltpu.VMEM((devices, 1, LANES), F32), pltpu.SemaphoreType.DMA],
        aliases={3: 0},
    )
    states = exchange(states_sent, "states_exchange")
    powers, more, side, spread = call(
        functools.partial(gram_kernel, local=local),
        [obs.shape, (8 * members * members // LANES - obs.shape[0], LANES), (2, 24, members), (patches, members)],
        (obs, extra, rows, counts),
        outs=[WHOLE, WHOLE, WHOLE, HBM],
        types=[F32, F32, F32, BF16],
        scratch=[
            pltpu.VMEM((2, members + 16, slots), BF16),
            pltpu.VMEM((2, members + 16, slots), BF16),
            pltpu.VMEM((patches, members), BF16),
            pltpu.SemaphoreType.DMA,
        ],
        aliases={0: 0},
    )
    (update,) = call(
        functools.partial(update_kernel, local=local),
        [(devices * state_rows, LANES)],
        (states, powers, more, side),
        scratch=[
            pltpu.VMEM((2, 2, members, members), BF16),
            pltpu.VMEM((2, 2, members, members), BF16),
            pltpu.VMEM((2, 2 * members, cells), BF16),
            pltpu.VMEM((2, 8, cells), F32),
        ],
    )
    returned = exchange(update, "return_exchange")
    (analysis,) = call(
        unpack_kernel,
        [(local, patches, cells)],
        (spread, returned),
        outs=[HBM],
        scratch=[pltpu.VMEM((local, patches, cells), F32), pltpu.SemaphoreType.DMA((2 * local,))],
    )
    return analysis


def solution(mesh):
    placed = (P(AXES, None, None), P(AXES, None, None), P(), P(), P())
    return jax.shard_map(
        per_device, mesh=mesh, in_specs=placed, out_specs=P(AXES, None, None), check_vma=False
    )
```
